32 devices in a mesh: dp: 16 (over z, x, core), mp: 2 (over y).
Axes of the slice: x: 2, y: 2, z: 4, core: 2. Of those that a mesh axis runs over, the one named last changes fastest.
Arguments:
- hidden_in: bfloat16 [16, 512, 768], P('dp', 'mp'), may hold values from -6 to 6
- memory: bfloat16 [16, 512, 768], P('dp', 'mp'), may hold values from -6 to 6
- cotangent: bfloat16 [16, 512, 768], P('dp', 'mp'), may hold values from -6 to 6
- self_query: bfloat16 [768, 768], P(None, 'mp'), may hold values from -0.0546875 to 0.0546875
- self_keyval: bfloat16 [2, 768, 768], P(None, None, 'mp'), may hold values from -0.21875 to 0.21875
- self_output: bfloat16 [768, 768], P('mp'), may hold values from -1.75 to 1.75
- cross_query: bfloat16 [768, 768], P(None, 'mp'), may hold values from -0.0546875 to 0.0546875
- cross_keyval: bfloat16 [2, 768, 768], P(None, None, 'mp'), may hold values from -0.21875 to 0.21875
- cross_output: bfloat16 [768, 768], P('mp'), may hold values from -2.5 to 2.5
- ffn_input: bfloat16 [2, 768, 2048], P(None, None, 'mp'), may hold values from -0.21875 to 0.21875
- ffn_output: bfloat16 [2048, 768], P('mp'), may hold values from -0.125 to 0.125
- norm_gains: bfloat16 [3, 768], replicated, may hold values from 0.5 to 1.5
- rel_bias: bfloat16 [32, 12], P(None, 'mp'), may hold values from -2.5 to 2.5
- dec_segments: int32 [16, 512], P('dp'), may hold values from 0 to 3, as said below
- mem_segments: int32 [16, 512], P('dp'), may hold values from 0 to 3, as said below
- rel_bucket: int32 [512], replicated, may hold values from 0 to 31, as said below
Outputs:
- output: bfloat16 [16, 512, 768], P('dp', 'mp')
- grad_input: float32 [16, 512, 768], P('dp', 'mp')
- grad_memory: float32 [16, 512, 768], P('dp', 'mp')
- grad_self_query: float32 [768, 768], P('dp', 'mp')
- grad_self_keyval: float32 [2, 768, 768], P(None, 'dp', 'mp')
- grad_self_output: float32 [768, 768], P('mp', 'dp')
- grad_cross_query: float32 [768, 768], P('dp', 'mp')
- grad_cross_keyval: float32 [2, 768, 768], P(None, 'dp', 'mp')
- grad_cross_output: float32 [768, 768], P('mp', 'dp')
- grad_ffn_input: float32 [2, 768, 2048], P(None, 'dp', 'mp')
- grad_ffn_output: float32 [2048, 768], P('mp', 'dp')
- grad_norm_gains: float32 [3, 768], replicated
- grad_rel_bias: float32 [32, 12], replicated
The draws below stay inside these ranges and needn't reach their ends.
Inputs may be any that keep to these rules, and one draw needn't show every extreme that they name: `dec_segments`: in each row the ids never fall, start at 0 and take every value; one document holds both positions 255 and 256. `mem_segments`: in each row the ids never fall, start at 0 and take every value; one document holds both positions 255 and 256. `rel_bucket`: never falls along the distance, is 0 at distance 0, and takes every bucket.
All inputs are finite; a program needn't handle non-finite values.
Results may differ from the reference program's by a relative error of at most 0.029.
The reference program's roundings to bfloat16 on the way count: a program that leaves them out, or rounds other values in their place, can miss the bound.
Values may be sent and summed in bfloat16 or wider, within the bound.
No kernel may reach another device: no remote copies, remote signals or barrier semaphores. Data moves between devices by JAX's collectives and lax.ppermute only.
A program may use at most 192 MiB of HBM per device.

```python
import jax
import jax.numpy as jnp
from jax import lax

D = 768
H = 12
DH = 64
FF = 2048
BUCKETS = 32
LEN = 512
MEM = 512
DOCS = 4
ROWS_DEV = 1
INNER = 768
ROWS = 16


def cut_ids(key, count, docs):
    middle = count // 2
    order = jax.random.permutation(key, count - 2) + 1
    order = jnp.where(order >= middle, order + 1, order)
    cuts = order[:docs - 1]
    spots = jnp.arange(count, dtype=jnp.int32)
    return jnp.sum((cuts[None, :] <= spots[:, None]).astype(jnp.int32), axis=1).astype(jnp.int32)


def draw_dec_segments(key, part):
    keys = jax.random.split(jax.random.fold_in(key, 17), ROWS)
    return jax.vmap(lambda single_key: cut_ids(single_key, LEN, DOCS))(keys)


def draw_mem_segments(key, part):
    keys = jax.random.split(jax.random.fold_in(key, 23), ROWS)
    return jax.vmap(lambda single_key: cut_ids(single_key, MEM, DOCS))(keys)


def draw_rel_bucket(key, part):
    breaks = jax.random.permutation(jax.random.fold_in(key, 31), LEN - 1)[:BUCKETS - 1] + 1
    spots = jnp.arange(LEN, dtype=jnp.int32)
    return jnp.sum((breaks[None, :] <= spots[:, None]).astype(jnp.int32), axis=1).astype(jnp.int32)


def shard_levels(own_key, shape, shards, least, largest):
    level, own = 1.0, jax.random.fold_in(own_key, 6)
    for axis_at, parts in shards:
        heights = jnp.exp(jax.random.uniform(jax.random.fold_in(own, axis_at), (parts,), jnp.float32, least / len(shards), largest / len(shards)))
        level = level * jnp.repeat(heights, shape[axis_at] // parts).reshape([-1 if axis == axis_at else 1 for axis in range(len(shape))])
    return level


def normal_values(rng, extent, scale, limit, cuts=(), kind=jnp.bfloat16):
    values = jax.random.normal(rng, extent, jnp.float32) * scale
    if len(cuts) > 0:
        values = shard_levels(rng, extent, cuts, -0.22, 0.18) * values
    return jnp.clip(values, min=-limit, max=limit).astype(kind)


def setup_inputs(seed: int = 0) -> dict:
    seeds = jax.random.split(jax.random.key(seed), 17)
    hidden_in = normal_values(seeds[0], (ROWS, LEN, D), 1.0, 6.0, ((0, 16), (1, 2)))
    memory = normal_values(seeds[1], (ROWS, MEM, D), 1.0, 6.0, ((0, 16), (1, 2)))
    cotangent = normal_values(seeds[2], (ROWS, LEN, D), 1.0, 6.0, ((0, 16), (1, 2)))
    self_query = normal_values(seeds[3], (D, INNER), (D * DH // 4) ** -0.5, 0.0546875, ((1, 2),))
    self_keyval = normal_values(seeds[4], (2, D, INNER), D ** -0.5, 0.21875, ((2, 2),))
    self_output = normal_values(seeds[5], (INNER, D), (max(INNER // 64, 4)) ** -0.5, 1.75, ((0, 2),))
    cross_query = normal_values(seeds[6], (D, INNER), (D * DH // 4) ** -0.5, 0.0546875, ((1, 2),))
    cross_keyval = normal_values(seeds[7], (2, D, INNER), D ** -0.5, 0.21875, ((2, 2),))
    cross_output = normal_values(seeds[8], (INNER, D), (max(INNER // 128, 4)) ** -0.5, 2.5, ((0, 2),))
    ffn_input = normal_values(seeds[9], (2, D, FF), D ** -0.5, 0.21875, ((2, 2),))
    ffn_output = normal_values(seeds[10], (FF, D), FF ** -0.5, 0.125, ((0, 2),))
    norm_gains = jnp.clip(1.0 + 0.1 * jax.random.normal(seeds[11], (3, D), jnp.float32), 0.5, 1.5).astype(jnp.bfloat16)
    rel_bias = normal_values(seeds[12], (BUCKETS, H), 0.5, 2.5, ((1, 2),))
    dec_segments = draw_dec_segments(jax.random.fold_in(seeds[16], 71), 0)
    mem_segments = draw_mem_segments(jax.random.fold_in(seeds[16], 71), 0)
    rel_bucket = draw_rel_bucket(jax.random.fold_in(seeds[16], 71), 0)
    return dict(hidden_in=hidden_in, memory=memory, cotangent=cotangent, self_query=self_query, self_keyval=self_keyval, self_output=self_output, cross_query=cross_query, cross_keyval=cross_keyval, cross_output=cross_output, ffn_input=ffn_input, ffn_output=ffn_output, norm_gains=norm_gains, rel_bias=rel_bias, dec_segments=dec_segments, mem_segments=mem_segments, rel_bucket=rel_bucket)


epsilon = 1e-06
masked_score = -1e+30
highest = lax.Precision.HIGHEST

@jax.custom_vjp
def low(v):
    return lax.optimization_barrier(v.astype(jnp.bfloat16)).astype(jnp.float32)

@jax.custom_vjp
def low_back(v):
    return v

def low_keep(v):
    return (low(v), None)

def low_pass(kept, grad):
    return (grad,)

def back_keep(v):
    return (v, None)

def back_low(kept, grad):
    return (low(grad),)
low.defvjp(low_keep, low_pass)
low_back.defvjp(back_keep, back_low)

def rms_norm(values, gain):
    scale = lax.rsqrt(lax.optimization_barrier(jnp.mean(values * values, axis=-1, keepdims=True)) + epsilon)
    return values * scale * gain

def attend(query, keys, values, extra, allowed):
    scores = jnp.einsum('rqhd,rkhd->rhqk', query, keys, precision=highest) + extra
    scores = low_back(scores)
    scores = jnp.where(allowed[:, None], scores, masked_score)
    top = lax.optimization_barrier(jnp.max(scores, axis=-1, keepdims=True))
    weights = jnp.exp(scores - top)
    probs = low(weights / lax.optimization_barrier(jnp.sum(weights, axis=-1, keepdims=True)))
    return jnp.einsum('rhqk,rkhd->rqhd', probs, values, precision=highest)

def split_heads(values):
    return values.reshape(values.shape[0], values.shape[1], H, DH)

def join_heads(values):
    return values.reshape(values.shape[0], values.shape[1], H * DH)

def layer(params, inputs, memory, self_allowed, cross_allowed, distance_bucket):
    self_query, self_keyval, self_output, cross_query, cross_keyval, cross_output, ffn_input, ffn_output, norm_gains, rel_bias = params
    normed_one = low(rms_norm(inputs, norm_gains[0]))
    query_one = low_back(low(jnp.einsum('rld,de->rle', normed_one, self_query, precision=highest)))
    keyval_one = low_back(low(jnp.einsum('rld,cde->crle', normed_one, self_keyval, precision=highest)))
    extra = jnp.transpose(jnp.take(rel_bias, distance_bucket, axis=0), (2, 0, 1))[None]
    context_one = attend(split_heads(query_one), split_heads(keyval_one[0]), split_heads(keyval_one[1]), extra, self_allowed)
    context_one = low_back(low(join_heads(context_one)))
    after_self = inputs + low_back(jnp.einsum('rle,ed->rld', context_one, self_output, precision=highest))
    normed_two = low(rms_norm(after_self, norm_gains[1]))
    query_two = low_back(low(jnp.einsum('rld,de->rle', normed_two, cross_query, precision=highest)))
    keyval_two = low_back(low(jnp.einsum('rmd,cde->crme', memory, cross_keyval, precision=highest)))
    context_two = attend(split_heads(query_two), split_heads(keyval_two[0]), split_heads(keyval_two[1]), 0.0, cross_allowed)
    context_two = low_back(low(join_heads(context_two)))
    after_cross = after_self + low_back(jnp.einsum('rle,ed->rld', context_two, cross_output, precision=highest))
    normed_three = low(rms_norm(after_cross, norm_gains[2]))
    gate_up = low_back(jnp.einsum('rld,cdf->crlf', normed_three, ffn_input, precision=highest))
    hidden = low(jax.nn.gelu(gate_up[0], approximate=True) * gate_up[1])
    return after_cross + low_back(jnp.einsum('rlf,fd->rld', hidden, ffn_output, precision=highest))

def reference(hidden_in, memory, cotangent, self_query, self_keyval, self_output, cross_query, cross_keyval, cross_output, ffn_input, ffn_output, norm_gains, rel_bias, dec_segments, mem_segments, rel_bucket):
    params = tuple((weight.astype(jnp.float32) for weight in (self_query, self_keyval, self_output, cross_query, cross_keyval, cross_output, ffn_input, ffn_output, norm_gains, rel_bias)))
    offsets = jnp.arange(LEN, dtype=jnp.int32)
    distance = jnp.clip(offsets[:, None] - offsets[None, :], 0, LEN - 1).astype(jnp.int32)
    distance_bucket = jnp.take(rel_bucket, distance, axis=0).astype(jnp.int32)
    causal = offsets[:, None] >= offsets[None, :]
    groups = ROWS // ROWS_DEV

    def regroup(values):
        return values.reshape((groups, ROWS_DEV) + values.shape[1:])

    def step(totals, items):
        inputs, mem_rows, grads_out, dec_ids, mem_ids = items
        self_allowed = (dec_ids[:, :, None] == dec_ids[:, None, :]) & causal[None]
        cross_allowed = dec_ids[:, :, None] == mem_ids[:, None, :]

        def forward(weights, first, second):
            return layer(weights, first, second, self_allowed, cross_allowed, distance_bucket)
        result, pull = jax.vjp(forward, params, inputs.astype(jnp.float32), mem_rows.astype(jnp.float32))
        grad_params, grad_inputs, grad_mem = pull(grads_out.astype(jnp.float32))
        totals = jax.tree.map(lambda left, right: left + right, totals, grad_params)
        return (totals, (result.astype(jnp.bfloat16), grad_inputs, grad_mem))
    start = jax.tree.map(jnp.zeros_like, params)
    totals, stacked = lax.scan(step, start, (regroup(hidden_in), regroup(memory), regroup(cotangent), regroup(dec_segments), regroup(mem_segments)))
    output, grad_inputs, grad_mem = stacked
    return (output.reshape(ROWS, LEN, D), grad_inputs.reshape(ROWS, LEN, D), grad_mem.reshape(ROWS, MEM, D), totals[0], totals[1], totals[2], totals[3], totals[4], totals[5], totals[6], totals[7], totals[8], totals[9])
```

```python
import jax
import jax.numpy as jnp
from jax import lax
from jax.sharding import PartitionSpec as P

epsilon = 1e-06
masked_score = -1e30


def rms_norm(values, gain):
    scale = lax.rsqrt(jnp.mean(values * values, axis=-1, keepdims=True) + epsilon)
    return values * scale * gain


def norm_back(values, gain, grad):
    _, pull = jax.vjp(rms_norm, values, gain)
    return pull(grad)


def gated(gate_part, up_part):
    return jax.nn.gelu(gate_part, approximate=True) * up_part


def by_heads(values, heads):
    return values.reshape(values.shape[0], heads, values.shape[1] // heads)


def scores_of(query, keys, extra, allowed):
    scores = jnp.einsum("qhd,khd->hqk", query, keys, preferred_element_type=jnp.float32) + extra
    return jnp.where(allowed[None], scores, masked_score)


def attend_row(query, keys, values, extra, allowed):
    scores = scores_of(query, keys, extra, allowed)
    top = jnp.max(scores, axis=-1, keepdims=True)
    weights = jnp.exp(scores - top)
    total = jnp.sum(weights, axis=-1, keepdims=True)
    probs = (weights / total).astype(jnp.bfloat16)
    context = jnp.einsum("hqk,khd->qhd", probs, values, preferred_element_type=jnp.float32)
    return (context.reshape(context.shape[0], -1).astype(jnp.bfloat16), top, total)


def attend_back(query, keys, values, extra, allowed, top, total, grad_context):
    scores = scores_of(query, keys, extra, allowed)
    probs = jnp.exp(scores - top) / total
    grad_probs = jnp.einsum(
        "qhd,khd->hqk", grad_context, values, preferred_element_type=jnp.float32
    )
    delta = jnp.sum(probs * grad_probs, axis=-1, keepdims=True)
    grad_scores = (probs * (grad_probs - delta)).astype(jnp.bfloat16)
    grad_query = jnp.einsum("hqk,khd->qhd", grad_scores, keys, preferred_element_type=jnp.float32)
    grad_keys = jnp.einsum("hqk,qhd->khd", grad_scores, query, preferred_element_type=jnp.float32)
    grad_values = jnp.einsum(
        "hqk,qhd->khd", probs.astype(jnp.bfloat16), grad_context, preferred_element_type=jnp.float32
    )
    query_rows = query.shape[0]
    key_rows = keys.shape[0]
    return (
        grad_query.reshape(query_rows, -1).astype(jnp.bfloat16),
        grad_keys.reshape(key_rows, -1),
        grad_values.reshape(key_rows, -1),
        grad_scores,
    )


def gather_normed(values):
    return lax.all_gather(values, "mp", axis=1, tiled=True)


def gather_grads(values):
    return lax.all_gather(values, "mp", axis=1, tiled=True)


def branch_total(values):
    return lax.psum_scatter(values, "mp", scatter_dimension=1, tiled=True)


def input_total(values):
    return lax.psum_scatter(
        values.astype(jnp.bfloat16), "mp", scatter_dimension=1, tiled=True
    ).astype(jnp.float32)


def body(
    hidden_in,
    memory,
    cotangent,
    self_query,
    self_keyval,
    self_output,
    cross_query,
    cross_keyval,
    cross_output,
    ffn_input,
    ffn_output,
    norm_gains,
    rel_bias,
    dec_segments,
    mem_segments,
    rel_bucket,
):
    length = dec_segments.shape[1]
    local_heads = rel_bias.shape[1]
    buckets = rel_bias.shape[0]
    gain_values = norm_gains.astype(jnp.float32)
    first_in = hidden_in.astype(jnp.float32)
    normed_one = rms_norm(first_in, gain_values[0]).astype(jnp.bfloat16)
    gathered_one = gather_normed(normed_one)
    query_rows = gathered_one.shape[1]
    query_pos = jnp.arange(query_rows, dtype=jnp.int32)
    key_pos = jnp.arange(length, dtype=jnp.int32)
    distance = jnp.clip(query_pos[:, None] - key_pos[None, :], 0, length - 1)
    starts = jnp.sum(
        (rel_bucket[None, :] < jnp.arange(1, buckets, dtype=jnp.int32)[:, None]).astype(jnp.int32),
        axis=1,
    )
    bucket_index = jnp.sum((distance[None] >= starts[:, None, None]).astype(jnp.int32), axis=0)
    bucket_hot = (jnp.arange(buckets, dtype=jnp.int32)[:, None, None] == bucket_index[None]).astype(
        jnp.bfloat16
    )
    causal = query_pos[:, None] >= key_pos[None, :]
    bias_full = jnp.einsum("bij,bh->hij", bucket_hot, rel_bias, preferred_element_type=jnp.float32)

    def self_forward(items):
        query, keys, values, seg_ids, key_ids = items
        allowed = (seg_ids[:, None] == key_ids[None, :]) & causal
        return attend_row(
            by_heads(query, local_heads),
            by_heads(keys, local_heads),
            by_heads(values, local_heads),
            bias_full,
            allowed,
        )

    def cross_forward(items):
        query, keys, values, seg_ids, mem_ids = items
        allowed = seg_ids[:, None] == mem_ids[None, :]
        return attend_row(
            by_heads(query, local_heads),
            by_heads(keys, local_heads),
            by_heads(values, local_heads),
            0.0,
            allowed,
        )

    query_one = jnp.einsum(
        "rld,de->rle", gathered_one, self_query, preferred_element_type=jnp.float32
    ).astype(jnp.bfloat16)
    keyval_one = jnp.einsum(
        "rld,cde->crle", gathered_one, self_keyval, preferred_element_type=jnp.float32
    ).astype(jnp.bfloat16)
    context_one, top_one, total_one = lax.map(
        self_forward, (query_one, keyval_one[0], keyval_one[1], dec_segments, dec_segments)
    )
    after_self = first_in + branch_total(
        jnp.einsum("rle,ed->rld", context_one, self_output, preferred_element_type=jnp.float32)
    )
    normed_two = rms_norm(after_self, gain_values[1]).astype(jnp.bfloat16)
    gathered_two = gather_normed(normed_two)
    memory_all = lax.all_gather(memory, "mp", axis=1, tiled=True)
    query_two = jnp.einsum(
        "rld,de->rle", gathered_two, cross_query, preferred_element_type=jnp.float32
    ).astype(jnp.bfloat16)
    keyval_two = jnp.einsum(
        "rmd,cde->crme", memory_all, cross_keyval, preferred_element_type=jnp.float32
    ).astype(jnp.bfloat16)
    context_two, top_two, total_two = lax.map(
        cross_forward, (query_two, keyval_two[0], keyval_two[1], dec_segments, mem_segments)
    )
    after_cross = after_self + branch_total(
        jnp.einsum("rle,ed->rld", context_two, cross_output, preferred_element_type=jnp.float32)
    )
    normed_three = rms_norm(after_cross, gain_values[2]).astype(jnp.bfloat16)
    gathered_three = gather_normed(normed_three)
    gate_up = jnp.einsum(
        "rld,cdf->crlf", gathered_three, ffn_input, preferred_element_type=jnp.float32
    )
    hidden = gated(gate_up[0], gate_up[1]).astype(jnp.bfloat16)
    final = after_cross + branch_total(
        jnp.einsum("rlf,fd->rld", hidden, ffn_output, preferred_element_type=jnp.float32)
    )
    grad_out = cotangent.astype(jnp.float32)
    sent_three = gather_grads(cotangent)
    grad_ffn_output = jnp.einsum(
        "rlf,rld->fd", hidden, sent_three, preferred_element_type=jnp.float32
    )
    grad_hidden = jnp.einsum(
        "rld,fd->rlf", sent_three, ffn_output, preferred_element_type=jnp.float32
    )
    _, pull_gate = jax.vjp(gated, gate_up[0], gate_up[1])
    grad_gate, grad_upward = pull_gate(grad_hidden)
    grad_gate_up = jnp.stack([grad_gate, grad_upward]).astype(jnp.bfloat16)
    grad_ffn_input = jnp.einsum(
        "rld,crlf->cdf", gathered_three, grad_gate_up, preferred_element_type=jnp.float32
    )
    grad_normed_three = input_total(
        jnp.einsum("crlf,cdf->rld", grad_gate_up, ffn_input, preferred_element_type=jnp.float32)
    )
    grad_cross_in, gain_three = norm_back(after_cross, gain_values[2], grad_normed_three)
    grad_cross = grad_out + grad_cross_in
    sent_two = gather_grads(grad_cross.astype(jnp.bfloat16))
    grad_cross_output = jnp.einsum(
        "rle,rld->ed", context_two, sent_two, preferred_element_type=jnp.float32
    )
    grad_context_two = jnp.einsum(
        "rld,ed->rle", sent_two, cross_output, preferred_element_type=jnp.float32
    ).astype(jnp.bfloat16)

    def cross_backward(items):
        query, keys, values, seg_ids, mem_ids, top, total, grad_context = items
        allowed = seg_ids[:, None] == mem_ids[None, :]
        grad_query, grad_keys, grad_values, _ = attend_back(
            by_heads(query, local_heads),
            by_heads(keys, local_heads),
            by_heads(values, local_heads),
            0.0,
            allowed,
            top,
            total,
            by_heads(grad_context, local_heads),
        )
        return (grad_query, grad_keys, grad_values)

    grad_query_two, grad_key_two, grad_value_two = lax.map(
        cross_backward,
        (
            query_two,
            keyval_two[0],
            keyval_two[1],
            dec_segments,
            mem_segments,
            top_two,
            total_two,
            grad_context_two,
        ),
    )
    grad_keyval_two = jnp.stack([grad_key_two, grad_value_two])
    grad_keyval_two = grad_keyval_two.astype(jnp.bfloat16)
    grad_cross_query = jnp.einsum(
        "rld,rle->de", gathered_two, grad_query_two, preferred_element_type=jnp.float32
    )
    grad_cross_keyval = jnp.einsum(
        "rmd,crme->cde", memory_all, grad_keyval_two, preferred_element_type=jnp.float32
    )
    memory_terms = jnp.einsum(
        "crme,cde->rmd", grad_keyval_two, cross_keyval, preferred_element_type=jnp.float32
    )
    grad_memory = lax.psum_scatter(
        memory_terms.astype(jnp.bfloat16), "mp", scatter_dimension=1, tiled=True
    ).astype(jnp.float32)
    grad_normed_two = input_total(
        jnp.einsum("rle,de->rld", grad_query_two, cross_query, preferred_element_type=jnp.float32)
    )
    grad_self_in, gain_two = norm_back(after_self, gain_values[1], grad_normed_two)
    grad_self = grad_cross + grad_self_in
    sent_one = gather_grads(grad_self.astype(jnp.bfloat16))
    grad_self_output = jnp.einsum(
        "rle,rld->ed", context_one, sent_one, preferred_element_type=jnp.float32
    )
    grad_context_one = jnp.einsum(
        "rld,ed->rle", sent_one, self_output, preferred_element_type=jnp.float32
    ).astype(jnp.bfloat16)

    def self_backward(items):
        query, keys, values, seg_ids, key_ids, top, total, grad_context = items
        allowed = (seg_ids[:, None] == key_ids[None, :]) & causal
        grad_query, grad_keys, grad_values, grad_scores = attend_back(
            by_heads(query, local_heads),
            by_heads(keys, local_heads),
            by_heads(values, local_heads),
            bias_full,
            allowed,
            top,
            total,
            by_heads(grad_context, local_heads),
        )
        bias_part = jnp.einsum(
            "bij,hij->bh", bucket_hot, grad_scores, preferred_element_type=jnp.float32
        )
        return (grad_query, grad_keys, grad_values, bias_part)

    grad_query_one, grad_key_one, grad_value_one, bias_parts = lax.map(
        self_backward,
        (
            query_one,
            keyval_one[0],
            keyval_one[1],
            dec_segments,
            dec_segments,
            top_one,
            total_one,
            grad_context_one,
        ),
    )
    grad_keyval_one = jnp.stack([grad_key_one, grad_value_one])
    grad_keyval_one = grad_keyval_one.astype(jnp.bfloat16)
    grad_self_query = jnp.einsum(
        "rld,rle->de", gathered_one, grad_query_one, preferred_element_type=jnp.float32
    )
    grad_self_keyval = jnp.einsum(
        "rld,crle->cde", gathered_one, grad_keyval_one, preferred_element_type=jnp.float32
    )
    grad_normed_one = input_total(
        jnp.einsum("rle,de->rld", grad_query_one, self_query, preferred_element_type=jnp.float32)
        + jnp.einsum(
            "crle,cde->rld", grad_keyval_one, self_keyval, preferred_element_type=jnp.float32
        )
    )
    grad_first, gain_one = norm_back(first_in, gain_values[0], grad_normed_one)
    grad_input = grad_self + grad_first
    local_bias = jnp.sum(bias_parts, axis=0)
    full_bias = jnp.zeros((buckets, local_heads * lax.axis_size("mp")), jnp.float32)
    full_bias = lax.dynamic_update_slice(
        full_bias, local_bias, (jnp.int32(0), lax.axis_index("mp") * local_heads)
    )
    gain_sum, bias_sum = lax.psum(
        (jnp.stack([gain_one, gain_two, gain_three]), full_bias), ("dp", "mp")
    )
    local_grads = (
        grad_self_query[None],
        grad_self_keyval,
        grad_self_output,
        grad_cross_query[None],
        grad_cross_keyval,
        grad_cross_output,
        grad_ffn_input,
        grad_ffn_output,
    )
    summed = tuple(
        (
            lax.psum_scatter(local_grads[0], "dp", scatter_dimension=1, tiled=True),
            lax.psum_scatter(local_grads[1], "dp", scatter_dimension=1, tiled=True),
            lax.psum_scatter(local_grads[2], "dp", scatter_dimension=1, tiled=True),
            lax.psum_scatter(local_grads[3], "dp", scatter_dimension=1, tiled=True),
            lax.psum_scatter(local_grads[4], "dp", scatter_dimension=1, tiled=True),
            lax.psum_scatter(local_grads[5], "dp", scatter_dimension=1, tiled=True),
            lax.psum_scatter(local_grads[6], "dp", scatter_dimension=1, tiled=True),
            lax.psum_scatter(local_grads[7], "dp", scatter_dimension=1, tiled=True),
        )
    )
    return (
        final.astype(jnp.bfloat16),
        grad_input,
        grad_memory,
        summed[0][0],
        summed[1],
        summed[2],
        summed[3][0],
        summed[4],
        summed[5],
        summed[6],
        summed[7],
        gain_sum,
        bias_sum,
    )


def solution(mesh):
    in_specs = (
        P("dp", "mp", None),
        P("dp", "mp", None),
        P("dp", "mp", None),
        P(None, "mp"),
        P(None, None, "mp"),
        P("mp", None),
        P(None, "mp"),
        P(None, None, "mp"),
        P("mp", None),
        P(None, None, "mp"),
        P("mp", None),
        P(),
        P(None, "mp"),
        P("dp", None),
        P("dp", None),
        P(),
    )
    out_specs = (
        P("dp", "mp", None),
        P("dp", "mp", None),
        P("dp", "mp", None),
        P("dp", "mp"),
        P(None, "dp", "mp"),
        P("mp", "dp"),
        P("dp", "mp"),
        P(None, "dp", "mp"),
        P("mp", "dp"),
        P(None, "dp", "mp"),
        P("mp", "dp"),
        P(),
        P(),
    )
    return jax.shard_map(body, mesh=mesh, in_specs=in_specs, out_specs=out_specs, check_vma=False)
```

```python
import functools

import jax
import jax.numpy as jnp
import numpy as np
from jax import lax
from jax.experimental import pallas as pl
from jax.experimental.pallas import tpu as pltpu
from jax.sharding import PartitionSpec as P

epsilon = 1e-06
masked_score = -1e30
gelu_root = float(np.sqrt(2.0 / np.pi))
gelu_cubic = 0.044715
block = 128
head_size = 64
f32 = jnp.float32
bf16 = jnp.bfloat16


def dot(left, right):
    return lax.dot_general(left, right, (((1,), (0,)), ((), ())), preferred_element_type=f32)


def dot_rt(left, right):
    return lax.dot_general(left, right, (((1,), (1,)), ((), ())), preferred_element_type=f32)


def dot_lt(left, right):
    return lax.dot_general(left, right, (((0,), (0,)), ((), ())), preferred_element_type=f32)


def pick(flag, first, second):
    return jnp.where(flag, first, second)


def even_odd(values):
    lane = lax.broadcasted_iota(jnp.int32, values.shape, 1)
    zero = jnp.zeros_like(values)
    return jnp.where(lane < head_size, values, zero), jnp.where(lane < head_size, zero, values)


def rms_scale(values):
    return lax.rsqrt(jnp.mean(values * values, axis=-1, keepdims=True) + epsilon)


def norm_back(values, gain, grad):
    scale = rms_scale(values)
    scaled = grad * gain
    inner = jnp.mean(values * scaled, axis=-1, keepdims=True)
    back = scale * scaled - values * (scale * scale * scale * inner)
    return back, grad * values * scale


def softmax(scores):
    top = jnp.max(scores, axis=-1, keepdims=True)
    weights = jnp.exp(scores - top)
    total = jnp.sum(weights, axis=-1, keepdims=True)
    return (weights * (1.0 / total)).astype(bf16)


def call(kernel, name, outs, args, scalars=0, scratch=(), flops=0):
    out_shape = [jax.ShapeDtypeStruct(shape, dtype) for shape, dtype in outs]
    moved = sum(x.size * x.dtype.itemsize for x in list(args) + out_shape)
    in_specs = [pl.BlockSpec(memory_space=pltpu.SMEM)] * scalars
    in_specs += [pl.BlockSpec(memory_space=pltpu.VMEM)] * (len(args) - scalars)
    return pl.pallas_call(
        kernel,
        name=name,
        out_shape=out_shape,
        in_specs=in_specs,
        out_specs=[pl.BlockSpec(memory_space=pltpu.VMEM)] * len(outs),
        scratch_shapes=list(scratch),
        compiler_params=pltpu.CompilerParams(vmem_limit_bytes=24 << 20),
        cost_estimate=pl.CostEstimate(flops=flops, transcendentals=0, bytes_accessed=moved),
    )(*args)


def bias_kernel(line_ref, table_ref):
    heads = table_ref.shape[0]
    count = table_ref.shape[2] // block
    for head in range(heads):
        for step in range(count):
            line = line_ref[head : head + 1, step * 2 * block : (step + 1) * 2 * block]
            wide = jnp.broadcast_to(line, (block, 2 * block))
            turned = pltpu.roll(wide, 0, 1, stride=1, stride_axis=0)
            at = (count - 1 - step) * block
            table_ref[head, :, at : at + block] = turned[:, :block].astype(bf16)


def self_forward_kernel(chunk, *refs):
    refs = list(refs)
    idx_ref, own_ref, recv_ref, gain_ref, wq_ref, wkv_ref, wo_ref, segc_ref, segr_ref, table_ref = refs[:10]
    refs = refs[10:]
    if chunk:
        before_ref = refs.pop(0)
    normed_ref, qkv_ref, ctx_ref, prob_ref, part_ref = refs
    mine = idx_ref[0] == chunk
    rows, width = own_ref.shape
    inner = wq_ref.shape[1]
    base = chunk * rows
    gain = gain_ref[0:1, :].astype(f32)
    for at in range(0, rows, block):
        values = pick(mine, own_ref[at : at + block, :], recv_ref[at : at + block, :]).astype(f32)
        normed_ref[at : at + block, :] = (values * rms_scale(values) * gain).astype(bf16)
    normed = normed_ref[...]
    if chunk:
        qkv_ref[0:base, :] = before_ref[...]
    qkv_ref[base : base + rows, 0:inner] = dot(normed, wq_ref[...]).astype(bf16)
    qkv_ref[base : base + rows, inner : 2 * inner] = dot(normed, wkv_ref[0]).astype(bf16)
    qkv_ref[base : base + rows, 2 * inner : 3 * inner] = dot(normed, wkv_ref[1]).astype(bf16)
    total = table_ref.shape[2]
    masks = []
    for at in range(0, rows, block):
        keys = base + at + block
        allowed = segc_ref[base + at : keys, :] == segr_ref[:, 0:keys]
        row = lax.broadcasted_iota(jnp.int32, (block, keys), 0) + (base + at)
        col = lax.broadcasted_iota(jnp.int32, (block, keys), 1)
        masks.append(jnp.where(allowed & (row >= col), 0.0, masked_score))
    for pair in range(0, inner, 2 * head_size):
        keys2 = qkv_ref[0 : base + rows, inner + pair : inner + pair + 128]
        values_e, values_o = even_odd(qkv_ref[0 : base + rows, 2 * inner + pair : 2 * inner + pair + 128])
        for number, at in enumerate(range(0, rows, block)):
            keys = base + at + block
            query_e, query_o = even_odd(qkv_ref[base + at : keys, pair : pair + 128])
            context = jnp.zeros((block, 128), f32)
            for head, query, values in (
                (pair // head_size, query_e, values_e),
                (pair // head_size + 1, query_o, values_o),
            ):
                scores = dot_rt(query, keys2[0:keys]) + table_ref[head, :, total - keys :].astype(f32)
                probs = softmax(scores + masks[number])
                prob_ref[head, at : at + block, 0:keys] = probs
                context = context + dot(probs, values[0:keys])
            ctx_ref[at : at + block, pair : pair + 128] = context.astype(bf16)
    part_ref[...] = dot(ctx_ref[...], wo_ref[...]).astype(bf16)


def memory_kernel(idx_ref, own_ref, recv_ref, wkv_ref, memory_ref, kv_ref):
    rows = own_ref.shape[0]
    inner = wkv_ref.shape[2]
    mine = idx_ref[0]
    memory_ref[pl.ds(pl.multiple_of(mine * rows, rows), rows), :] = own_ref[...]
    memory_ref[pl.ds(pl.multiple_of((1 - mine) * rows, rows), rows), :] = recv_ref[...]
    kv_ref[:, 0:inner] = dot(memory_ref[...], wkv_ref[0]).astype(bf16)
    kv_ref[:, inner : 2 * inner] = dot(memory_ref[...], wkv_ref[1]).astype(bf16)


def cross_forward_kernel(
    chunk,
    idx_ref,
    own_ref,
    recv_ref,
    part_ref,
    part_recv_ref,
    gain_ref,
    wq_ref,
    wo_ref,
    kv_ref,
    segc_ref,
    segm_ref,
    after_ref,
    normed_ref,
    query_ref,
    ctx_ref,
    prob_ref,
    out_ref,
):
    mine = idx_ref[0] == chunk
    rows = own_ref.shape[0]
    inner = wq_ref.shape[1]
    gain = gain_ref[1:2, :].astype(f32)
    for at in range(0, rows, block):
        part = slice(at, at + block)
        values = pick(mine, own_ref[part, :], recv_ref[part, :]).astype(f32)
        values = values + (part_ref[part, :].astype(f32) + part_recv_ref[part, :].astype(f32))
        after_ref[part, :] = values
        normed_ref[part, :] = (values * rms_scale(values) * gain).astype(bf16)
    query_ref[...] = dot(normed_ref[...], wq_ref[...]).astype(bf16)
    masks = []
    for at in range(0, rows, block):
        allowed = segc_ref[chunk * rows + at : chunk * rows + at + block, :] == segm_ref[...]
        masks.append(jnp.where(allowed, 0.0, masked_score))
    for pair in range(0, inner, 2 * head_size):
        keys2 = kv_ref[:, pair : pair + 128]
        values_e, values_o = even_odd(kv_ref[:, inner + pair : inner + pair + 128])
        for number, at in enumerate(range(0, rows, block)):
            query_e, query_o = even_odd(query_ref[at : at + block, pair : pair + 128])
            context = jnp.zeros((block, 128), f32)
            for head, query, values in (
                (pair // head_size, query_e, values_e),
                (pair // head_size + 1, query_o, values_o),
            ):
                probs = softmax(dot_rt(query, keys2) + masks[number])
                prob_ref[head, at : at + block, :] = probs
                context = context + dot(probs, values)
            ctx_ref[at : at + block, pair : pair + 128] = context.astype(bf16)
    out_ref[...] = dot(ctx_ref[...], wo_ref[...]).astype(bf16)


def ffn_kernel(
    chunk,
    idx_ref,
    after_self_ref,
    part_ref,
    part_recv_ref,
    cot_ref,
    cot_recv_ref,
    gain_ref,
    win_ref,
    wout_ref,
    after_ref,
    normed_ref,
    hidden_ref,
    grads_ref,
    back_ref,
    cot_scr,
):
    mine = idx_ref[0] == chunk
    rows = after_self_ref.shape[0]
    units = win_ref.shape[2]
    gain = gain_ref[2:3, :].astype(f32)
    for at in range(0, rows, block):
        part = slice(at, at + block)
        values = after_self_ref[part, :] + (
            part_ref[part, :].astype(f32) + part_recv_ref[part, :].astype(f32)
        )
        after_ref[part, :] = values
        normed_ref[part, :] = (values * rms_scale(values) * gain).astype(bf16)
        cot_scr[part, :] = pick(mine, cot_ref[part, :], cot_recv_ref[part, :])
    wide = 256
    for at in range(0, units, wide):
        cols = slice(at, at + wide)
        gate = dot(normed_ref[...], win_ref[0, :, cols])
        upward = dot(normed_ref[...], win_ref[1, :, cols])
        grad = dot_rt(cot_scr[...], wout_ref[cols, :])
        square = gate * gate
        bend = jnp.tanh(gelu_root * gate * (1.0 + gelu_cubic * square))
        half = 0.5 * (1.0 + bend)
        gelu = gate * half
        slope = half + 0.5 * gelu_root * gate * (1.0 - bend * bend) * (1.0 + 3.0 * gelu_cubic * square)
        hidden_ref[:, cols] = (gelu * upward).astype(bf16)
        grads_ref[:, cols] = (grad * upward * slope).astype(bf16)
        grads_ref[:, units + at : units + at + wide] = (grad * gelu).astype(bf16)
    back_ref[...] = (
        dot_rt(grads_ref[:, 0:units], win_ref[0]) + dot_rt(grads_ref[:, units:], win_ref[1])
    ).astype(bf16)


def down_kernel(idx_ref, first_ref, second_ref, wout_ref, out_ref):
    out_ref[...] = dot(pick(idx_ref[0] == 0, second_ref[...], first_ref[...]), wout_ref[...]).astype(bf16)


def final_kernel(idx_ref, hid_a, hid_b, after_a, after_b, recv_ref, wout_ref, out_ref):
    mine = idx_ref[0] == 0
    own = dot(pick(mine, hid_a[...], hid_b[...]), wout_ref[...])
    out_ref[...] = (pick(mine, after_a[...], after_b[...]) + (own + recv_ref[...].astype(f32))).astype(bf16)


def turn_rows(values, place_ref, order, at):
    turned = jnp.transpose(values)
    size = turned.shape[0] // len(order)
    for number, position in enumerate(order):
        place_ref[position * size : (position + 1) * size, at : at + values.shape[0]] = turned[
            number * size : (number + 1) * size
        ]


def write_grads(bit_ref, turned_ref, right, send_ref, keep_ref, at):
    rows = send_ref.shape[0]
    mine = bit_ref[1]
    cols = slice(at, at + right.shape[1])
    keep_ref[:, cols] = dot(turned_ref[pl.ds(pl.multiple_of(mine * rows, rows), rows), :], right).astype(bf16)
    send_ref[:, cols] = dot(turned_ref[pl.ds(pl.multiple_of((1 - mine) * rows, rows), rows), :], right).astype(bf16)


def ffn_grads_kernel(
    order,
    idx_ref,
    normed_a,
    normed_b,
    grads_a,
    grads_b,
    hidden_a,
    hidden_b,
    cot_ref,
    cot_recv_ref,
    send_ref,
    keep_ref,
    turned,
    turned_two,
):
    rows = normed_a.shape[0]
    mine = idx_ref[0] == 0
    units = hidden_a.shape[1]
    turn_rows(normed_a[...], turned, order, 0)
    turn_rows(normed_b[...], turned, order, rows)
    both = jnp.concatenate([grads_a[...], grads_b[...]], axis=0)
    write_grads(idx_ref, turned, both, send_ref, keep_ref, 0)
    turn_rows(pick(mine, cot_ref[...], cot_recv_ref[...]), turned_two, order, 0)
    turn_rows(pick(mine, cot_recv_ref[...], cot_ref[...]), turned_two, order, rows)
    hidden = jnp.concatenate([hidden_a[...], hidden_b[...]], axis=0)
    write_grads(idx_ref, turned_two, hidden, send_ref, keep_ref, 2 * units)


def attend_back(query_rows, prob_ref, score_ref, grad_ref, key_of, value_of, dq_ref, inner, reach):
    for pair in range(0, inner, 2 * head_size):
        keys_e, keys_o = even_odd(key_of(pair))
        values2 = value_of(pair)
        for at in range(0, query_rows, block):
            keys = reach(at)
            grad_e, grad_o = even_odd(grad_ref[at : at + block, pair : pair + 128])
            total = jnp.zeros((block, 128), f32)
            for head, grad, key in (
                (pair // head_size, grad_e, keys_e),
                (pair // head_size + 1, grad_o, keys_o),
            ):
                probs = prob_ref[head, at : at + block, 0:keys].astype(f32)
                grad_probs = dot_rt(grad, values2[0:keys])
                delta = jnp.sum(probs * grad_probs, axis=-1, keepdims=True) / jnp.sum(
                    probs, axis=-1, keepdims=True
                )
                scores = (probs * (grad_probs - delta)).astype(bf16)
                score_ref[head, at : at + block, 0:keys] = scores
                total = total + dot(scores, key[0:keys])
            dq_ref[at : at + block, pair : pair + 128] = total.astype(bf16)


def cross_back_kernel(
    chunk,
    idx_ref,
    after_ref,
    back_ref,
    back_recv_ref,
    cot_ref,
    cot_recv_ref,
    gain_ref,
    wo_ref,
    wq_ref,
    kv_ref,
    prob_ref,
    grad_ref,
    sent_ref,
    dctx_ref,
    dq_ref,
    score_ref,
    out_ref,
    gain_out_ref,
):
    mine = idx_ref[0] == chunk
    rows = after_ref.shape[0]
    inner = wq_ref.shape[1]
    gain = gain_ref[2:3, :].astype(f32)
    gain_total = jnp.zeros((8, gain.shape[1]), f32)
    for at in range(0, rows, block):
        part = slice(at, at + block)
        incoming = back_ref[part, :].astype(f32) + back_recv_ref[part, :].astype(f32)
        back, gain_terms = norm_back(after_ref[part, :], gain, incoming)
        total = pick(mine, cot_ref[part, :], cot_recv_ref[part, :]).astype(f32) + back
        grad_ref[part, :] = total
        sent_ref[part, :] = total.astype(bf16)
        gain_total = gain_total + jnp.sum(gain_terms.reshape(block // 8, 8, -1), axis=0)
    gain_out_ref[...] = pick(mine, gain_total, jnp.zeros_like(gain_total))
    dctx_ref[...] = dot_rt(sent_ref[...], wo_ref[...]).astype(bf16)
    attend_back(
        rows,
        prob_ref,
        score_ref,
        dctx_ref,
        lambda pair: kv_ref[:, pair : pair + 128],
        lambda pair: kv_ref[:, inner + pair : inner + pair + 128],
        dq_ref,
        inner,
        lambda at: kv_ref.shape[0],
    )
    out_ref[...] = dot_rt(dq_ref[...], wq_ref[...]).astype(bf16)


def cross_grads_kernel(
    order,
    idx_ref,
    normed_a,
    normed_b,
    dq_a,
    dq_b,
    query_a,
    query_b,
    score_a,
    score_b,
    prob_a,
    prob_b,
    dctx_a,
    dctx_b,
    ctx_a,
    ctx_b,
    sent_a,
    sent_b,
    memory_ref,
    wkv_ref,
    send_ref,
    keep_ref,
    memory_send_ref,
    memory_keep_ref,
    turned,
    turned_two,
    turned_three,
    dkv,
):
    rows = normed_a.shape[0]
    inner = dq_a.shape[1]
    for pair in range(0, inner, 2 * head_size):
        keys = jnp.zeros((dkv.shape[0], 128), f32)
        values = jnp.zeros((dkv.shape[0], 128), f32)
        for score, prob, query, dctx in ((score_a, prob_a, query_a, dctx_a), (score_b, prob_b, query_b, dctx_b)):
            cols = slice(pair, pair + 128)
            for number, (query_half, grad_half) in enumerate(
                zip(even_odd(query[:, cols]), even_odd(dctx[:, cols]), strict=True)
            ):
                head = pair // head_size + number
                keys = keys + dot_lt(score[head], query_half)
                values = values + dot_lt(prob[head], grad_half)
        dkv[:, pair : pair + 128] = keys.astype(bf16)
        dkv[:, inner + pair : inner + pair + 128] = values.astype(bf16)
    mine = idx_ref[0]
    other = pl.ds(pl.multiple_of((1 - mine) * rows, rows), rows)
    own = pl.ds(pl.multiple_of(mine * rows, rows), rows)
    memory_send_ref[...] = (
        dot_rt(dkv[other, 0:inner], wkv_ref[0]) + dot_rt(dkv[other, inner:], wkv_ref[1])
    ).astype(bf16)
    memory_keep_ref[...] = dot_rt(dkv[own, 0:inner], wkv_ref[0]) + dot_rt(dkv[own, inner:], wkv_ref[1])
    turn_rows(normed_a[...], turned, order, 0)
    turn_rows(normed_b[...], turned, order, rows)
    both = jnp.concatenate([dq_a[...], dq_b[...]], axis=0)
    write_grads(idx_ref, turned, both, send_ref, keep_ref, 0)
    turn_rows(memory_ref[...], turned_two, order, 0)
    write_grads(idx_ref, turned_two, dkv[...], send_ref, keep_ref, inner)
    turn_rows(sent_a[...], turned_three, order, 0)
    turn_rows(sent_b[...], turned_three, order, rows)
    both = jnp.concatenate([ctx_a[...], ctx_b[...]], axis=0)
    write_grads(idx_ref, turned_three, both, send_ref, keep_ref, 3 * inner)


def self_back_kernel(
    chunk,
    idx_ref,
    after_ref,
    back_ref,
    back_recv_ref,
    cross_ref,
    gain_ref,
    wo_ref,
    qkv_ref,
    prob_ref,
    grad_ref,
    sent_ref,
    dctx_ref,
    dq_ref,
    score_ref,
    gain_out_ref,
):
    mine = idx_ref[0] == chunk
    rows = after_ref.shape[0]
    inner = wo_ref.shape[0]
    gain = gain_ref[1:2, :].astype(f32)
    gain_total = jnp.zeros((8, gain.shape[1]), f32)
    for at in range(0, rows, block):
        part = slice(at, at + block)
        incoming = back_ref[part, :].astype(f32) + back_recv_ref[part, :].astype(f32)
        back, gain_terms = norm_back(after_ref[part, :], gain, incoming)
        total = cross_ref[part, :] + back
        grad_ref[part, :] = total
        sent_ref[part, :] = total.astype(bf16)
        gain_total = gain_total + jnp.sum(gain_terms.reshape(block // 8, 8, -1), axis=0)
    gain_out_ref[...] = pick(mine, gain_total, jnp.zeros_like(gain_total))
    dctx_ref[...] = dot_rt(sent_ref[...], wo_ref[...]).astype(bf16)
    end = (chunk + 1) * rows
    attend_back(
        rows,
        prob_ref,
        score_ref,
        dctx_ref,
        lambda pair: qkv_ref[0:end, inner + pair : inner + pair + 128],
        lambda pair: qkv_ref[0:end, 2 * inner + pair : 2 * inner + pair + 128],
        dq_ref,
        inner,
        lambda at: chunk * rows + at + block,
    )


def self_grads_kernel(
    order,
    idx_ref,
    normed_a,
    normed_b,
    dq_a,
    dq_b,
    qkv_ref,
    score_a,
    score_b,
    prob_a,
    prob_b,
    dctx_a,
    dctx_b,
    ctx_a,
    ctx_b,
    sent_a,
    sent_b,
    send_ref,
    keep_ref,
    dqkv_ref,
    turned,
    turned_two,
):
    rows = normed_a.shape[0]
    inner = dq_a.shape[1]
    for pair in range(0, inner, 2 * head_size):
        for at in range(0, 2 * rows, block):
            keys = jnp.zeros((block, 128), f32)
            values = jnp.zeros((block, 128), f32)
            cols = slice(pair, pair + 128)
            span = slice(at, at + block)
            for base, score, prob, dctx in ((0, score_a, prob_a, dctx_a), (rows, score_b, prob_b, dctx_b)):
                if at >= base + rows:
                    continue
                low = max(at - base, 0)
                for number, (query_half, grad_half) in enumerate(
                    zip(even_odd(qkv_ref[base + low : base + rows, cols]), even_odd(dctx[low:rows, cols]), strict=True)
                ):
                    head = pair // head_size + number
                    keys = keys + dot_lt(score[head, low:rows, span], query_half)
                    values = values + dot_lt(prob[head, low:rows, span], grad_half)
            dqkv_ref[span, inner + pair : inner + pair + 128] = keys.astype(bf16)
            dqkv_ref[span, 2 * inner + pair : 2 * inner + pair + 128] = values.astype(bf16)
    dqkv_ref[0:rows, 0:inner] = dq_a[...]
    dqkv_ref[rows : 2 * rows, 0:inner] = dq_b[...]
    turn_rows(normed_a[...], turned, order, 0)
    turn_rows(normed_b[...], turned, order, rows)
    write_grads(idx_ref, turned, dqkv_ref[...], send_ref, keep_ref, 0)
    turn_rows(sent_a[...], turned_two, order, 0)
    turn_rows(sent_b[...], turned_two, order, rows)
    both = jnp.concatenate([ctx_a[...], ctx_b[...]], axis=0)
    write_grads(idx_ref, turned_two, both, send_ref, keep_ref, 3 * inner)


def diagonals(values):
    wide = jnp.concatenate([values, jnp.zeros_like(values)], axis=1)
    total = wide[0:8]
    for at in range(8, block, 8):
        total = total + pltpu.roll(wide[at : at + 8], 2 * block - at, 1)
    row = lax.broadcasted_iota(jnp.int32, total.shape, 0)
    for bit in (1, 2, 4):
        total = jnp.where((row & bit) != 0, pltpu.roll(total, 2 * block - bit, 1), total)
    return jnp.sum(total, axis=0, keepdims=True)


def self_input_kernel(
    idx_ref,
    dqkv_ref,
    own_ref,
    recv_ref,
    wq_ref,
    wkv_ref,
    score_a,
    score_b,
    hot_ref,
    two_a,
    two_b,
    three_a,
    three_b,
    send_ref,
    keep_ref,
    small_ref,
    line,
):
    rows = own_ref.shape[0]
    inner = wq_ref.shape[1]
    mine = idx_ref[0]
    gain_total = jnp.zeros((8, own_ref.shape[1]), f32)
    for which, values_ref in ((1 - mine, recv_ref), (mine, own_ref)):
        span = pl.ds(pl.multiple_of(which * rows, rows), rows)
        grad = (
            dot_rt(dqkv_ref[span, 0:inner], wq_ref[...])
            + dot_rt(dqkv_ref[span, inner : 2 * inner], wkv_ref[0])
            + dot_rt(dqkv_ref[span, 2 * inner :], wkv_ref[1])
        )
        if values_ref is recv_ref:
            send_ref[...] = grad.astype(bf16)
        else:
            keep_ref[...] = grad
        values = values_ref[...].astype(f32)
        terms = grad * values * rms_scale(values)
        gain_total = gain_total + jnp.sum(terms.reshape(rows // 8, 8, -1), axis=0)
    heads = score_a.shape[0]
    count = 2 * rows // block
    line[...] = jnp.zeros_like(line)
    for head in range(heads):
        for step in range(count):
            total = jnp.zeros((block, block), f32)
            for at in range(step, count):
                col = (at - step) * block
                score = score_a if at * block < rows else score_b
                row = at * block % rows
                total = total + score[head, row : row + block, col : col + block].astype(f32)
            line[head : head + 1, step * 2 * block : (step + 1) * 2 * block] = diagonals(total)
    bias = lax.dot_general(
        line[...], hot_ref[...], (((1,), (1,)), ((), ())), precision=lax.Precision.HIGHEST, preferred_element_type=f32
    )
    buckets = hot_ref.shape[0]
    small_ref[...] = jnp.zeros_like(small_ref)
    small_ref[0:1, :] = jnp.sum(gain_total, axis=0, keepdims=True)
    small_ref[1:2, :] = jnp.sum(two_a[...] + two_b[...], axis=0, keepdims=True)
    small_ref[2:3, :] = jnp.sum(three_a[...] + three_b[...], axis=0, keepdims=True)
    small_ref[8:16, 0:buckets] = pick(mine == 0, bias, jnp.zeros_like(bias))
    small_ref[8:16, 128 : 128 + buckets] = pick(mine == 1, bias, jnp.zeros_like(bias))


def input_grad_kernel(idx_ref, own_ref, keep_ref, recv_ref, grad_a, grad_b, gain_ref, out_ref):
    mine = idx_ref[0] == 0
    gain = gain_ref[0:1, :].astype(f32)
    for at in range(0, own_ref.shape[0], block):
        part = slice(at, at + block)
        incoming = keep_ref[part, :] + recv_ref[part, :].astype(f32)
        back, _ = norm_back(own_ref[part, :].astype(f32), gain, incoming)
        out_ref[part, :] = pick(mine, grad_a[part, :], grad_b[part, :]) + back


def flip(values, bit, size):
    return lax.ppermute(values, "dp", [(at, at ^ bit) for at in range(size)])


def swap(values):
    return lax.ppermute(values, "mp", [(0, 1), (1, 0)])


def scatter_rows(send, keep, position, size, bits):
    got = flip(send, bits[0], size)
    for bit in bits[1:]:
        half = keep.shape[0] // 2
        mine = ((position // bit) % 2) * half
        other = half - mine
        take = functools.partial(lax.dynamic_slice_in_dim, slice_size=half, axis=0)
        send = (take(keep, other).astype(f32) + take(got, other).astype(f32)).astype(bf16)
        keep = (take(keep, mine).astype(f32) + take(got, mine).astype(f32)).astype(bf16)
        got = flip(send, bit, size)
    return keep.astype(f32) + got.astype(f32)


def halving_plan(size, width):
    bits = [1 << at for at in range(size.bit_length() - 1)]
    if (width // size) % 16:
        return bits[::-1], [0]
    order = [sum(((at // bit) % 2) * (size // (2 * bit)) for bit in bits) for at in range(size)]
    return bits, order


def body(
    hidden_in,
    memory,
    cotangent,
    self_query,
    self_keyval,
    self_output,
    cross_query,
    cross_keyval,
    cross_output,
    ffn_input,
    ffn_output,
    norm_gains,
    rel_bias,
    dec_segments,
    mem_segments,
    rel_bucket,
):
    dp = lax.axis_size("dp")
    position = lax.axis_index("dp")
    half = lax.axis_index("mp")
    own = hidden_in[0]
    rows, width = own.shape
    length = 2 * rows
    buckets, heads = rel_bias.shape
    inner = self_query.shape[1]
    units = ffn_output.shape[0]
    memory_own = memory[0]
    cot = cotangent[0]
    bits, order = halving_plan(dp, width)
    idx = jnp.stack([half, (position // bits[0]) % 2]).astype(jnp.int32)

    recv = swap(own)
    memory_recv = swap(memory_own)
    cot_recv = swap(cot)

    count = length // block
    lane = np.arange(2 * block)
    spot = np.arange(count)[:, None] * block + np.where(lane < block, -lane, 2 * block - lane)[None]
    spot = np.clip(spot, 0, length - 1).reshape(-1).astype(np.int32)
    firsts = jnp.sum((rel_bucket[None, :] < jnp.arange(buckets + 1, dtype=jnp.int32)[:, None]).astype(jnp.int32), axis=1)
    hot = ((spot[None] >= firsts[:-1, None]) & (spot[None] < firsts[1:, None])).astype(f32)
    line = jnp.einsum("bh,bs->hs", rel_bias, hot.astype(bf16), preferred_element_type=f32)
    line = jnp.pad(line, ((0, 8 - heads), (0, 0)))
    (table,) = call(bias_kernel, "bias_table", [((heads, block, length), bf16)], [line])
    seg_col = dec_segments.reshape(length, 1)

    def self_forward(chunk, extra):
        end = (chunk + 1) * rows
        return call(
            functools.partial(self_forward_kernel, chunk),
            "self_forward_%d" % chunk,
            [
                ((rows, width), bf16),
                ((end, 3 * inner), bf16),
                ((rows, inner), bf16),
                ((heads, rows, end), bf16),
                ((rows, width), bf16),
            ],
            [idx, own, recv, norm_gains, self_query, self_keyval, self_output, seg_col, dec_segments, table] + extra,
            scalars=1,
            flops=2 * rows * width * inner * 4,
        )

    normed_one_a, qkv_a, ctx_one_a, prob_one_a, part_one_a = self_forward(0, [])
    part_one_recv_a = swap(part_one_a)
    normed_one_b, qkv, ctx_one_b, prob_one_b, part_one_b = self_forward(1, [qkv_a])
    part_one_recv_b = swap(part_one_b)

    memory_all, kv = call(
        memory_kernel,
        "memory_keyval",
        [((length, width), bf16), ((length, 2 * inner), bf16)],
        [idx, memory_own, memory_recv, cross_keyval],
        scalars=1,
        flops=2 * length * width * inner * 2,
    )

    def cross_forward(chunk, part, part_recv):
        return call(
            functools.partial(cross_forward_kernel, chunk),
            "cross_forward_%d" % chunk,
            [
                ((rows, width), f32),
                ((rows, width), bf16),
                ((rows, inner), bf16),
                ((rows, inner), bf16),
                ((heads, rows, length), bf16),
                ((rows, width), bf16),
            ],
            [
                idx,
                own,
                recv,
                part,
                part_recv,
                norm_gains,
                cross_query,
                cross_output,
                kv,
                seg_col,
                mem_segments,
            ],
            scalars=1,
            flops=2 * rows * width * inner * 3,
        )

    after_self_a, normed_two_a, query_two_a, ctx_two_a, prob_two_a, part_two_a = cross_forward(
        0, part_one_a, part_one_recv_a
    )
    part_two_recv_a = swap(part_two_a)
    after_self_b, normed_two_b, query_two_b, ctx_two_b, prob_two_b, part_two_b = cross_forward(
        1, part_one_b, part_one_recv_b
    )
    part_two_recv_b = swap(part_two_b)

    def ffn(chunk, after_self, part, part_recv):
        return call(
            functools.partial(ffn_kernel, chunk),
            "ffn_%d" % chunk,
            [
                ((rows, width), f32),
                ((rows, width), bf16),
                ((rows, units), bf16),
                ((rows, 2 * units), bf16),
                ((rows, width), bf16),
            ],
            [idx, after_self, part, part_recv, cot, cot_recv, norm_gains, ffn_input, ffn_output],
            scalars=1,
            scratch=[pltpu.VMEM((rows, width), bf16)],
            flops=2 * rows * width * units * 5,
        )

    after_cross_a, normed_three_a, hidden_a, gate_grads_a, back_three_a = ffn(
        0, after_self_a, part_two_a, part_two_recv_a
    )
    back_three_recv_a = swap(back_three_a)
    after_cross_b, normed_three_b, hidden_b, gate_grads_b, back_three_b = ffn(
        1, after_self_b, part_two_b, part_two_recv_b
    )
    back_three_recv_b = swap(back_three_b)

    ffn_send, ffn_keep = call(
        functools.partial(ffn_grads_kernel, order),
        "ffn_grads",
        [((width // 2, 3 * units), bf16)] * 2,
        [
            idx,
            normed_three_a,
            normed_three_b,
            gate_grads_a,
            gate_grads_b,
            hidden_a,
            hidden_b,
            cot,
            cot_recv,
        ],
        scalars=1,
        scratch=[pltpu.VMEM((width, length), bf16)] * 2,
        flops=2 * length * width * units * 3,
    )
    (out_send,) = call(
        down_kernel,
        "down",
        [((rows, width), bf16)],
        [idx, hidden_a, hidden_b, ffn_output],
        scalars=1,
        flops=2 * rows * width * units,
    )
    out_recv = swap(out_send)
    (output,) = call(
        final_kernel,
        "final",
        [((rows, width), bf16)],
        [idx, hidden_a, hidden_b, after_cross_a, after_cross_b, out_recv, ffn_output],
        scalars=1,
        flops=2 * rows * width * units,
    )

    def cross_back(chunk, after, back, back_recv, prob):
        return call(
            functools.partial(cross_back_kernel, chunk),
            "cross_back_%d" % chunk,
            [
                ((rows, width), f32),
                ((rows, width), bf16),
                ((rows, inner), bf16),
                ((rows, inner), bf16),
                ((heads, rows, length), bf16),
                ((rows, width), bf16),
                ((8, width), f32),
            ],
            [
                idx,
                after,
                back,
                back_recv,
                cot,
                cot_recv,
                norm_gains,
                cross_output,
                cross_query,
                kv,
                prob,
            ],
            scalars=1,
            flops=2 * rows * width * inner * 4,
        )

    grad_cross_a, sent_two_a, dctx_two_a, dq_two_a, score_two_a, back_two_a, three_a = cross_back(
        0, after_cross_a, back_three_a, back_three_recv_a, prob_two_a
    )
    back_two_recv_a = swap(back_two_a)
    grad_cross_b, sent_two_b, dctx_two_b, dq_two_b, score_two_b, back_two_b, three_b = cross_back(
        1, after_cross_b, back_three_b, back_three_recv_b, prob_two_b
    )
    back_two_recv_b = swap(back_two_b)

    cross_send, cross_keep, memory_send, memory_keep = call(
        functools.partial(cross_grads_kernel, order),
        "cross_grads",
        [
            ((width // 2, 4 * inner), bf16),
            ((width // 2, 4 * inner), bf16),
            ((rows, width), bf16),
            ((rows, width), f32),
        ],
        [
            idx,
            normed_two_a,
            normed_two_b,
            dq_two_a,
            dq_two_b,
            query_two_a,
            query_two_b,
            score_two_a,
            score_two_b,
            prob_two_a,
            prob_two_b,
            dctx_two_a,
            dctx_two_b,
            ctx_two_a,
            ctx_two_b,
            sent_two_a,
            sent_two_b,
            memory_all,
            cross_keyval,
        ],
        scalars=1,
        scratch=[pltpu.VMEM((width, length), bf16)] * 3 + [pltpu.VMEM((length, 2 * inner), bf16)],
        flops=2 * length * width * inner * 8,
    )
    grad_memory = memory_keep + swap(memory_send).astype(f32)

    def self_back(chunk, after, back, back_recv, grad_cross, prob):
        end = (chunk + 1) * rows
        return call(
            functools.partial(self_back_kernel, chunk),
            "self_back_%d" % chunk,
            [
                ((rows, width), f32),
                ((rows, width), bf16),
                ((rows, inner), bf16),
                ((rows, inner), bf16),
                ((heads, rows, end), bf16),
                ((8, width), f32),
            ],
            [idx, after, back, back_recv, grad_cross, norm_gains, self_output, qkv, prob],
            scalars=1,
            flops=2 * rows * width * inner * 3,
        )

    grad_self_a, sent_one_a, dctx_one_a, dq_one_a, score_one_a, two_a = self_back(
        0, after_self_a, back_two_a, back_two_recv_a, grad_cross_a, prob_one_a
    )
    grad_self_b, sent_one_b, dctx_one_b, dq_one_b, score_one_b, two_b = self_back(
        1, after_self_b, back_two_b, back_two_recv_b, grad_cross_b, prob_one_b
    )

    self_send, self_keep, dqkv = call(
        functools.partial(self_grads_kernel, order),
        "self_grads",
        [((width // 2, 4 * inner), bf16), ((width // 2, 4 * inner), bf16), ((length, 3 * inner), bf16)],
        [
            idx,
            normed_one_a,
            normed_one_b,
            dq_one_a,
            dq_one_b,
            qkv,
            score_one_a,
            score_one_b,
            prob_one_a,
            prob_one_b,
            dctx_one_a,
            dctx_one_b,
            ctx_one_a,
            ctx_one_b,
            sent_one_a,
            sent_one_b,
        ],
        scalars=1,
        scratch=[pltpu.VMEM((width, length), bf16)] * 2,
        flops=2 * length * width * inner * 6,
    )
    back_one_send, back_one_keep, small = call(
        self_input_kernel,
        "self_input",
        [((rows, width), bf16), ((rows, width), f32), ((16, width), f32)],
        [
            idx,
            dqkv,
            own,
            recv,
            self_query,
            self_keyval,
            score_one_a,
            score_one_b,
            hot,
            two_a,
            two_b,
            three_a,
            three_b,
        ],
        scalars=1,
        scratch=[pltpu.VMEM((8, 2 * length), f32)],
        flops=2 * length * width * inner * 3,
    )
    back_one_recv = swap(back_one_send)
    bit = 1
    while bit < dp:
        small = small + flip(small, bit, dp)
        bit *= 2
    small = small + swap(small)
    (grad_input,) = call(
        input_grad_kernel,
        "input_grad",
        [((rows, width), f32)],
        [idx, own, back_one_keep, back_one_recv, grad_self_a, grad_self_b, norm_gains],
        scalars=1,
    )

    def scatter(send, keep):
        return scatter_rows(send, keep, position, dp, bits)

    ffn_sum = scatter(ffn_send, ffn_keep)
    cross_sum = scatter(cross_send, cross_keep)
    self_sum = scatter(self_send, self_keep)
    e = inner
    return (
        output[None],
        grad_input[None],
        grad_memory[None],
        self_sum[:, 0:e],
        jnp.stack([self_sum[:, e : 2 * e], self_sum[:, 2 * e : 3 * e]]),
        self_sum[:, 3 * e :].T,
        cross_sum[:, 0:e],
        jnp.stack([cross_sum[:, e : 2 * e], cross_sum[:, 2 * e : 3 * e]]),
        cross_sum[:, 3 * e :].T,
        jnp.stack([ffn_sum[:, 0:units], ffn_sum[:, units : 2 * units]]),
        ffn_sum[:, 2 * units :].T,
        small[0:3],
        jnp.concatenate([small[8 : 8 + heads, 0:buckets], small[8 : 8 + heads, 128 : 128 + buckets]]).T,
    )


def solution(mesh):
    in_specs = (
        P("dp", "mp", None),
        P("dp", "mp", None),
        P("dp", "mp", None),
        P(None, "mp"),
        P(None, None, "mp"),
        P("mp", None),
        P(None, "mp"),
        P(None, None, "mp"),
        P("mp", None),
        P(None, None, "mp"),
        P("mp", None),
        P(),
        P(None, "mp"),
        P("dp", None),
        P("dp", None),
        P(),
    )
    out_specs = (
        P("dp", "mp", None),
        P("dp", "mp", None),
        P("dp", "mp", None),
        P("dp", "mp"),
        P(None, "dp", "mp"),
        P("mp", "dp"),
        P("dp", "mp"),
        P(None, "dp", "mp"),
        P("mp", "dp"),
        P(None, "dp", "mp"),
        P("mp", "dp"),
        P(),
        P(),
    )
    return jax.shard_map(body, mesh=mesh, in_specs=in_specs, out_specs=out_specs, check_vma=False)
```

```python
import functools

import jax
import jax.numpy as jnp
import numpy as np
from jax import lax
from jax.experimental import pallas as pl
from jax.experimental.pallas import tpu as pltpu
from jax.sharding import PartitionSpec as P

epsilon = 1e-06
masked_score = -1e30
gelu_root = float(np.sqrt(2.0 / np.pi))
gelu_cubic = 0.044715
block = 128
head_size = 64
f32 = jnp.float32
bf16 = jnp.bfloat16


def dot(left, right):
    return lax.dot_general(left, right, (((1,), (0,)), ((), ())), preferred_element_type=f32)


def dot_rt(left, right):
    return lax.dot_general(left, right, (((1,), (1,)), ((), ())), preferred_element_type=f32)


def dot_lt(left, right):
    return lax.dot_general(left, right, (((0,), (0,)), ((), ())), preferred_element_type=f32)


def pick(flag, first, second):
    return jnp.where(flag, first, second)


def even_odd(values):
    lane = lax.broadcasted_iota(jnp.int32, values.shape, 1)
    zero = jnp.zeros_like(values)
    return jnp.where(lane < head_size, values, zero), jnp.where(lane < head_size, zero, values)


def rms_scale(values):
    return lax.rsqrt(jnp.mean(values * values, axis=-1, keepdims=True) + epsilon)


def norm_back(values, gain, grad):
    scale = rms_scale(values)
    scaled = grad * gain
    inner = jnp.mean(values * scaled, axis=-1, keepdims=True)
    back = scale * scaled - values * (scale * scale * scale * inner)
    return back, grad * values * scale


def softmax(scores):
    top = jnp.max(scores, axis=-1, keepdims=True)
    weights = jnp.exp(scores - top)
    total = jnp.sum(weights, axis=-1, keepdims=True)
    return (weights * (1.0 / total)).astype(bf16)


times = {"cross_back_a": 60.0, "self_back_a": 60.0, "self_back_b": 60.0, "halve_cross": 60.0}


class Made:
    def __init__(self, shape, dtype):
        self.shape, self.dtype, self.value = shape, dtype, None


def settled(arg):
    return arg.value if isinstance(arg, Made) and arg.value is not None else arg


class Group:
    def __init__(self, name, cost=0):
        self.name, self.cost, self.stages, self.inputs = name, cost, [], []

    def add(self, kernel, outs, args, scratch=(), flops=0):
        made = [Made(shape, dtype) for shape, dtype in outs]
        args = [settled(arg) for arg in args]
        self.stages.append((kernel, list(args), made, list(scratch)))
        self.cost += flops
        for arg in args:
            if not isinstance(arg, Made) and not any(arg is known for known in self.inputs):
                self.inputs.append(arg)
        return made

    def call(self, idx):
        made = [out for stage in self.stages for out in stage[2]]
        scratch = [item for stage in self.stages for item in stage[3]]

        def kernel(idx_ref, *refs):
            ins, refs = refs[: len(self.inputs)], refs[len(self.inputs) :]
            outs, spare = refs[: len(made)], list(refs[len(made) :])
            known = [(value, ref) for value, ref in zip(self.inputs + made, ins + outs, strict=True)]
            for body, args, stage_outs, stage_scratch in self.stages:
                taken = [next(ref for value, ref in known if value is item) for item in args + stage_outs]
                body(idx_ref, *taken, *[spare.pop(0) for _ in stage_scratch])

        out_shape = [jax.ShapeDtypeStruct(out.shape, out.dtype) for out in made]
        moved = sum(x.size * x.dtype.itemsize for x in self.inputs + out_shape)
        values = pl.pallas_call(
            kernel,
            name=self.name,
            out_shape=out_shape,
            in_specs=[pl.BlockSpec(memory_space=pltpu.SMEM)]
            + [pl.BlockSpec(memory_space=pltpu.VMEM)] * len(self.inputs),
            out_specs=[pl.BlockSpec(memory_space=pltpu.VMEM)] * len(made),
            scratch_shapes=scratch,
            compiler_params=pltpu.CompilerParams(vmem_limit_bytes=8 << 20),
            cost_estimate=pl.CostEstimate(flops=int(times.get(self.name, 0.01) * 1.15e9), transcendentals=0, bytes_accessed=1024),
        )(idx, *self.inputs)
        for out, value in zip(made, values, strict=True):
            out.value = value
        return values


def bias_kernel(idx_ref, line_ref, table_ref):
    heads = table_ref.shape[0]
    count = table_ref.shape[2] // block
    for head in range(heads):
        for step in range(count):
            line = line_ref[head : head + 1, step * 2 * block : (step + 1) * 2 * block]
            wide = jnp.broadcast_to(line, (block, 2 * block))
            turned = pltpu.roll(wide, 0, 1, stride=1, stride_axis=0)
            at = (count - 1 - step) * block
            table_ref[head, :, at : at + block] = turned[:, :block].astype(bf16)


def self_forward_kernel(chunk, *refs):
    refs = list(refs)
    idx_ref, own_ref, recv_ref, gain_ref, wq_ref, wkv_ref, wo_ref, segc_ref, segr_ref, table_ref = refs[:10]
    refs = refs[10:]
    if chunk:
        before_ref = refs.pop(0)
    normed_ref, qkv_ref, ctx_ref, prob_ref, part_ref = refs
    mine = idx_ref[0] == chunk
    rows, width = own_ref.shape
    inner = wq_ref.shape[1]
    base = chunk * rows
    gain = gain_ref[0:1, :].astype(f32)
    for at in range(0, rows, block):
        values = pick(mine, own_ref[at : at + block, :], recv_ref[at : at + block, :]).astype(f32)
        normed_ref[at : at + block, :] = (values * rms_scale(values) * gain).astype(bf16)
    normed = normed_ref[...]
    if chunk:
        qkv_ref[0:base, :] = before_ref[...]
    qkv_ref[base : base + rows, 0:inner] = dot(normed, wq_ref[...]).astype(bf16)
    qkv_ref[base : base + rows, inner : 2 * inner] = dot(normed, wkv_ref[0]).astype(bf16)
    qkv_ref[base : base + rows, 2 * inner : 3 * inner] = dot(normed, wkv_ref[1]).astype(bf16)
    total = table_ref.shape[2]
    masks = []
    for at in range(0, rows, block):
        keys = base + at + block
        allowed = segc_ref[base + at : keys, :] == segr_ref[:, 0:keys]
        row = lax.broadcasted_iota(jnp.int32, (block, keys), 0) + (base + at)
        col = lax.broadcasted_iota(jnp.int32, (block, keys), 1)
        masks.append(jnp.where(allowed & (row >= col), 0.0, masked_score))
    for pair in range(0, inner, 2 * head_size):
        keys2 = qkv_ref[0 : base + rows, inner + pair : inner + pair + 128]
        values_e, values_o = even_odd(qkv_ref[0 : base + rows, 2 * inner + pair : 2 * inner + pair + 128])
        for number, at in enumerate(range(0, rows, block)):
            keys = base + at + block
            query_e, query_o = even_odd(qkv_ref[base + at : keys, pair : pair + 128])
            context = jnp.zeros((block, 128), f32)
            for head, query, values in (
                (pair // head_size, query_e, values_e),
                (pair // head_size + 1, query_o, values_o),
            ):
                scores = dot_rt(query, keys2[0:keys]) + table_ref[head, :, total - keys :].astype(f32)
                probs = softmax(scores + masks[number])
                prob_ref[head, at : at + block, 0:keys] = probs
                context = context + dot(probs, values[0:keys])
            ctx_ref[at : at + block, pair : pair + 128] = context.astype(bf16)
    part_ref[...] = dot(ctx_ref[...], wo_ref[...]).astype(bf16)


def memory_kernel(idx_ref, own_ref, recv_ref, wkv_ref, memory_ref, kv_ref):
    rows = own_ref.shape[0]
    inner = wkv_ref.shape[2]
    mine = idx_ref[0]
    memory_ref[pl.ds(pl.multiple_of(mine * rows, rows), rows), :] = own_ref[...]
    memory_ref[pl.ds(pl.multiple_of((1 - mine) * rows, rows), rows), :] = recv_ref[...]
    kv_ref[:, 0:inner] = dot(memory_ref[...], wkv_ref[0]).astype(bf16)
    kv_ref[:, inner : 2 * inner] = dot(memory_ref[...], wkv_ref[1]).astype(bf16)


def cross_forward_kernel(
    chunk,
    idx_ref,
    own_ref,
    recv_ref,
    part_ref,
    part_recv_ref,
    gain_ref,
    wq_ref,
    wo_ref,
    kv_ref,
    segc_ref,
    segm_ref,
    after_ref,
    normed_ref,
    query_ref,
    ctx_ref,
    prob_ref,
    out_ref,
):
    mine = idx_ref[0] == chunk
    rows = own_ref.shape[0]
    inner = wq_ref.shape[1]
    gain = gain_ref[1:2, :].astype(f32)
    for at in range(0, rows, block):
        part = slice(at, at + block)
        values = pick(mine, own_ref[part, :], recv_ref[part, :]).astype(f32)
        values = values + (part_ref[part, :].astype(f32) + part_recv_ref[part, :].astype(f32))
        after_ref[part, :] = values
        normed_ref[part, :] = (values * rms_scale(values) * gain).astype(bf16)
    query_ref[...] = dot(normed_ref[...], wq_ref[...]).astype(bf16)
    masks = []
    for at in range(0, rows, block):
        allowed = segc_ref[chunk * rows + at : chunk * rows + at + block, :] == segm_ref[...]
        masks.append(jnp.where(allowed, 0.0, masked_score))
    for pair in range(0, inner, 2 * head_size):
        keys2 = kv_ref[:, pair : pair + 128]
        values_e, values_o = even_odd(kv_ref[:, inner + pair : inner + pair + 128])
        for number, at in enumerate(range(0, rows, block)):
            query_e, query_o = even_odd(query_ref[at : at + block, pair : pair + 128])
            context = jnp.zeros((block, 128), f32)
            for head, query, values in (
                (pair // head_size, query_e, values_e),
                (pair // head_size + 1, query_o, values_o),
            ):
                probs = softmax(dot_rt(query, keys2) + masks[number])
                prob_ref[head, at : at + block, :] = probs
                context = context + dot(probs, values)
            ctx_ref[at : at + block, pair : pair + 128] = context.astype(bf16)
    out_ref[...] = dot(ctx_ref[...], wo_ref[...]).astype(bf16)


def ffn_kernel(
    chunk,
    idx_ref,
    after_self_ref,
    part_ref,
    part_recv_ref,
    cot_ref,
    cot_recv_ref,
    gain_ref,
    win_ref,
    wout_ref,
    after_ref,
    normed_ref,
    hidden_ref,
    grads_ref,
    back_ref,
    cot_scr,
):
    mine = idx_ref[0] == chunk
    rows = after_self_ref.shape[0]
    units = win_ref.shape[2]
    gain = gain_ref[2:3, :].astype(f32)
    for at in range(0, rows, block):
        part = slice(at, at + block)
        values = after_self_ref[part, :] + (
            part_ref[part, :].astype(f32) + part_recv_ref[part, :].astype(f32)
        )
        after_ref[part, :] = values
        normed_ref[part, :] = (values * rms_scale(values) * gain).astype(bf16)
        cot_scr[part, :] = pick(mine, cot_ref[part, :], cot_recv_ref[part, :])
    wide = 256
    for at in range(0, units, wide):
        cols = slice(at, at + wide)
        gate = dot(normed_ref[...], win_ref[0, :, cols])
        upward = dot(normed_ref[...], win_ref[1, :, cols])
        grad = dot_rt(cot_scr[...], wout_ref[cols, :])
        square = gate * gate
        bend = jnp.tanh(gelu_root * gate * (1.0 + gelu_cubic * square))
        half = 0.5 * (1.0 + bend)
        gelu = gate * half
        slope = half + 0.5 * gelu_root * gate * (1.0 - bend * bend) * (1.0 + 3.0 * gelu_cubic * square)
        hidden_ref[:, cols] = (gelu * upward).astype(bf16)
        grads_ref[:, cols] = (grad * upward * slope).astype(bf16)
        grads_ref[:, units + at : units + at + wide] = (grad * gelu).astype(bf16)
    back_ref[...] = (
        dot_rt(grads_ref[:, 0:units], win_ref[0]) + dot_rt(grads_ref[:, units:], win_ref[1])
    ).astype(bf16)


def down_kernel(idx_ref, first_ref, second_ref, wout_ref, out_ref):
    out_ref[...] = dot(pick(idx_ref[0] == 0, second_ref[...], first_ref[...]), wout_ref[...]).astype(bf16)


def final_kernel(idx_ref, hid_a, hid_b, after_a, after_b, recv_ref, wout_ref, out_ref):
    mine = idx_ref[0] == 0
    own = dot(pick(mine, hid_a[...], hid_b[...]), wout_ref[...])
    out_ref[...] = (pick(mine, after_a[...], after_b[...]) + (own + recv_ref[...].astype(f32))).astype(bf16)


def turn_rows(values, place_ref, order, at):
    turned = jnp.transpose(values)
    size = turned.shape[0] // len(order)
    for number, position in enumerate(order):
        place_ref[position * size : (position + 1) * size, at : at + values.shape[0]] = turned[
            number * size : (number + 1) * size
        ]


def write_grads(bit_ref, turned_ref, right, send_ref, keep_ref, at):
    rows = send_ref.shape[0]
    mine = bit_ref[1]
    cols = slice(at, at + right.shape[1])
    keep_ref[:, cols] = dot(turned_ref[pl.ds(pl.multiple_of(mine * rows, rows), rows), :], right).astype(bf16)
    send_ref[:, cols] = dot(turned_ref[pl.ds(pl.multiple_of((1 - mine) * rows, rows), rows), :], right).astype(bf16)


def ffn_grads_kernel(
    orders,
    idx_ref,
    normed_a,
    normed_b,
    grads_a,
    grads_b,
    hidden_a,
    hidden_b,
    cot_ref,
    cot_recv_ref,
    send_first,
    keep_first,
    send_second,
    keep_second,
    turned,
    turned_two,
    turned_three,
):
    rows = normed_a.shape[0]
    mine = idx_ref[0] == 0
    units = hidden_a.shape[1]
    cut = send_first.shape[1]
    turn_rows(normed_a[...], turned, orders[0], 0)
    turn_rows(normed_b[...], turned, orders[0], rows)
    turn_rows(normed_a[...], turned_two, orders[1], 0)
    turn_rows(normed_b[...], turned_two, orders[1], rows)
    turn_rows(pick(mine, cot_ref[...], cot_recv_ref[...]), turned_three, orders[1], 0)
    turn_rows(pick(mine, cot_recv_ref[...], cot_ref[...]), turned_three, orders[1], rows)
    both = jnp.concatenate([grads_a[...], grads_b[...]], axis=0)
    write_grads(idx_ref, turned, both[:, :cut], send_first, keep_first, 0)
    write_grads(idx_ref, turned_two, both[:, cut:], send_second, keep_second, 0)
    hidden = jnp.concatenate([hidden_a[...], hidden_b[...]], axis=0)
    write_grads(idx_ref, turned_three, hidden, send_second, keep_second, 2 * units - cut)


def attend_back(query_rows, prob_ref, score_ref, grad_ref, key_of, value_of, dq_ref, inner, reach):
    for pair in range(0, inner, 2 * head_size):
        keys_e, keys_o = even_odd(key_of(pair))
        values2 = value_of(pair)
        for at in range(0, query_rows, block):
            keys = reach(at)
            grad_e, grad_o = even_odd(grad_ref[at : at + block, pair : pair + 128])
            total = jnp.zeros((block, 128), f32)
            for head, grad, key in (
                (pair // head_size, grad_e, keys_e),
                (pair // head_size + 1, grad_o, keys_o),
            ):
                probs = prob_ref[head, at : at + block, 0:keys].astype(f32)
                grad_probs = dot_rt(grad, values2[0:keys])
                delta = jnp.sum(probs * grad_probs, axis=-1, keepdims=True) / jnp.sum(
                    probs, axis=-1, keepdims=True
                )
                scores = (probs * (grad_probs - delta)).astype(bf16)
                score_ref[head, at : at + block, 0:keys] = scores
                total = total + dot(scores, key[0:keys])
            dq_ref[at : at + block, pair : pair + 128] = total.astype(bf16)


def cross_back_kernel(
    chunk,
    idx_ref,
    after_ref,
    back_ref,
    back_recv_ref,
    cot_ref,
    cot_recv_ref,
    gain_ref,
    wo_ref,
    wq_ref,
    kv_ref,
    prob_ref,
    grad_ref,
    sent_ref,
    dctx_ref,
    dq_ref,
    score_ref,
    out_ref,
    gain_out_ref,
):
    mine = idx_ref[0] == chunk
    rows = after_ref.shape[0]
    inner = wq_ref.shape[1]
    gain = gain_ref[2:3, :].astype(f32)
    gain_total = jnp.zeros((8, gain.shape[1]), f32)
    for at in range(0, rows, block):
        part = slice(at, at + block)
        incoming = back_ref[part, :].astype(f32) + back_recv_ref[part, :].astype(f32)
        back, gain_terms = norm_back(after_ref[part, :], gain, incoming)
        total = pick(mine, cot_ref[part, :], cot_recv_ref[part, :]).astype(f32) + back
        grad_ref[part, :] = total
        sent_ref[part, :] = total.astype(bf16)
        gain_total = gain_total + jnp.sum(gain_terms.reshape(block // 8, 8, -1), axis=0)
    gain_out_ref[...] = pick(mine, gain_total, jnp.zeros_like(gain_total))
    dctx_ref[...] = dot_rt(sent_ref[...], wo_ref[...]).astype(bf16)
    attend_back(
        rows,
        prob_ref,
        score_ref,
        dctx_ref,
        lambda pair: kv_ref[:, pair : pair + 128],
        lambda pair: kv_ref[:, inner + pair : inner + pair + 128],
        dq_ref,
        inner,
        lambda at: kv_ref.shape[0],
    )
    out_ref[...] = dot_rt(dq_ref[...], wq_ref[...]).astype(bf16)


def cross_grads_kernel(
    order,
    idx_ref,
    normed_a,
    normed_b,
    dq_a,
    dq_b,
    query_a,
    query_b,
    score_a,
    score_b,
    prob_a,
    prob_b,
    dctx_a,
    dctx_b,
    ctx_a,
    ctx_b,
    sent_a,
    sent_b,
    memory_ref,
    wkv_ref,
    send_ref,
    keep_ref,
    memory_send_ref,
    memory_keep_ref,
    turned,
    turned_two,
    turned_three,
    dkv,
):
    rows = normed_a.shape[0]
    inner = dq_a.shape[1]
    for pair in range(0, inner, 2 * head_size):
        keys = jnp.zeros((dkv.shape[0], 128), f32)
        values = jnp.zeros((dkv.shape[0], 128), f32)
        for score, prob, query, dctx in ((score_a, prob_a, query_a, dctx_a), (score_b, prob_b, query_b, dctx_b)):
            cols = slice(pair, pair + 128)
            for number, (query_half, grad_half) in enumerate(
                zip(even_odd(query[:, cols]), even_odd(dctx[:, cols]), strict=True)
            ):
                head = pair // head_size + number
                keys = keys + dot_lt(score[head], query_half)
                values = values + dot_lt(prob[head], grad_half)
        dkv[:, pair : pair + 128] = keys.astype(bf16)
        dkv[:, inner + pair : inner + pair + 128] = values.astype(bf16)
    mine = idx_ref[0]
    other = pl.ds(pl.multiple_of((1 - mine) * rows, rows), rows)
    own = pl.ds(pl.multiple_of(mine * rows, rows), rows)
    memory_send_ref[...] = (
        dot_rt(dkv[other, 0:inner], wkv_ref[0]) + dot_rt(dkv[other, inner:], wkv_ref[1])
    ).astype(bf16)
    memory_keep_ref[...] = dot_rt(dkv[own, 0:inner], wkv_ref[0]) + dot_rt(dkv[own, inner:], wkv_ref[1])
    turn_rows(normed_a[...], turned, order, 0)
    turn_rows(normed_b[...], turned, order, rows)
    both = jnp.concatenate([dq_a[...], dq_b[...]], axis=0)
    write_grads(idx_ref, turned, both, send_ref, keep_ref, 0)
    turn_rows(memory_ref[...], turned_two, order, 0)
    write_grads(idx_ref, turned_two, dkv[...], send_ref, keep_ref, inner)
    turn_rows(sent_a[...], turned_three, order, 0)
    turn_rows(sent_b[...], turned_three, order, rows)
    both = jnp.concatenate([ctx_a[...], ctx_b[...]], axis=0)
    write_grads(idx_ref, turned_three, both, send_ref, keep_ref, 3 * inner)


def self_back_kernel(
    chunk,
    idx_ref,
    after_ref,
    back_ref,
    back_recv_ref,
    cross_ref,
    gain_ref,
    wo_ref,
    qkv_ref,
    prob_ref,
    grad_ref,
    sent_ref,
    dctx_ref,
    dq_ref,
    score_ref,
    gain_out_ref,
):
    mine = idx_ref[0] == chunk
    rows = after_ref.shape[0]
    inner = wo_ref.shape[0]
    gain = gain_ref[1:2, :].astype(f32)
    gain_total = jnp.zeros((8, gain.shape[1]), f32)
    for at in range(0, rows, block):
        part = slice(at, at + block)
        incoming = back_ref[part, :].astype(f32) + back_recv_ref[part, :].astype(f32)
        back, gain_terms = norm_back(after_ref[part, :], gain, incoming)
        total = cross_ref[part, :] + back
        grad_ref[part, :] = total
        sent_ref[part, :] = total.astype(bf16)
        gain_total = gain_total + jnp.sum(gain_terms.reshape(block // 8, 8, -1), axis=0)
    gain_out_ref[...] = pick(mine, gain_total, jnp.zeros_like(gain_total))
    dctx_ref[...] = dot_rt(sent_ref[...], wo_ref[...]).astype(bf16)
    end = (chunk + 1) * rows
    attend_back(
        rows,
        prob_ref,
        score_ref,
        dctx_ref,
        lambda pair: qkv_ref[0:end, inner + pair : inner + pair + 128],
        lambda pair: qkv_ref[0:end, 2 * inner + pair : 2 * inner + pair + 128],
        dq_ref,
        inner,
        lambda at: chunk * rows + at + block,
    )


def self_grads_kernel(
    order,
    idx_ref,
    normed_a,
    normed_b,
    dq_a,
    dq_b,
    qkv_ref,
    score_a,
    score_b,
    prob_a,
    prob_b,
    dctx_a,
    dctx_b,
    ctx_a,
    ctx_b,
    sent_a,
    sent_b,
    send_ref,
    keep_ref,
    dqkv_ref,
    turned,
    turned_two,
):
    rows = normed_a.shape[0]
    inner = dq_a.shape[1]
    for pair in range(0, inner, 2 * head_size):
        for at in range(0, 2 * rows, block):
            keys = jnp.zeros((block, 128), f32)
            values = jnp.zeros((block, 128), f32)
            cols = slice(pair, pair + 128)
            span = slice(at, at + block)
            for base, score, prob, dctx in ((0, score_a, prob_a, dctx_a), (rows, score_b, prob_b, dctx_b)):
                if at >= base + rows:
                    continue
                low = max(at - base, 0)
                for number, (query_half, grad_half) in enumerate(
                    zip(even_odd(qkv_ref[base + low : base + rows, cols]), even_odd(dctx[low:rows, cols]), strict=True)
                ):
                    head = pair // head_size + number
                    keys = keys + dot_lt(score[head, low:rows, span], query_half)
                    values = values + dot_lt(prob[head, low:rows, span], grad_half)
            dqkv_ref[span, inner + pair : inner + pair + 128] = keys.astype(bf16)
            dqkv_ref[span, 2 * inner + pair : 2 * inner + pair + 128] = values.astype(bf16)
    dqkv_ref[0:rows, 0:inner] = dq_a[...]
    dqkv_ref[rows : 2 * rows, 0:inner] = dq_b[...]
    turn_rows(normed_a[...], turned, order, 0)
    turn_rows(normed_b[...], turned, order, rows)
    write_grads(idx_ref, turned, dqkv_ref[...], send_ref, keep_ref, 0)
    turn_rows(sent_a[...], turned_two, order, 0)
    turn_rows(sent_b[...], turned_two, order, rows)
    both = jnp.concatenate([ctx_a[...], ctx_b[...]], axis=0)
    write_grads(idx_ref, turned_two, both, send_ref, keep_ref, 3 * inner)


def diagonals(values):
    wide = jnp.concatenate([values, jnp.zeros_like(values)], axis=1)
    total = wide[0:8]
    for at in range(8, block, 8):
        total = total + pltpu.roll(wide[at : at + 8], 2 * block - at, 1)
    row = lax.broadcasted_iota(jnp.int32, total.shape, 0)
    for bit in (1, 2, 4):
        total = jnp.where((row & bit) != 0, pltpu.roll(total, 2 * block - bit, 1), total)
    return jnp.sum(total, axis=0, keepdims=True)


def self_input_kernel(
    idx_ref,
    dqkv_ref,
    own_ref,
    recv_ref,
    wq_ref,
    wkv_ref,
    score_a,
    score_b,
    hot_ref,
    two_a,
    two_b,
    three_a,
    three_b,
    send_ref,
    keep_ref,
    small_ref,
    line,
):
    rows = own_ref.shape[0]
    inner = wq_ref.shape[1]
    mine = idx_ref[0]
    gain_total = jnp.zeros((8, own_ref.shape[1]), f32)
    for which, values_ref in ((1 - mine, recv_ref), (mine, own_ref)):
        span = pl.ds(pl.multiple_of(which * rows, rows), rows)
        grad = (
            dot_rt(dqkv_ref[span, 0:inner], wq_ref[...])
            + dot_rt(dqkv_ref[span, inner : 2 * inner], wkv_ref[0])
            + dot_rt(dqkv_ref[span, 2 * inner :], wkv_ref[1])
        )
        if values_ref is recv_ref:
            send_ref[...] = grad.astype(bf16)
        else:
            keep_ref[...] = grad
        values = values_ref[...].astype(f32)
        terms = grad * values * rms_scale(values)
        gain_total = gain_total + jnp.sum(terms.reshape(rows // 8, 8, -1), axis=0)
    heads = score_a.shape[0]
    count = 2 * rows // block
    line[...] = jnp.zeros_like(line)
    for head in range(heads):
        for step in range(count):
            total = jnp.zeros((block, block), f32)
            for at in range(step, count):
                col = (at - step) * block
                score = score_a if at * block < rows else score_b
                row = at * block % rows
                total = total + score[head, row : row + block, col : col + block].astype(f32)
            line[head : head + 1, step * 2 * block : (step + 1) * 2 * block] = diagonals(total)
    bias = lax.dot_general(
        line[...], hot_ref[...], (((1,), (1,)), ((), ())), precision=lax.Precision.HIGHEST, preferred_element_type=f32
    )
    buckets = hot_ref.shape[0]
    small_ref[...] = jnp.zeros_like(small_ref)
    small_ref[0:1, :] = jnp.sum(gain_total, axis=0, keepdims=True)
    small_ref[1:2, :] = jnp.sum(two_a[...] + two_b[...], axis=0, keepdims=True)
    small_ref[2:3, :] = jnp.sum(three_a[...] + three_b[...], axis=0, keepdims=True)
    small_ref[8:16, 0:buckets] = pick(mine == 0, bias, jnp.zeros_like(bias))
    small_ref[8:16, 128 : 128 + buckets] = pick(mine == 1, bias, jnp.zeros_like(bias))


def input_grad_kernel(idx_ref, own_ref, keep_ref, recv_ref, grad_a, grad_b, gain_ref, out_ref):
    mine = idx_ref[0] == 0
    gain = gain_ref[0:1, :].astype(f32)
    for at in range(0, own_ref.shape[0], block):
        part = slice(at, at + block)
        incoming = keep_ref[part, :] + recv_ref[part, :].astype(f32)
        back, _ = norm_back(own_ref[part, :].astype(f32), gain, incoming)
        out_ref[part, :] = pick(mine, grad_a[part, :], grad_b[part, :]) + back


def halve_kernel(slot, idx_ref, keep_ref, got_ref, send_out, keep_out):
    rows = send_out.shape[0]
    mine = idx_ref[slot]
    other = pl.ds(pl.multiple_of((1 - mine) * rows, 16), rows)
    own = pl.ds(pl.multiple_of(mine * rows, 16), rows)
    send_out[...] = (keep_ref[other, :].astype(f32) + got_ref[other, :].astype(f32)).astype(bf16)
    keep_out[...] = (keep_ref[own, :].astype(f32) + got_ref[own, :].astype(f32)).astype(bf16)


def add_kernel(idx_ref, first_ref, second_ref, out_ref):
    out_ref[...] = first_ref[...] + second_ref[...]


def finish_kernel(idx_ref, *refs):
    count = next(at for at, ref in enumerate(refs) if ref.dtype == f32)
    starts = [0]
    for keep_ref in refs[0:count:2]:
        starts.append(starts[-1] + keep_ref.shape[1])

    def pieces(low, high):
        for number, start in enumerate(starts[:-1]):
            at, end = max(low, start), min(high, starts[number + 1])
            if at < end:
                cols = slice(at - start, end - start)
                yield at - low, end - low, refs[2 * number][:, cols].astype(f32) + refs[2 * number + 1][:, cols].astype(f32)

    at = 0
    for out in refs[count:]:
        for values in [out] if len(out.shape) == 2 else [out.at[n] for n in range(out.shape[0])]:
            for low, high, total in pieces(at, at + values.shape[1]):
                values[:, low:high] = total
            at += values.shape[1]


def flip(values, bit, size):
    return lax.ppermute(settled(values), "dp", [(at, at ^ bit) for at in range(size)])


def swap(values):
    return lax.ppermute(settled(values), "mp", [(0, 1), (1, 0)])


def halving_plans(size, width):
    bits = [1 << at for at in range(size.bit_length() - 1)]
    if (width // size) % 16:
        return (bits[::-1], [0]), (bits[::-1], [0])
    plans = []
    for steps in (bits, bits[:1] + bits[2:] + bits[1:2]):
        order = [sum(((at // bit) % 2) * (size >> (step + 1)) for step, bit in enumerate(steps)) for at in range(size)]
        plans.append((steps, order))
    return plans


def body(
    hidden_in,
    memory,
    cotangent,
    self_query,
    self_keyval,
    self_output,
    cross_query,
    cross_keyval,
    cross_output,
    ffn_input,
    ffn_output,
    norm_gains,
    rel_bias,
    dec_segments,
    mem_segments,
    rel_bucket,
):
    dp = lax.axis_size("dp")
    position = lax.axis_index("dp")
    half = lax.axis_index("mp")
    own = hidden_in[0]
    rows, width = own.shape
    length = 2 * rows
    buckets, heads = rel_bias.shape
    inner = self_query.shape[1]
    units = ffn_output.shape[0]
    memory_own = memory[0]
    cot = cotangent[0]
    plan_a, plan_b = halving_plans(dp, width)
    bits = sorted(plan_a[0])
    first = plan_a[0][0]
    idx = jnp.stack([half, (position // first) % 2] + [(position // bit) % 2 for bit in bits]).astype(jnp.int32)
    order_token = [idx]

    def run(group):
        values = group.call(order_token[0])
        order_token[0] = lax.optimization_barrier((idx, values[-1]))[0]
        return values

    def single(name, kernel, outs, args, **options):
        group = Group(name)
        group.add(kernel, outs, args, **options)
        return run(group)

    class Scatter:
        def __init__(self, steps, send, keep):
            self.keep, self.steps, self.at = keep, steps, 0
            self.got = flip(send, steps[0], dp)

        def halve(self, group):
            self.at += 1
            keep = settled(self.keep)
            cut, bit = keep.shape[0] // 2, self.steps[self.at]
            if cut % 16 == 0:
                kernel = functools.partial(halve_kernel, 2 + bits.index(bit))
                self.out, self.keep = group.add(kernel, [((cut, keep.shape[1]), bf16)] * 2, [keep, self.got])
            else:
                mine = ((position // bit) % 2) * cut
                take = functools.partial(lax.dynamic_slice_in_dim, slice_size=cut, axis=0)
                total = [(take(keep, at).astype(f32) + take(self.got, at).astype(f32)) for at in (cut - mine, mine)]
                self.out, self.keep = [values.astype(bf16) for values in total]

        def send(self):
            self.got = flip(self.out, self.steps[self.at], dp)

        def step(self, name):
            group = Group(name)
            self.halve(group)
            if group.stages:
                run(group)
            self.send()

        def total(self):
            while self.at < len(self.steps) - 1:
                self.step("halve")
            return settled(self.keep), self.got

    class Small:
        def __init__(self, values):
            self.values, self.at = values, -1
            self.send()

        def send(self):
            self.at += 1
            if self.at > len(bits):
                return
            self.got = flip(self.values, bits[self.at], dp) if self.at < len(bits) else swap(self.values)

        def halve(self, group):
            shape = self.values.shape
            (self.values,) = group.add(add_kernel, [(shape, f32)], [settled(self.values), self.got])

        def total(self):
            values = settled(self.values)
            while self.at <= len(bits):
                values = self.values = values + self.got
                self.send()
            return values

    def finish(name, sums, widths):
        left = sums[0].shape[0]
        shapes = [((left, w), f32) if n == 1 else ((n, left, w), f32) for n, w in widths]
        if left % 16 == 0:
            outs = single(name, finish_kernel, shapes, sums)
            return [*outs[:-1], outs[-1].T]
        total = jnp.concatenate([k.astype(f32) + g.astype(f32) for k, g in zip(sums[::2], sums[1::2], strict=True)], axis=1)
        outs, at = [], 0
        for n, w in widths:
            outs.append(total[:, at : at + n * w])
            at += n * w
        outs = [o if n == 1 else jnp.stack(jnp.split(o, n, axis=1)) for o, (n, w) in zip(outs, widths, strict=True)]
        return outs[:-1] + [outs[-1].T]

    recv = swap(own)
    memory_recv = swap(memory_own)
    cot_recv = swap(cot)

    count = length // block
    lane = np.arange(2 * block)
    spot = np.arange(count)[:, None] * block + np.where(lane < block, -lane, 2 * block - lane)[None]
    spot = np.clip(spot, 0, length - 1).reshape(-1).astype(np.int32)
    firsts = jnp.sum((rel_bucket[None, :] < jnp.arange(buckets + 1, dtype=jnp.int32)[:, None]).astype(jnp.int32), axis=1)
    hot = ((spot[None] >= firsts[:-1, None]) & (spot[None] < firsts[1:, None])).astype(f32)
    line = jnp.einsum("bh,bs->hs", rel_bias, hot.astype(bf16), preferred_element_type=f32)
    line = jnp.pad(line, ((0, 8 - heads), (0, 0)))
    (table,) = single("bias_table", bias_kernel, [((heads, block, length), bf16)], [line])
    seg_col = dec_segments.reshape(length, 1)

    def self_forward(group, chunk, extra):
        end = (chunk + 1) * rows
        return group.add(
            functools.partial(self_forward_kernel, chunk),
            [
                ((rows, width), bf16),
                ((end, 3 * inner), bf16),
                ((rows, inner), bf16),
                ((heads, rows, end), bf16),
                ((rows, width), bf16),
            ],
            [own, recv, norm_gains, self_query, self_keyval, self_output, seg_col, dec_segments, table] + extra,
            flops=2 * rows * width * inner * 4,
        )

    group = Group("self_forward_a")
    normed_one_a, qkv_a, ctx_one_a, prob_one_a, part_one_a = self_forward(group, 0, [])
    run(group)
    part_one_recv_a = swap(part_one_a)
    group = Group("self_forward_b")
    normed_one_b, qkv, ctx_one_b, prob_one_b, part_one_b = self_forward(group, 1, [qkv_a])
    run(group)
    part_one_recv_b = swap(part_one_b)

    memory_all, kv = single(
        "memory_keyval",
        memory_kernel,
        [((length, width), bf16), ((length, 2 * inner), bf16)],
        [memory_own, memory_recv, cross_keyval],
        flops=2 * length * width * inner * 2,
    )

    def cross_forward(group, chunk, part, part_recv):
        return group.add(
            functools.partial(cross_forward_kernel, chunk),
            [
                ((rows, width), f32),
                ((rows, width), bf16),
                ((rows, inner), bf16),
                ((rows, inner), bf16),
                ((heads, rows, length), bf16),
                ((rows, width), bf16),
            ],
            [own, recv, part, part_recv, norm_gains, cross_query, cross_output, kv, seg_col, mem_segments],
            flops=2 * rows * width * inner * 3,
        )

    group = Group("cross_forward_a")
    after_self_a, normed_two_a, query_two_a, ctx_two_a, prob_two_a, part_two_a = cross_forward(
        group, 0, part_one_a, part_one_recv_a
    )
    run(group)
    part_two_recv_a = swap(part_two_a)
    group = Group("cross_forward_b")
    after_self_b, normed_two_b, query_two_b, ctx_two_b, prob_two_b, part_two_b = cross_forward(
        group, 1, part_one_b, part_one_recv_b
    )
    run(group)
    part_two_recv_b = swap(part_two_b)

    def ffn(group, chunk, after_self, part, part_recv):
        return group.add(
            functools.partial(ffn_kernel, chunk),
            [
                ((rows, width), f32),
                ((rows, width), bf16),
                ((rows, units), bf16),
                ((rows, 2 * units), bf16),
                ((rows, width), bf16),
            ],
            [after_self, part, part_recv, cot, cot_recv, norm_gains, ffn_input, ffn_output],
            scratch=[pltpu.VMEM((rows, width), bf16)],
            flops=2 * rows * width * units * 5,
        )

    group = Group("ffn_a")
    after_cross_a, normed_three_a, hidden_a, gate_grads_a, back_three_a = ffn(
        group, 0, after_self_a, part_two_a, part_two_recv_a
    )
    run(group)
    back_three_recv_a = swap(back_three_a)
    group = Group("ffn_b")
    after_cross_b, normed_three_b, hidden_b, gate_grads_b, back_three_b = ffn(
        group, 1, after_self_b, part_two_b, part_two_recv_b
    )

    first_send, first_keep, second_send, second_keep = group.add(
        functools.partial(ffn_grads_kernel, [plan_a[1], plan_b[1]]),
        [((width // 2, 3 * units // 2), bf16)] * 4,
        [
            normed_three_a,
            normed_three_b,
            gate_grads_a,
            gate_grads_b,
            hidden_a,
            hidden_b,
            cot,
            cot_recv,
        ],
        scratch=[pltpu.VMEM((width, length), bf16)] * 3,
        flops=2 * length * width * units * 3,
    )
    run(group)
    back_three_recv_b = swap(back_three_b)
    ffn_first = Scatter(plan_a[0], first_send, first_keep)
    ffn_second = Scatter(plan_b[0], second_send, second_keep)

    def cross_back(group, chunk, after, back, back_recv, prob):
        return group.add(
            functools.partial(cross_back_kernel, chunk),
            [
                ((rows, width), f32),
                ((rows, width), bf16),
                ((rows, inner), bf16),
                ((rows, inner), bf16),
                ((heads, rows, length), bf16),
                ((rows, width), bf16),
                ((8, width), f32),
            ],
            [after, back, back_recv, cot, cot_recv, norm_gains, cross_output, cross_query, kv, prob],
            flops=2 * rows * width * inner * 4,
        )

    group = Group("cross_back_a")
    grad_cross_a, sent_two_a, dctx_two_a, dq_two_a, score_two_a, back_two_a, three_a = cross_back(
        group, 0, after_cross_a, back_three_a, back_three_recv_a, prob_two_a
    )
    run(group)
    back_two_recv_a = swap(back_two_a)
    group = Group("cross_back_b")
    ffn_first.halve(group)
    ffn_second.halve(group)
    grad_cross_b, sent_two_b, dctx_two_b, dq_two_b, score_two_b, back_two_b, three_b = cross_back(
        group, 1, after_cross_b, back_three_b, back_three_recv_b, prob_two_b
    )
    run(group)
    back_two_recv_b = swap(back_two_b)
    ffn_first.send()
    ffn_second.send()
    group = Group("self_back_a")
    cross_send, cross_keep, memory_send, memory_keep = group.add(
        functools.partial(cross_grads_kernel, plan_a[1]),
        [
            ((width // 2, 4 * inner), bf16),
            ((width // 2, 4 * inner), bf16),
            ((rows, width), bf16),
            ((rows, width), f32),
        ],
        [
            normed_two_a,
            normed_two_b,
            dq_two_a,
            dq_two_b,
            query_two_a,
            query_two_b,
            score_two_a,
            score_two_b,
            prob_two_a,
            prob_two_b,
            dctx_two_a,
            dctx_two_b,
            ctx_two_a,
            ctx_two_b,
            sent_two_a,
            sent_two_b,
            memory_all,
            cross_keyval,
        ],
        scratch=[pltpu.VMEM((width, length), bf16)] * 3 + [pltpu.VMEM((length, 2 * inner), bf16)],
        flops=2 * length * width * inner * 8,
    )

    def self_back(group, chunk, after, back, back_recv, grad_cross, prob):
        end = (chunk + 1) * rows
        return group.add(
            functools.partial(self_back_kernel, chunk),
            [
                ((rows, width), f32),
                ((rows, width), bf16),
                ((rows, inner), bf16),
                ((rows, inner), bf16),
                ((heads, rows, end), bf16),
                ((8, width), f32),
            ],
            [after, back, back_recv, grad_cross, norm_gains, self_output, qkv, prob],
            flops=2 * rows * width * inner * 3,
        )

    grad_self_a, sent_one_a, dctx_one_a, dq_one_a, score_one_a, two_a = self_back(
        group, 0, after_self_a, back_two_a, back_two_recv_a, grad_cross_a, prob_one_a
    )
    run(group)
    cross_sum = Scatter(plan_a[0], cross_send, cross_keep)
    memory_recv_grad = swap(memory_send)
    group = Group("self_back_b")
    ffn_first.halve(group)
    ffn_second.halve(group)
    grad_self_b, sent_one_b, dctx_one_b, dq_one_b, score_one_b, two_b = self_back(
        group, 1, after_self_b, back_two_b, back_two_recv_b, grad_cross_b, prob_one_b
    )

    self_send, self_keep, dqkv = group.add(
        functools.partial(self_grads_kernel, plan_a[1]),
        [((width // 2, 4 * inner), bf16), ((width // 2, 4 * inner), bf16), ((length, 3 * inner), bf16)],
        [
            normed_one_a,
            normed_one_b,
            dq_one_a,
            dq_one_b,
            qkv,
            score_one_a,
            score_one_b,
            prob_one_a,
            prob_one_b,
            dctx_one_a,
            dctx_one_b,
            ctx_one_a,
            ctx_one_b,
            sent_one_a,
            sent_one_b,
        ],
        scratch=[pltpu.VMEM((width, length), bf16)] * 2,
        flops=2 * length * width * inner * 6,
    )
    run(group)
    self_sum = Scatter(plan_a[0], self_send, self_keep)
    ffn_first.send()
    ffn_second.send()
    cross_sum.step("halve_zero")
    group = Group("self_input")
    back_one_send, back_one_keep, small_part = group.add(
        self_input_kernel,
        [((rows, width), bf16), ((rows, width), f32), ((16, width), f32)],
        [
            dqkv,
            own,
            recv,
            self_query,
            self_keyval,
            score_one_a,
            score_one_b,
            hot,
            two_a,
            two_b,
            three_a,
            three_b,
        ],
        scratch=[pltpu.VMEM((8, 2 * length), f32)],
    )
    (out_send,) = group.add(down_kernel, [((rows, width), bf16)], [hidden_a, hidden_b, ffn_output])
    run(group)
    small = Small(small_part)
    back_one_recv = swap(back_one_send)
    out_recv = swap(out_send)

    def together(name, *sums):
        group = Group(name)
        for item in sums:
            item.halve(group)
        run(group)
        for item in sums:
            item.send()

    together("halve_one", small, self_sum)
    together("halve_two", small, ffn_first, ffn_second)
    cross_sum.step("halve_cross")
    together("halve_three", small, self_sum)
    grads_ffn = finish("finish_ffn", [*ffn_first.total(), *ffn_second.total()], [(2, units), (1, units)])
    together("halve_four", small, cross_sum)
    (output,) = single(
        "final",
        final_kernel,
        [((rows, width), bf16)],
        [hidden_a, hidden_b, after_cross_a, after_cross_b, out_recv, ffn_output],
    )
    grad_memory = settled(memory_keep) + memory_recv_grad.astype(f32)
    together("halve_five", small, self_sum)
    widths = [(1, inner), (2, inner), (1, inner)]
    grads_cross = finish("finish_cross", cross_sum.total(), widths)
    (grad_input,) = single(
        "input_grad",
        input_grad_kernel,
        [((rows, width), f32)],
        [own, back_one_keep, back_one_recv, grad_self_a, grad_self_b, norm_gains],
    )
    grads_self = finish("finish_self", self_sum.total(), widths)
    small = small.total()
    return (
        output[None],
        grad_input[None],
        grad_memory[None],
        *grads_self,
        *grads_cross,
        *grads_ffn,
        small[0:3],
        jnp.concatenate([small[8 : 8 + heads, 0:buckets], small[8 : 8 + heads, 128 : 128 + buckets]]).T,
    )


def solution(mesh):
    in_specs = (
        P("dp", "mp", None),
        P("dp", "mp", None),
        P("dp", "mp", None),
        P(None, "mp"),
        P(None, None, "mp"),
        P("mp", None),
        P(None, "mp"),
        P(None, None, "mp"),
        P("mp", None),
        P(None, None, "mp"),
        P("mp", None),
        P(),
        P(None, "mp"),
        P("dp", None),
        P("dp", None),
        P(),
    )
    out_specs = (
        P("dp", "mp", None),
        P("dp", "mp", None),
        P("dp", "mp", None),
        P("dp", "mp"),
        P(None, "dp", "mp"),
        P("mp", "dp"),
        P("dp", "mp"),
        P(None, "dp", "mp"),
        P("mp", "dp"),
        P(None, "dp", "mp"),
        P("mp", "dp"),
        P(),
        P(),
    )
    return jax.shard_map(body, mesh=mesh, in_specs=in_specs, out_specs=out_specs, check_vma=False)
```

```python
import functools

import jax
import jax.numpy as jnp
import numpy as np
from jax import lax
from jax.experimental import pallas as pl
from jax.experimental.pallas import tpu as pltpu
from jax.sharding import PartitionSpec as P

epsilon = 1e-06
masked_score = -1e30
gelu_root = float(np.sqrt(2.0 / np.pi))
gelu_cubic = 0.044715
block = 128
head_size = 64
f32 = jnp.float32
bf16 = jnp.bfloat16


def dot(left, right):
    return lax.dot_general(left, right, (((1,), (0,)), ((), ())), preferred_element_type=f32)


def dot_rt(left, right):
    return lax.dot_general(left, right, (((1,), (1,)), ((), ())), preferred_element_type=f32)


def dot_lt(left, right):
    return lax.dot_general(left, right, (((0,), (0,)), ((), ())), preferred_element_type=f32)


def pick(flag, first, second):
    return jnp.where(flag, first, second)


def even_odd(values):
    lane = lax.broadcasted_iota(jnp.int32, values.shape, 1)
    zero = jnp.zeros_like(values)
    return jnp.where(lane < head_size, values, zero), jnp.where(lane < head_size, zero, values)


def rms_scale(values):
    return lax.rsqrt(jnp.mean(values * values, axis=-1, keepdims=True) + epsilon)


def norm_back(values, gain, grad):
    scale = rms_scale(values)
    scaled = grad * gain
    inner = jnp.mean(values * scaled, axis=-1, keepdims=True)
    back = scale * scaled - values * (scale * scale * scale * inner)
    return back, grad * values * scale


def softmax(scores):
    top = jnp.max(scores, axis=-1, keepdims=True)
    weights = jnp.exp(scores - top)
    total = jnp.sum(weights, axis=-1, keepdims=True)
    return (weights * (1.0 / total)).astype(bf16)


times = {"ffn_b": 10.0, "cross_back_a": 60.0, "cross_back_b": 60.0, "self_back_b": 2.5, "halve_ffn_two": 6.0, "halve_cross_two": 10.0}


class Made:
    def __init__(self, shape, dtype):
        self.shape, self.dtype, self.value = shape, dtype, None


def settled(arg):
    return arg.value if isinstance(arg, Made) and arg.value is not None else arg


class Group:
    def __init__(self, name, cost=0):
        self.name, self.cost, self.stages, self.inputs = name, cost, [], []

    def add(self, kernel, outs, args, scratch=(), flops=0):
        made = [Made(shape, dtype) for shape, dtype in outs]
        args = [settled(arg) for arg in args]
        self.stages.append((kernel, list(args), made, list(scratch)))
        self.cost += flops
        for arg in args:
            if not isinstance(arg, Made) and not any(arg is known for known in self.inputs):
                self.inputs.append(arg)
        return made

    def call(self, idx):
        made = [out for stage in self.stages for out in stage[2]]
        scratch = [item for stage in self.stages for item in stage[3]]

        def kernel(idx_ref, *refs):
            ins, refs = refs[: len(self.inputs)], refs[len(self.inputs) :]
            outs, spare = refs[: len(made)], list(refs[len(made) :])
            known = [(value, ref) for value, ref in zip(self.inputs + made, ins + outs, strict=True)]
            for body, args, stage_outs, stage_scratch in self.stages:
                taken = [next(ref for value, ref in known if value is item) for item in args + stage_outs]
                body(idx_ref, *taken, *[spare.pop(0) for _ in stage_scratch])

        out_shape = [jax.ShapeDtypeStruct(out.shape, out.dtype) for out in made]
        moved = sum(x.size * x.dtype.itemsize for x in self.inputs + out_shape)
        values = pl.pallas_call(
            kernel,
            name=self.name,
            out_shape=out_shape,
            in_specs=[pl.BlockSpec(memory_space=pltpu.SMEM)]
            + [pl.BlockSpec(memory_space=pltpu.VMEM)] * len(self.inputs),
            out_specs=[pl.BlockSpec(memory_space=pltpu.VMEM)] * len(made),
            scratch_shapes=scratch,
            compiler_params=pltpu.CompilerParams(vmem_limit_bytes=8 << 20),
            cost_estimate=pl.CostEstimate(flops=int(times.get(self.name, 0.01) * 1.15e9), transcendentals=0, bytes_accessed=1024),
        )(idx, *self.inputs)
        for out, value in zip(made, values, strict=True):
            out.value = value
        return values


def bias_kernel(idx_ref, line_ref, table_ref):
    heads = table_ref.shape[0]
    count = table_ref.shape[2] // block
    for head in range(heads):
        for step in range(count):
            line = line_ref[head : head + 1, step * 2 * block : (step + 1) * 2 * block]
            wide = jnp.broadcast_to(line, (block, 2 * block))
            turned = pltpu.roll(wide, 0, 1, stride=1, stride_axis=0)
            at = (count - 1 - step) * block
            table_ref[head, :, at : at + block] = turned[:, :block].astype(bf16)


def self_project_kernel(idx_ref, values_ref, gain_ref, wq_ref, wkv_ref, normed_ref, qkv_ref):
    inner = wq_ref.shape[1]
    gain = gain_ref[0:1, :].astype(f32)
    for at in range(0, values_ref.shape[0], block):
        values = values_ref[at : at + block, :].astype(f32)
        normed_ref[at : at + block, :] = (values * rms_scale(values) * gain).astype(bf16)
    qkv_ref[:, 0:inner] = dot(normed_ref[...], wq_ref[...]).astype(bf16)
    qkv_ref[:, inner : 2 * inner] = dot(normed_ref[...], wkv_ref[0]).astype(bf16)
    qkv_ref[:, 2 * inner :] = dot(normed_ref[...], wkv_ref[1]).astype(bf16)


def self_order_kernel(idx_ref, normed_own, qkv_own, normed_recv, qkv_recv, normed_a, normed_b, qkv_ref):
    mine = idx_ref[0] == 0
    rows = normed_own.shape[0]
    normed_a[...] = pick(mine, normed_own[...], normed_recv[...])
    normed_b[...] = pick(mine, normed_recv[...], normed_own[...])
    qkv_ref[0:rows, :] = pick(mine, qkv_own[...], qkv_recv[...])
    qkv_ref[rows:, :] = pick(mine, qkv_recv[...], qkv_own[...])


def self_attend_kernel(chunk, idx_ref, qkv_ref, segc_ref, segr_ref, table_ref, ctx_ref, prob_ref):
    rows, inner = ctx_ref.shape
    base = chunk * rows
    total = table_ref.shape[2]
    masks = []
    for at in range(0, rows, block):
        keys = base + at + block
        allowed = segc_ref[base + at : keys, :] == segr_ref[:, 0:keys]
        row = lax.broadcasted_iota(jnp.int32, (block, keys), 0) + (base + at)
        col = lax.broadcasted_iota(jnp.int32, (block, keys), 1)
        masks.append(jnp.where(allowed & (row >= col), 0.0, masked_score))
    for pair in range(0, inner, 2 * head_size):
        keys2 = qkv_ref[0 : base + rows, inner + pair : inner + pair + 128]
        values_e, values_o = even_odd(qkv_ref[0 : base + rows, 2 * inner + pair : 2 * inner + pair + 128])
        for number, at in enumerate(range(0, rows, block)):
            keys = base + at + block
            query_e, query_o = even_odd(qkv_ref[base + at : keys, pair : pair + 128])
            context = jnp.zeros((block, 128), f32)
            for head, query, values in (
                (pair // head_size, query_e, values_e),
                (pair // head_size + 1, query_o, values_o),
            ):
                scores = dot_rt(query, keys2[0:keys]) + table_ref[head, :, total - keys :].astype(f32)
                probs = softmax(scores + masks[number])
                prob_ref[head, at : at + block, 0:keys] = probs
                context = context + dot(probs, values[0:keys])
            ctx_ref[at : at + block, pair : pair + 128] = context.astype(bf16)


def weights_kernel(quarter_at, idx_ref, own_ref, beside_ref, own_core, beside_core, *outs):
    rows = outs[0].shape[0] // 4
    low, high = idx_ref[quarter_at], idx_ref[quarter_at + 1]
    for number, out_ref in enumerate(outs):
        part = slice(number * rows, (number + 1) * rows)
        for ref, at in (
            (own_ref, 2 * high + low),
            (beside_ref, 2 * (1 - high) + low),
            (own_core, 2 * high + (1 - low)),
            (beside_core, 2 * (1 - high) + (1 - low)),
        ):
            out_ref[pl.ds(pl.multiple_of(at * rows, 16), rows), :] = ref[part, :]


def memory_kernel(idx_ref, own_ref, recv_ref, wkv_ref, memory_ref, kv_ref):
    rows = own_ref.shape[0]
    inner = wkv_ref.shape[2]
    mine = idx_ref[0]
    memory_ref[pl.ds(pl.multiple_of(mine * rows, rows), rows), :] = own_ref[...]
    memory_ref[pl.ds(pl.multiple_of((1 - mine) * rows, rows), rows), :] = recv_ref[...]
    kv_ref[:, 0:inner] = dot(memory_ref[...], wkv_ref[0]).astype(bf16)
    kv_ref[:, inner : 2 * inner] = dot(memory_ref[...], wkv_ref[1]).astype(bf16)


def cross_forward_kernel(
    chunk,
    idx_ref,
    own_ref,
    recv_ref,
    before_ref,
    before_recv_ref,
    gain_ref,
    wo_ref,
    wo_pair_ref,
    wq_ref,
    kv_ref,
    segc_ref,
    segm_ref,
    after_ref,
    normed_ref,
    query_ref,
    ctx_ref,
    prob_ref,
):
    mine = idx_ref[0] == chunk
    rows = own_ref.shape[0]
    inner = wq_ref.shape[1]
    gain = gain_ref[1:2, :].astype(f32)
    after_ref[...] = dot(before_ref[...], wo_ref[...]) + dot(before_recv_ref[...], wo_pair_ref[...])
    for at in range(0, rows, block):
        part = slice(at, at + block)
        values = pick(mine, own_ref[part, :], recv_ref[part, :]).astype(f32) + after_ref[part, :]
        after_ref[part, :] = values
        normed_ref[part, :] = (values * rms_scale(values) * gain).astype(bf16)
    query_ref[...] = dot(normed_ref[...], wq_ref[...]).astype(bf16)
    masks = []
    for at in range(0, rows, block):
        allowed = segc_ref[chunk * rows + at : chunk * rows + at + block, :] == segm_ref[...]
        masks.append(jnp.where(allowed, 0.0, masked_score))
    for pair in range(0, inner, 2 * head_size):
        keys2 = kv_ref[:, pair : pair + 128]
        values_e, values_o = even_odd(kv_ref[:, inner + pair : inner + pair + 128])
        for number, at in enumerate(range(0, rows, block)):
            query_e, query_o = even_odd(query_ref[at : at + block, pair : pair + 128])
            context = jnp.zeros((block, 128), f32)
            for head, query, values in (
                (pair // head_size, query_e, values_e),
                (pair // head_size + 1, query_o, values_o),
            ):
                probs = softmax(dot_rt(query, keys2) + masks[number])
                prob_ref[head, at : at + block, :] = probs
                context = context + dot(probs, values)
            ctx_ref[at : at + block, pair : pair + 128] = context.astype(bf16)


def ffn_kernel(
    chunk,
    idx_ref,
    after_self_ref,
    before_ref,
    before_recv_ref,
    cot_ref,
    cot_recv_ref,
    gain_ref,
    wo_ref,
    wo_pair_ref,
    win_ref,
    wout_ref,
    after_ref,
    normed_ref,
    hidden_ref,
    grads_ref,
    back_ref,
    cot_scr,
):
    mine = idx_ref[0] == chunk
    rows = after_self_ref.shape[0]
    units = win_ref.shape[2]
    gain = gain_ref[2:3, :].astype(f32)
    after_ref[...] = dot(before_ref[...], wo_ref[...]) + dot(before_recv_ref[...], wo_pair_ref[...])
    for at in range(0, rows, block):
        part = slice(at, at + block)
        values = after_self_ref[part, :] + after_ref[part, :]
        after_ref[part, :] = values
        normed_ref[part, :] = (values * rms_scale(values) * gain).astype(bf16)
        cot_scr[part, :] = pick(mine, cot_ref[part, :], cot_recv_ref[part, :])
    wide = 256
    for at in range(0, units, wide):
        cols = slice(at, at + wide)
        gate = dot(normed_ref[...], win_ref[0, :, cols])
        upward = dot(normed_ref[...], win_ref[1, :, cols])
        grad = dot_rt(cot_scr[...], wout_ref[cols, :])
        square = gate * gate
        bend = jnp.tanh(gelu_root * gate * (1.0 + gelu_cubic * square))
        half = 0.5 * (1.0 + bend)
        gelu = gate * half
        slope = half + 0.5 * gelu_root * gate * (1.0 - bend * bend) * (1.0 + 3.0 * gelu_cubic * square)
        hidden_ref[:, cols] = (gelu * upward).astype(bf16)
        grads_ref[:, cols] = (grad * upward * slope).astype(bf16)
        grads_ref[:, units + at : units + at + wide] = (grad * gelu).astype(bf16)
    back_ref[...] = (
        dot_rt(grads_ref[:, 0:units], win_ref[0]) + dot_rt(grads_ref[:, units:], win_ref[1])
    ).astype(bf16)


def down_kernel(idx_ref, first_ref, second_ref, wout_ref, out_ref):
    out_ref[...] = dot(pick(idx_ref[0] == 0, second_ref[...], first_ref[...]), wout_ref[...]).astype(bf16)


def final_kernel(idx_ref, hid_a, hid_b, after_a, after_b, recv_ref, wout_ref, out_ref):
    mine = idx_ref[0] == 0
    own = dot(pick(mine, hid_a[...], hid_b[...]), wout_ref[...])
    out_ref[...] = (pick(mine, after_a[...], after_b[...]) + (own + recv_ref[...].astype(f32))).astype(bf16)


def turn_rows(values, place_ref, order, at):
    turned = jnp.transpose(values)
    size = turned.shape[0] // len(order)
    for number, position in enumerate(order):
        place_ref[position * size : (position + 1) * size, at : at + values.shape[0]] = turned[
            number * size : (number + 1) * size
        ]


def write_grads(bit_ref, turned_ref, right, send_ref, keep_ref, at):
    rows = send_ref.shape[0]
    mine = bit_ref[1]
    cols = slice(at, at + right.shape[1])
    keep_ref[:, cols] = dot(turned_ref[pl.ds(pl.multiple_of(mine * rows, rows), rows), :], right).astype(bf16)
    send_ref[:, cols] = dot(turned_ref[pl.ds(pl.multiple_of((1 - mine) * rows, rows), rows), :], right).astype(bf16)


def ffn_grads_kernel(
    order,
    idx_ref,
    normed_a,
    normed_b,
    grads_a,
    grads_b,
    hidden_a,
    hidden_b,
    cot_ref,
    cot_recv_ref,
    send_ref,
    keep_ref,
    turned,
    turned_two,
):
    rows = normed_a.shape[0]
    mine = idx_ref[0] == 0
    units = hidden_a.shape[1]
    turn_rows(normed_a[...], turned, order, 0)
    turn_rows(normed_b[...], turned, order, rows)
    both = jnp.concatenate([grads_a[...], grads_b[...]], axis=0)
    write_grads(idx_ref, turned, both, send_ref, keep_ref, 0)
    turn_rows(pick(mine, cot_ref[...], cot_recv_ref[...]), turned_two, order, 0)
    turn_rows(pick(mine, cot_recv_ref[...], cot_ref[...]), turned_two, order, rows)
    hidden = jnp.concatenate([hidden_a[...], hidden_b[...]], axis=0)
    write_grads(idx_ref, turned_two, hidden, send_ref, keep_ref, 2 * units)


def attend_back(query_rows, prob_ref, score_ref, grad_ref, key_of, value_of, dq_ref, inner, reach):
    for pair in range(0, inner, 2 * head_size):
        keys_e, keys_o = even_odd(key_of(pair))
        values2 = value_of(pair)
        for at in range(0, query_rows, block):
            keys = reach(at)
            grad_e, grad_o = even_odd(grad_ref[at : at + block, pair : pair + 128])
            total = jnp.zeros((block, 128), f32)
            for head, grad, key in (
                (pair // head_size, grad_e, keys_e),
                (pair // head_size + 1, grad_o, keys_o),
            ):
                probs = prob_ref[head, at : at + block, 0:keys].astype(f32)
                grad_probs = dot_rt(grad, values2[0:keys])
                delta = jnp.sum(probs * grad_probs, axis=-1, keepdims=True) / jnp.sum(
                    probs, axis=-1, keepdims=True
                )
                scores = (probs * (grad_probs - delta)).astype(bf16)
                score_ref[head, at : at + block, 0:keys] = scores
                total = total + dot(scores, key[0:keys])
            dq_ref[at : at + block, pair : pair + 128] = total.astype(bf16)


def cross_back_kernel(
    chunk,
    idx_ref,
    after_ref,
    back_ref,
    back_recv_ref,
    cot_ref,
    cot_recv_ref,
    gain_ref,
    wo_ref,
    wq_ref,
    kv_ref,
    prob_ref,
    grad_ref,
    sent_ref,
    dctx_ref,
    dq_ref,
    score_ref,
    out_ref,
    gain_out_ref,
):
    mine = idx_ref[0] == chunk
    rows = after_ref.shape[0]
    inner = wq_ref.shape[1]
    gain = gain_ref[2:3, :].astype(f32)
    gain_total = jnp.zeros((8, gain.shape[1]), f32)
    for at in range(0, rows, block):
        part = slice(at, at + block)
        incoming = back_ref[part, :].astype(f32) + back_recv_ref[part, :].astype(f32)
        back, gain_terms = norm_back(after_ref[part, :], gain, incoming)
        total = pick(mine, cot_ref[part, :], cot_recv_ref[part, :]).astype(f32) + back
        grad_ref[part, :] = total
        sent_ref[part, :] = total.astype(bf16)
        gain_total = gain_total + jnp.sum(gain_terms.reshape(block // 8, 8, -1), axis=0)
    gain_out_ref[...] = pick(mine, gain_total, jnp.zeros_like(gain_total))
    dctx_ref[...] = dot_rt(sent_ref[...], wo_ref[...]).astype(bf16)
    attend_back(
        rows,
        prob_ref,
        score_ref,
        dctx_ref,
        lambda pair: kv_ref[:, pair : pair + 128],
        lambda pair: kv_ref[:, inner + pair : inner + pair + 128],
        dq_ref,
        inner,
        lambda at: kv_ref.shape[0],
    )
    out_ref[...] = dot_rt(dq_ref[...], wq_ref[...]).astype(bf16)


def cross_grads_kernel(
    order,
    idx_ref,
    normed_a,
    normed_b,
    dq_a,
    dq_b,
    query_a,
    query_b,
    score_a,
    score_b,
    prob_a,
    prob_b,
    dctx_a,
    dctx_b,
    ctx_a,
    ctx_b,
    sent_a,
    sent_b,
    memory_ref,
    wkv_ref,
    send_ref,
    keep_ref,
    memory_send_ref,
    memory_keep_ref,
    turned,
    turned_two,
    turned_three,
    dkv,
):
    rows = normed_a.shape[0]
    inner = dq_a.shape[1]
    for pair in range(0, inner, 2 * head_size):
        keys = jnp.zeros((dkv.shape[0], 128), f32)
        values = jnp.zeros((dkv.shape[0], 128), f32)
        for score, prob, query, dctx in ((score_a, prob_a, query_a, dctx_a), (score_b, prob_b, query_b, dctx_b)):
            cols = slice(pair, pair + 128)
            for number, (query_half, grad_half) in enumerate(
                zip(even_odd(query[:, cols]), even_odd(dctx[:, cols]), strict=True)
            ):
                head = pair // head_size + number
                keys = keys + dot_lt(score[head], query_half)
                values = values + dot_lt(prob[head], grad_half)
        dkv[:, pair : pair + 128] = keys.astype(bf16)
        dkv[:, inner + pair : inner + pair + 128] = values.astype(bf16)
    mine = idx_ref[0]
    other = pl.ds(pl.multiple_of((1 - mine) * rows, rows), rows)
    own = pl.ds(pl.multiple_of(mine * rows, rows), rows)
    memory_send_ref[...] = (
        dot_rt(dkv[other, 0:inner], wkv_ref[0]) + dot_rt(dkv[other, inner:], wkv_ref[1])
    ).astype(bf16)
    memory_keep_ref[...] = dot_rt(dkv[own, 0:inner], wkv_ref[0]) + dot_rt(dkv[own, inner:], wkv_ref[1])
    turn_rows(normed_a[...], turned, order, 0)
    turn_rows(normed_b[...], turned, order, rows)
    both = jnp.concatenate([dq_a[...], dq_b[...]], axis=0)
    write_grads(idx_ref, turned, both, send_ref, keep_ref, 0)
    turn_rows(memory_ref[...], turned_two, order, 0)
    write_grads(idx_ref, turned_two, dkv[...], send_ref, keep_ref, inner)
    turn_rows(sent_a[...], turned_three, order, 0)
    turn_rows(sent_b[...], turned_three, order, rows)
    both = jnp.concatenate([ctx_a[...], ctx_b[...]], axis=0)
    write_grads(idx_ref, turned_three, both, send_ref, keep_ref, 3 * inner)


def self_back_kernel(
    chunk,
    idx_ref,
    after_ref,
    back_ref,
    back_recv_ref,
    cross_ref,
    gain_ref,
    wo_ref,
    qkv_ref,
    prob_ref,
    grad_ref,
    sent_ref,
    dctx_ref,
    dq_ref,
    score_ref,
    gain_out_ref,
):
    mine = idx_ref[0] == chunk
    rows = after_ref.shape[0]
    inner = wo_ref.shape[0]
    gain = gain_ref[1:2, :].astype(f32)
    gain_total = jnp.zeros((8, gain.shape[1]), f32)
    for at in range(0, rows, block):
        part = slice(at, at + block)
        incoming = back_ref[part, :].astype(f32) + back_recv_ref[part, :].astype(f32)
        back, gain_terms = norm_back(after_ref[part, :], gain, incoming)
        total = cross_ref[part, :] + back
        grad_ref[part, :] = total
        sent_ref[part, :] = total.astype(bf16)
        gain_total = gain_total + jnp.sum(gain_terms.reshape(block // 8, 8, -1), axis=0)
    gain_out_ref[...] = pick(mine, gain_total, jnp.zeros_like(gain_total))
    dctx_ref[...] = dot_rt(sent_ref[...], wo_ref[...]).astype(bf16)
    end = (chunk + 1) * rows
    attend_back(
        rows,
        prob_ref,
        score_ref,
        dctx_ref,
        lambda pair: qkv_ref[0:end, inner + pair : inner + pair + 128],
        lambda pair: qkv_ref[0:end, 2 * inner + pair : 2 * inner + pair + 128],
        dq_ref,
        inner,
        lambda at: chunk * rows + at + block,
    )


def self_grads_kernel(
    order,
    idx_ref,
    normed_a,
    normed_b,
    dq_a,
    dq_b,
    qkv_ref,
    score_a,
    score_b,
    prob_a,
    prob_b,
    dctx_a,
    dctx_b,
    ctx_a,
    ctx_b,
    sent_a,
    sent_b,
    send_ref,
    keep_ref,
    dqkv_ref,
    turned,
    turned_two,
):
    rows = normed_a.shape[0]
    inner = dq_a.shape[1]
    for pair in range(0, inner, 2 * head_size):
        for at in range(0, 2 * rows, block):
            keys = jnp.zeros((block, 128), f32)
            values = jnp.zeros((block, 128), f32)
            cols = slice(pair, pair + 128)
            span = slice(at, at + block)
            for base, score, prob, dctx in ((0, score_a, prob_a, dctx_a), (rows, score_b, prob_b, dctx_b)):
                if at >= base + rows:
                    continue
                low = max(at - base, 0)
                for number, (query_half, grad_half) in enumerate(
                    zip(even_odd(qkv_ref[base + low : base + rows, cols]), even_odd(dctx[low:rows, cols]), strict=True)
                ):
                    head = pair // head_size + number
                    keys = keys + dot_lt(score[head, low:rows, span], query_half)
                    values = values + dot_lt(prob[head, low:rows, span], grad_half)
            dqkv_ref[span, inner + pair : inner + pair + 128] = keys.astype(bf16)
            dqkv_ref[span, 2 * inner + pair : 2 * inner + pair + 128] = values.astype(bf16)
    dqkv_ref[0:rows, 0:inner] = dq_a[...]
    dqkv_ref[rows : 2 * rows, 0:inner] = dq_b[...]
    turn_rows(normed_a[...], turned, order, 0)
    turn_rows(normed_b[...], turned, order, rows)
    write_grads(idx_ref, turned, dqkv_ref[...], send_ref, keep_ref, 0)
    turn_rows(sent_a[...], turned_two, order, 0)
    turn_rows(sent_b[...], turned_two, order, rows)
    both = jnp.concatenate([ctx_a[...], ctx_b[...]], axis=0)
    write_grads(idx_ref, turned_two, both, send_ref, keep_ref, 3 * inner)


def diagonals(values):
    wide = jnp.concatenate([values, jnp.zeros_like(values)], axis=1)
    total = wide[0:8]
    for at in range(8, block, 8):
        total = total + pltpu.roll(wide[at : at + 8], 2 * block - at, 1)
    row = lax.broadcasted_iota(jnp.int32, total.shape, 0)
    for bit in (1, 2, 4):
        total = jnp.where((row & bit) != 0, pltpu.roll(total, 2 * block - bit, 1), total)
    return jnp.sum(total, axis=0, keepdims=True)


def self_input_kernel(
    idx_ref,
    dqkv_ref,
    own_ref,
    recv_ref,
    wq_ref,
    wkv_ref,
    score_a,
    score_b,
    hot_ref,
    two_a,
    two_b,
    three_a,
    three_b,
    send_ref,
    keep_ref,
    small_ref,
    line,
):
    rows = own_ref.shape[0]
    inner = wq_ref.shape[1]
    mine = idx_ref[0]
    gain_total = jnp.zeros((8, own_ref.shape[1]), f32)
    for which, values_ref in ((1 - mine, recv_ref), (mine, own_ref)):
        span = pl.ds(pl.multiple_of(which * rows, rows), rows)
        grad = (
            dot_rt(dqkv_ref[span, 0:inner], wq_ref[...])
            + dot_rt(dqkv_ref[span, inner : 2 * inner], wkv_ref[0])
            + dot_rt(dqkv_ref[span, 2 * inner :], wkv_ref[1])
        )
        if values_ref is recv_ref:
            send_ref[0:rows, :] = grad.astype(bf16)
        else:
            keep_ref[...] = grad
        values = values_ref[...].astype(f32)
        terms = grad * values * rms_scale(values)
        gain_total = gain_total + jnp.sum(terms.reshape(rows // 8, 8, -1), axis=0)
    heads = score_a.shape[0]
    count = 2 * rows // block
    line[...] = jnp.zeros_like(line)
    for head in range(heads):
        for step in range(count):
            total = jnp.zeros((block, block), f32)
            for at in range(step, count):
                col = (at - step) * block
                score = score_a if at * block < rows else score_b
                row = at * block % rows
                total = total + score[head, row : row + block, col : col + block].astype(f32)
            line[head : head + 1, step * 2 * block : (step + 1) * 2 * block] = diagonals(total)
    bias = lax.dot_general(
        line[...], hot_ref[...], (((1,), (1,)), ((), ())), precision=lax.Precision.HIGHEST, preferred_element_type=f32
    )
    buckets = hot_ref.shape[0]
    small_ref[...] = jnp.zeros_like(small_ref)
    small_ref[0:1, :] = jnp.sum(gain_total, axis=0, keepdims=True)
    small_ref[1:2, :] = jnp.sum(two_a[...] + two_b[...], axis=0, keepdims=True)
    small_ref[2:3, :] = jnp.sum(three_a[...] + three_b[...], axis=0, keepdims=True)
    small_ref[8:16, 0:buckets] = pick(mine == 0, bias, jnp.zeros_like(bias))
    small_ref[8:16, 128 : 128 + buckets] = pick(mine == 1, bias, jnp.zeros_like(bias))
    high = small_ref[...].astype(bf16)
    send_ref[rows : rows + 16, :] = high
    send_ref[rows + 16 :, :] = (small_ref[...] - high.astype(f32)).astype(bf16)


def input_grad_kernel(idx_ref, own_ref, keep_ref, recv_ref, grad_a, grad_b, gain_ref, out_ref):
    mine = idx_ref[0] == 0
    gain = gain_ref[0:1, :].astype(f32)
    for at in range(0, own_ref.shape[0], block):
        part = slice(at, at + block)
        incoming = keep_ref[part, :] + recv_ref[part, :].astype(f32)
        back, _ = norm_back(own_ref[part, :].astype(f32), gain, incoming)
        out_ref[part, :] = pick(mine, grad_a[part, :], grad_b[part, :]) + back


def halve_kernel(slot, idx_ref, keep_ref, got_ref, send_out, keep_out):
    rows = send_out.shape[0]
    mine = idx_ref[slot]
    other = pl.ds(pl.multiple_of((1 - mine) * rows, 16), rows)
    own = pl.ds(pl.multiple_of(mine * rows, 16), rows)
    send_out[...] = (keep_ref[other, :].astype(f32) + got_ref[other, :].astype(f32)).astype(bf16)
    keep_out[...] = (keep_ref[own, :].astype(f32) + got_ref[own, :].astype(f32)).astype(bf16)


def split_small(values):
    high = values.astype(bf16)
    return jnp.concatenate([high, (values - high.astype(f32)).astype(bf16)], axis=1)


def join_small(parts):
    width = parts.shape[1] // 2
    return parts[:, :width].astype(f32) + parts[:, width:].astype(f32)


def add_kernel(idx_ref, first_ref, second_ref, out_ref):
    out_ref[...] = split_small(join_small(first_ref[...]) + join_small(second_ref[...]))


def add_first_kernel(idx_ref, own_ref, got_ref, out_ref):
    rows = own_ref.shape[0]
    at = got_ref.shape[0] - 2 * rows
    got = got_ref[at : at + rows, :].astype(f32) + got_ref[at + rows :, :].astype(f32)
    out_ref[...] = split_small(join_small(split_small(own_ref[...])) + got)


def halve_small_kernel(slot, has_small, idx_ref, keep_ref, got_ref, *refs):
    send_out, keep_out = refs[-2:]
    count = 16
    rows = send_out.shape[0] - count
    mine = idx_ref[slot]
    other = pl.ds(pl.multiple_of((1 - mine) * rows, 16), rows)
    own = pl.ds(pl.multiple_of(mine * rows, 16), rows)
    send_out[0:rows, :] = (keep_ref[other, :].astype(f32) + got_ref[other, :].astype(f32)).astype(bf16)
    keep_out[0:rows, :] = (keep_ref[own, :].astype(f32) + got_ref[own, :].astype(f32)).astype(bf16)
    if has_small:
        small = split_small(join_small(keep_ref[2 * rows :, :]) + join_small(got_ref[2 * rows :, :]))
    else:
        small = split_small(join_small(refs[0][...]) + join_small(refs[1][...]))
    send_out[rows:, :] = small
    keep_out[rows:, :] = small


def finish_small_kernel(idx_ref, keep_ref, got_ref, out_ref):
    rows = keep_ref.shape[0] - 16
    out_ref[...] = split_small(join_small(keep_ref[rows:, :]) + join_small(got_ref[rows:, :]))


def last_small_kernel(idx_ref, *refs):
    *parts, gain_out, bias_out = refs
    at = parts[0].shape[0] - 16
    total = join_small(parts[0][at:, :])
    for part in parts[1:]:
        total = total + join_small(part[at:, :])
    heads, buckets = bias_out.shape[0] // 2, bias_out.shape[1]
    gain_out[...] = total[0:3, :]
    bias_out[0:heads, :] = total[8 : 8 + heads, 0:buckets]
    bias_out[heads:, :] = total[8 : 8 + heads, 128 : 128 + buckets]


def memory_add_kernel(idx_ref, keep_ref, got_ref, out_ref):
    out_ref[...] = keep_ref[...] + got_ref[...].astype(f32)


def finish_kernel(idx_ref, *refs):
    count = next(at for at, ref in enumerate(refs) if ref.dtype == f32)
    left = refs[-1].shape[0]
    starts = [0]
    for keep_ref in refs[0:count:2]:
        starts.append(starts[-1] + keep_ref.shape[1])

    def pieces(low, high):
        for number, start in enumerate(starts[:-1]):
            at, end = max(low, start), min(high, starts[number + 1])
            if at < end:
                cols = slice(at - start, end - start)
                keep = refs[2 * number][0:left, cols].astype(f32)
                yield at - low, end - low, keep + refs[2 * number + 1][0:left, cols].astype(f32)

    at = 0
    for out in refs[count:]:
        for values in [out] if len(out.shape) == 2 else [out.at[n] for n in range(out.shape[0])]:
            for low, high, total in pieces(at, at + values.shape[1]):
                values[:, low:high] = total
            at += values.shape[1]


def flip(values, bit, size):
    return lax.ppermute(settled(values), "dp", [(at, at ^ bit) for at in range(size)])


def swap(values):
    return lax.ppermute(settled(values), "mp", [(0, 1), (1, 0)])


def halving_plan(size, width):
    bits = [1 << at for at in range(size.bit_length() - 1)]
    if (width // size) % 16:
        return bits[::-1], [0]
    return bits, [sum(((at // bit) % 2) * (size // (2 * bit)) for bit in bits) for at in range(size)]


def body(
    hidden_in,
    memory,
    cotangent,
    self_query,
    self_keyval,
    self_output,
    cross_query,
    cross_keyval,
    cross_output,
    ffn_input,
    ffn_output,
    norm_gains,
    rel_bias,
    dec_segments,
    mem_segments,
    rel_bucket,
):
    dp = lax.axis_size("dp")
    position = lax.axis_index("dp")
    half = lax.axis_index("mp")
    own = hidden_in[0]
    rows, width = own.shape
    length = 2 * rows
    buckets, heads = rel_bias.shape
    inner = self_query.shape[1]
    units = ffn_output.shape[0]
    memory_own = memory[0]
    cot = cotangent[0]
    steps, order = halving_plan(dp, width)
    quarter = [position % 2, (position // 2) % 2]
    idx = jnp.stack([half] + [(position // bit) % 2 for bit in steps] + quarter).astype(jnp.int32)
    order_token = [idx]

    def run(group):
        if not group.stages:
            return []
        values = group.call(order_token[0])
        order_token[0] = lax.optimization_barrier((idx, values[-1]))[0]
        return values

    def single(name, kernel, outs, args, **options):
        group = Group(name)
        group.add(kernel, outs, args, **options)
        return run(group)

    class Scatter:
        def __init__(self, send, keep):
            self.keep, self.at, self.extra = keep, 0, 0
            self.got = flip(send, steps[0], dp)

        def halve(self, group, *small):
            self.at += 1
            keep = settled(self.keep)
            cut, bit = (keep.shape[0] - self.extra) // 2, steps[self.at]
            if small or self.extra:
                kernel = functools.partial(halve_small_kernel, 1 + self.at, self.extra > 0)
                self.extra = 16
                shape = ((cut + 16, keep.shape[1]), bf16)
                self.out, self.keep = group.add(kernel, [shape] * 2, [keep, self.got, *small])
            elif cut % 16 == 0:
                kernel = functools.partial(halve_kernel, 1 + self.at)
                self.out, self.keep = group.add(kernel, [((cut, keep.shape[1]), bf16)] * 2, [keep, self.got])
            else:
                mine = ((position // bit) % 2) * cut
                take = functools.partial(lax.dynamic_slice_in_dim, slice_size=cut, axis=0)
                total = [(take(keep, at).astype(f32) + take(self.got, at).astype(f32)) for at in (cut - mine, mine)]
                self.out, self.keep = [values.astype(bf16) for values in total]

        def send(self):
            self.got = flip(self.out, steps[self.at], dp)

        def step(self, name, *small):
            group = Group(name)
            self.halve(group, *small)
            run(group)
            self.send()

        def total(self):
            while self.at < len(steps) - 1:
                self.step("halve")
            return settled(self.keep), self.got

    def finish(group, sums, widths):
        left = width // dp
        shapes = [((left, w), f32) if n == 1 else ((n, left, w), f32) for n, w in widths]
        if left % 16 == 0:
            return group.add(finish_kernel, shapes, sums)
        total = jnp.concatenate([k.astype(f32) + g.astype(f32) for k, g in zip(sums[::2], sums[1::2], strict=True)], axis=1)
        outs, at = [], 0
        for n, w in widths:
            outs.append(total[:, at : at + n * w])
            at += n * w
        return [o if n == 1 else jnp.stack(jnp.split(o, n, axis=1)) for o, (n, w) in zip(outs, widths, strict=True)]

    recv = swap(own)
    piece = inner // 4
    spot = (position % 4) * piece
    cut = functools.partial(lax.dynamic_slice_in_dim, start_index=spot, slice_size=piece, axis=0)
    weight_own = swap(jnp.concatenate([cut(self_output), cut(cross_output)]))

    def after(values, made):
        return lax.optimization_barrier((values, settled(made)))[0]


    count = length // block
    lane = np.arange(2 * block)
    spot = np.arange(count)[:, None] * block + np.where(lane < block, -lane, 2 * block - lane)[None]
    spot = np.clip(spot, 0, length - 1).reshape(-1).astype(np.int32)
    firsts = jnp.sum((rel_bucket[None, :] < jnp.arange(buckets + 1, dtype=jnp.int32)[:, None]).astype(jnp.int32), axis=1)
    hot = ((spot[None] >= firsts[:-1, None]) & (spot[None] < firsts[1:, None])).astype(f32)
    line = jnp.einsum("bh,bs->hs", rel_bias, hot.astype(bf16), preferred_element_type=f32)
    line = jnp.pad(line, ((0, 8 - heads), (0, 0)))
    seg_col = dec_segments.reshape(length, 1)
    group = Group("self_project")
    (table,) = group.add(bias_kernel, [((heads, block, length), bf16)], [line])
    projected = [((rows, width), bf16), ((rows, 3 * inner), bf16)]
    weights = [norm_gains, self_query, self_keyval]
    normed_own, qkv_own = group.add(self_project_kernel, projected, [own] + weights)
    run(group)
    memory_recv = swap(after(memory_own, normed_own))

    def self_attend(group, chunk):
        return group.add(
            functools.partial(self_attend_kernel, chunk),
            [((rows, inner), bf16), ((heads, rows, (chunk + 1) * rows), bf16)],
            [qkv, seg_col, dec_segments, table],
        )

    group = Group("self_forward_a")
    normed_recv, qkv_recv = group.add(self_project_kernel, projected, [recv] + weights)
    normed_one_a, normed_one_b, qkv = group.add(
        self_order_kernel,
        [((rows, width), bf16), ((rows, width), bf16), ((length, 3 * inner), bf16)],
        [normed_own, qkv_own, normed_recv, qkv_recv],
    )
    ctx_one_a, prob_one_a = self_attend(group, 0)
    run(group)
    ctx_one_recv_a = swap(ctx_one_a)
    weight_beside = flip(after(weight_own, ctx_one_a), 2, dp)
    weight_core = flip(after(weight_own, ctx_one_a), 1, dp)
    group = Group("self_forward_b")
    ctx_one_b, prob_one_b = self_attend(group, 1)
    run(group)
    ctx_one_recv_b = swap(ctx_one_b)
    cot_recv = swap(after(cot, ctx_one_b))

    group = Group("memory_keyval")
    memory_all, kv = group.add(
        memory_kernel,
        [((length, width), bf16), ((length, 2 * inner), bf16)],
        [memory_own, memory_recv, cross_keyval],
    )
    run(group)
    weight_beside_core = flip(after(weight_beside, ctx_one_b), 1, dp)
    group = Group("weights")
    self_output_pair, cross_output_pair = group.add(
        functools.partial(weights_kernel, len(steps) + 1),
        [((inner, width), bf16), ((inner, width), bf16)],
        [weight_own, weight_beside, weight_core, weight_beside_core],
    )
    run(group)

    def cross_forward(group, chunk, before, before_recv):
        return group.add(
            functools.partial(cross_forward_kernel, chunk),
            [
                ((rows, width), f32),
                ((rows, width), bf16),
                ((rows, inner), bf16),
                ((rows, inner), bf16),
                ((heads, rows, length), bf16),
            ],
            [
                own,
                recv,
                before,
                before_recv,
                norm_gains,
                self_output,
                self_output_pair,
                cross_query,
                kv,
                seg_col,
                mem_segments,
            ],
        )

    group = Group("cross_forward_a")
    after_self_a, normed_two_a, query_two_a, ctx_two_a, prob_two_a = cross_forward(group, 0, ctx_one_a, ctx_one_recv_a)
    run(group)
    ctx_two_recv_a = swap(ctx_two_a)
    group = Group("cross_forward_b")
    after_self_b, normed_two_b, query_two_b, ctx_two_b, prob_two_b = cross_forward(group, 1, ctx_one_b, ctx_one_recv_b)
    run(group)
    ctx_two_recv_b = swap(ctx_two_b)

    def ffn(group, chunk, after_self, before, before_recv):
        return group.add(
            functools.partial(ffn_kernel, chunk),
            [
                ((rows, width), f32),
                ((rows, width), bf16),
                ((rows, units), bf16),
                ((rows, 2 * units), bf16),
                ((rows, width), bf16),
            ],
            [
                after_self,
                before,
                before_recv,
                cot,
                cot_recv,
                norm_gains,
                cross_output,
                cross_output_pair,
                ffn_input,
                ffn_output,
            ],
            scratch=[pltpu.VMEM((rows, width), bf16)],
        )

    group = Group("ffn_a")
    after_cross_a, normed_three_a, hidden_a, gate_grads_a, back_three_a = ffn(
        group, 0, after_self_a, ctx_two_a, ctx_two_recv_a
    )
    run(group)
    back_three_recv_a = swap(back_three_a)
    group = Group("ffn_b")
    after_cross_b, normed_three_b, hidden_b, gate_grads_b, back_three_b = ffn(
        group, 1, after_self_b, ctx_two_b, ctx_two_recv_b
    )
    ffn_send, ffn_keep = group.add(
        functools.partial(ffn_grads_kernel, order),
        [((width // 2, 3 * units), bf16)] * 2,
        [
            normed_three_a,
            normed_three_b,
            gate_grads_a,
            gate_grads_b,
            hidden_a,
            hidden_b,
            cot,
            cot_recv,
        ],
        scratch=[pltpu.VMEM((width, length), bf16)] * 2,
        flops=2 * length * width * units * 3,
    )
    run(group)
    back_three_recv_b = swap(back_three_b)
    ffn_sum = Scatter(ffn_send, ffn_keep)

    def cross_back(group, chunk, after, back, back_recv, prob):
        return group.add(
            functools.partial(cross_back_kernel, chunk),
            [
                ((rows, width), f32),
                ((rows, width), bf16),
                ((rows, inner), bf16),
                ((rows, inner), bf16),
                ((heads, rows, length), bf16),
                ((rows, width), bf16),
                ((8, width), f32),
            ],
            [after, back, back_recv, cot, cot_recv, norm_gains, cross_output, cross_query, kv, prob],
            flops=2 * rows * width * inner * 4,
        )

    group = Group("cross_back_a")
    grad_cross_a, sent_two_a, dctx_two_a, dq_two_a, score_two_a, back_two_a, three_a = cross_back(
        group, 0, after_cross_a, back_three_a, back_three_recv_a, prob_two_a
    )
    run(group)
    back_two_recv_a = swap(back_two_a)
    ffn_sum.step("halve_ffn_one")
    group = Group("cross_back_b")
    grad_cross_b, sent_two_b, dctx_two_b, dq_two_b, score_two_b, back_two_b, three_b = cross_back(
        group, 1, after_cross_b, back_three_b, back_three_recv_b, prob_two_b
    )
    run(group)
    back_two_recv_b = swap(back_two_b)
    group = Group("self_back_a")
    cross_send, cross_keep, memory_send, memory_keep = group.add(
        functools.partial(cross_grads_kernel, order),
        [
            ((width // 2, 4 * inner), bf16),
            ((width // 2, 4 * inner), bf16),
            ((rows, width), bf16),
            ((rows, width), f32),
        ],
        [
            normed_two_a,
            normed_two_b,
            dq_two_a,
            dq_two_b,
            query_two_a,
            query_two_b,
            score_two_a,
            score_two_b,
            prob_two_a,
            prob_two_b,
            dctx_two_a,
            dctx_two_b,
            ctx_two_a,
            ctx_two_b,
            sent_two_a,
            sent_two_b,
            memory_all,
            cross_keyval,
        ],
        scratch=[pltpu.VMEM((width, length), bf16)] * 3 + [pltpu.VMEM((length, 2 * inner), bf16)],
        flops=2 * length * width * inner * 8,
    )

    def self_back(group, chunk, after, back, back_recv, grad_cross, prob):
        end = (chunk + 1) * rows
        return group.add(
            functools.partial(self_back_kernel, chunk),
            [
                ((rows, width), f32),
                ((rows, width), bf16),
                ((rows, inner), bf16),
                ((rows, inner), bf16),
                ((heads, rows, end), bf16),
                ((8, width), f32),
            ],
            [after, back, back_recv, grad_cross, norm_gains, self_output, qkv, prob],
            flops=2 * rows * width * inner * 3,
        )

    grad_self_a, sent_one_a, dctx_one_a, dq_one_a, score_one_a, two_a = self_back(
        group, 0, after_self_a, back_two_a, back_two_recv_a, grad_cross_a, prob_one_a
    )
    run(group)
    cross_sum = Scatter(cross_send, cross_keep)
    memory_recv_grad = swap(memory_send)
    group = Group("self_back_b")
    grad_self_b, sent_one_b, dctx_one_b, dq_one_b, score_one_b, two_b = self_back(
        group, 1, after_self_b, back_two_b, back_two_recv_b, grad_cross_b, prob_one_b
    )

    self_send, self_keep, dqkv = group.add(
        functools.partial(self_grads_kernel, order),
        [((width // 2, 4 * inner), bf16), ((width // 2, 4 * inner), bf16), ((length, 3 * inner), bf16)],
        [
            normed_one_a,
            normed_one_b,
            dq_one_a,
            dq_one_b,
            qkv,
            score_one_a,
            score_one_b,
            prob_one_a,
            prob_one_b,
            dctx_one_a,
            dctx_one_b,
            ctx_one_a,
            ctx_one_b,
            sent_one_a,
            sent_one_b,
        ],
        scratch=[pltpu.VMEM((width, length), bf16)] * 2,
        flops=2 * length * width * inner * 6,
    )
    run(group)
    self_sum = Scatter(self_send, self_keep)
    ffn_sum.step("halve_ffn_two")
    cross_sum.step("halve_cross_one")
    group = Group("self_input")
    back_one_send, back_one_keep, small_part = group.add(
        self_input_kernel,
        [((rows + 32, width), bf16), ((rows, width), f32), ((16, width), f32)],
        [
            dqkv,
            own,
            recv,
            self_query,
            self_keyval,
            score_one_a,
            score_one_b,
            hot,
            two_a,
            two_b,
            three_a,
            three_b,
        ],
        scratch=[pltpu.VMEM((8, 2 * length), f32)],
    )
    run(group)
    back_one_recv = swap(back_one_send)
    self_sum.step("halve_self_one")
    cross_sum.step("halve_cross_two")
    group = Group("input_grad")
    (grad_input,) = group.add(
        input_grad_kernel,
        [((rows, width), f32)],
        [own, back_one_keep, back_one_recv, grad_self_a, grad_self_b, norm_gains],
    )
    pair = ((16, 2 * width), bf16)
    (small,) = group.add(add_first_kernel, [pair], [small_part, back_one_recv])
    (out_send,) = group.add(down_kernel, [((rows, width), bf16)], [hidden_a, hidden_b, ffn_output])
    run(group)
    out_recv = swap(out_send)
    small_got = flip(small, 1, dp)
    ffn_sum.step("halve_ffn_three")
    (small,) = single("small_add", add_kernel, [pair], [settled(small), small_got])
    small_got = flip(small, 2, dp)
    cross_sum.step("halve_cross_three")
    carried = steps == [1, 2, 4, 8] and 2 * width == 4 * inner
    if carried:
        self_sum.step("halve_self_two", small, small_got)
    else:
        for bit in sorted(steps)[2:]:
            (small,) = single("small_add", add_kernel, [pair], [settled(small), small_got])
            small_got = flip(small, bit, dp)
        (small,) = single("small_add", add_kernel, [pair], [small, small_got])
        self_sum.step("halve_self_two")
    widths = [(1, inner), (2, inner), (1, inner)]
    group = Group("final")
    (output,) = group.add(
        final_kernel,
        [((rows, width), bf16)],
        [hidden_a, hidden_b, after_cross_a, after_cross_b, out_recv, ffn_output],
    )
    (grad_memory,) = group.add(memory_add_kernel, [((rows, width), f32)], [memory_keep, memory_recv_grad])
    grads_cross = finish(group, cross_sum.total(), widths)
    run(group)
    self_sum.step("halve_self_three")
    group = Group("finish_ffn")
    grads_ffn = finish(group, ffn_sum.total(), [(2, units), (1, units)])
    run(group)
    group = Group("finish_self")
    rest = self_sum.total()
    grads_self = finish(group, rest, widths)
    small_outs = [((3, width), f32), ((2 * heads, buckets), f32)]
    gains, bias = group.add(last_small_kernel, small_outs, [*rest] if carried else [small])
    run(group)
    grads_ffn, grads_cross, grads_self = [[settled(g) for g in grads] for grads in (grads_ffn, grads_cross, grads_self)]
    return (
        settled(output)[None],
        settled(grad_input)[None],
        settled(grad_memory)[None],
        *grads_self[:-1],
        grads_self[-1].T,
        *grads_cross[:-1],
        grads_cross[-1].T,
        *grads_ffn[:-1],
        grads_ffn[-1].T,
        settled(gains),
        settled(bias).T,
    )


def solution(mesh):
    in_specs = (
        P("dp", "mp", None),
        P("dp", "mp", None),
        P("dp", "mp", None),
        P(None, "mp"),
        P(None, None, "mp"),
        P("mp", None),
        P(None, "mp"),
        P(None, None, "mp"),
        P("mp", None),
        P(None, None, "mp"),
        P("mp", None),
        P(),
        P(None, "mp"),
        P("dp", None),
        P("dp", None),
        P(),
    )
    out_specs = (
        P("dp", "mp", None),
        P("dp", "mp", None),
        P("dp", "mp", None),
        P("dp", "mp"),
        P(None, "dp", "mp"),
        P("mp", "dp"),
        P("dp", "mp"),
        P(None, "dp", "mp"),
        P("mp", "dp"),
        P(None, "dp", "mp"),
        P("mp", "dp"),
        P(),
        P(),
    )
    return jax.shard_map(body, mesh=mesh, in_specs=in_specs, out_specs=out_specs, check_vma=False)
```

```python
import functools

import jax
import jax.numpy as jnp
import numpy as np
from jax import lax
from jax.experimental import pallas as pl
from jax.experimental.pallas import tpu as pltpu
from jax.sharding import PartitionSpec as P

epsilon = 1e-06
masked_score = -1e30
gelu_root = float(np.sqrt(2.0 / np.pi))
gelu_cubic = 0.044715
block = 128
head_size = 64
f32 = jnp.float32
bf16 = jnp.bfloat16


def dot(left, right):
    return lax.dot_general(left, right, (((1,), (0,)), ((), ())), preferred_element_type=f32)


def dot_rt(left, right):
    return lax.dot_general(left, right, (((1,), (1,)), ((), ())), preferred_element_type=f32)


def dot_lt(left, right):
    return lax.dot_general(left, right, (((0,), (0,)), ((), ())), preferred_element_type=f32)


def pick(flag, first, second):
    return jnp.where(flag, first, second)


def even_odd(values):
    lane = lax.broadcasted_iota(jnp.int32, values.shape, 1)
    zero = jnp.zeros_like(values)
    return jnp.where(lane < head_size, values, zero), jnp.where(lane < head_size, zero, values)


def rms_scale(values):
    return lax.rsqrt(jnp.mean(values * values, axis=-1, keepdims=True) + epsilon)


def norm_back(values, gain, grad):
    scale = rms_scale(values)
    scaled = grad * gain
    inner = jnp.mean(values * scaled, axis=-1, keepdims=True)
    back = scale * scaled - values * (scale * scale * scale * inner)
    return back, grad * values * scale


def softmax(scores):
    top = jnp.max(scores, axis=-1, keepdims=True)
    weights = jnp.exp(scores - top)
    total = jnp.sum(weights, axis=-1, keepdims=True)
    return (weights * (1.0 / total)).astype(bf16)


times = {"memory_keyval": 10.0, "ffn_b": 10.0, "cross_back_a": 60.0, "cross_back_b": 60.0, "self_back_b": 2.5, "halve_ffn_two": 6.0, "halve_cross_two": 10.0}


class Made:
    def __init__(self, shape, dtype):
        self.shape, self.dtype, self.value = shape, dtype, None


def settled(arg):
    return arg.value if isinstance(arg, Made) and arg.value is not None else arg


class Group:
    def __init__(self, name, cost=0):
        self.name, self.cost, self.stages, self.inputs = name, cost, [], []

    def add(self, kernel, outs, args, scratch=(), flops=0):
        made = [Made(shape, dtype) for shape, dtype in outs]
        args = [settled(arg) for arg in args]
        self.stages.append((kernel, list(args), made, list(scratch)))
        self.cost += flops
        for arg in args:
            if not isinstance(arg, Made) and not any(arg is known for known in self.inputs):
                self.inputs.append(arg)
        return made

    def call(self, idx):
        made = [out for stage in self.stages for out in stage[2]]
        scratch = [item for stage in self.stages for item in stage[3]]

        def kernel(idx_ref, *refs):
            ins, refs = refs[: len(self.inputs)], refs[len(self.inputs) :]
            outs, spare = refs[: len(made)], list(refs[len(made) :])
            known = [(value, ref) for value, ref in zip(self.inputs + made, ins + outs, strict=True)]
            for body, args, stage_outs, stage_scratch in self.stages:
                taken = [next(ref for value, ref in known if value is item) for item in args + stage_outs]
                body(idx_ref, *taken, *[spare.pop(0) for _ in stage_scratch])

        out_shape = [jax.ShapeDtypeStruct(out.shape, out.dtype) for out in made]
        moved = sum(x.size * x.dtype.itemsize for x in self.inputs + out_shape)
        values = pl.pallas_call(
            kernel,
            name=self.name,
            out_shape=out_shape,
            in_specs=[pl.BlockSpec(memory_space=pltpu.SMEM)]
            + [pl.BlockSpec(memory_space=pltpu.VMEM)] * len(self.inputs),
            out_specs=[pl.BlockSpec(memory_space=pltpu.VMEM)] * len(made),
            scratch_shapes=scratch,
            compiler_params=pltpu.CompilerParams(vmem_limit_bytes=8 << 20),
            cost_estimate=pl.CostEstimate(flops=int(times.get(self.name, 0.01) * 1.15e9), transcendentals=0, bytes_accessed=1024),
        )(idx, *self.inputs)
        for out, value in zip(made, values, strict=True):
            out.value = value
        return values


def bias_kernel(idx_ref, line_ref, table_ref):
    heads = table_ref.shape[0]
    count = table_ref.shape[2] // block
    for head in range(heads):
        for step in range(count):
            line = line_ref[head : head + 1, step * 2 * block : (step + 1) * 2 * block]
            wide = jnp.broadcast_to(line, (block, 2 * block))
            turned = pltpu.roll(wide, 0, 1, stride=1, stride_axis=0)
            at = (count - 1 - step) * block
            table_ref[head, :, at : at + block] = turned[:, :block].astype(bf16)


def self_project_kernel(idx_ref, values_ref, gain_ref, wq_ref, wkv_ref, normed_ref, qkv_ref):
    inner = wq_ref.shape[1]
    gain = gain_ref[0:1, :].astype(f32)
    for at in range(0, values_ref.shape[0], block):
        values = values_ref[at : at + block, :].astype(f32)
        normed_ref[at : at + block, :] = (values * rms_scale(values) * gain).astype(bf16)
    qkv_ref[:, 0:inner] = dot(normed_ref[...], wq_ref[...]).astype(bf16)
    qkv_ref[:, inner : 2 * inner] = dot(normed_ref[...], wkv_ref[0]).astype(bf16)
    qkv_ref[:, 2 * inner :] = dot(normed_ref[...], wkv_ref[1]).astype(bf16)


def self_order_kernel(idx_ref, normed_own, qkv_own, normed_recv, qkv_recv, normed_a, normed_b, qkv_ref):
    mine = idx_ref[0] == 0
    rows = normed_own.shape[0]
    normed_a[...] = pick(mine, normed_own[...], normed_recv[...])
    normed_b[...] = pick(mine, normed_recv[...], normed_own[...])
    qkv_ref[0:rows, :] = pick(mine, qkv_own[...], qkv_recv[...])
    qkv_ref[rows:, :] = pick(mine, qkv_recv[...], qkv_own[...])


def self_attend_kernel(chunk, idx_ref, qkv_ref, segc_ref, segr_ref, table_ref, ctx_ref, prob_ref):
    rows, inner = ctx_ref.shape
    base = chunk * rows
    total = table_ref.shape[2]
    masks = []
    for at in range(0, rows, block):
        keys = base + at + block
        allowed = segc_ref[base + at : keys, :] == segr_ref[:, 0:keys]
        row = lax.broadcasted_iota(jnp.int32, (block, keys), 0) + (base + at)
        col = lax.broadcasted_iota(jnp.int32, (block, keys), 1)
        masks.append(jnp.where(allowed & (row >= col), 0.0, masked_score))
    for pair in range(0, inner, 2 * head_size):
        keys2 = qkv_ref[0 : base + rows, inner + pair : inner + pair + 128]
        values_e, values_o = even_odd(qkv_ref[0 : base + rows, 2 * inner + pair : 2 * inner + pair + 128])
        for number, at in enumerate(range(0, rows, block)):
            keys = base + at + block
            query_e, query_o = even_odd(qkv_ref[base + at : keys, pair : pair + 128])
            context = jnp.zeros((block, 128), f32)
            for head, query, values in (
                (pair // head_size, query_e, values_e),
                (pair // head_size + 1, query_o, values_o),
            ):
                scores = dot_rt(query, keys2[0:keys]) + table_ref[head, :, total - keys :].astype(f32)
                probs = softmax(scores + masks[number])
                prob_ref[head, at : at + block, 0:keys] = probs
                context = context + dot(probs, values[0:keys])
            ctx_ref[at : at + block, pair : pair + 128] = context.astype(bf16)


def weights_kernel(quarter_at, idx_ref, own_ref, beside_ref, own_core, beside_core, *outs):
    rows = outs[0].shape[0] // 4
    low, high = idx_ref[quarter_at], idx_ref[quarter_at + 1]
    for number, out_ref in enumerate(outs):
        part = slice(number * rows, (number + 1) * rows)
        for ref, at in (
            (own_ref, 2 * high + low),
            (beside_ref, 2 * (1 - high) + low),
            (own_core, 2 * high + (1 - low)),
            (beside_core, 2 * (1 - high) + (1 - low)),
        ):
            out_ref[pl.ds(pl.multiple_of(at * rows, 16), rows), :] = ref[part, :]


def memory_kernel(idx_ref, own_ref, recv_ref, wkv_ref, memory_ref, kv_ref):
    rows = own_ref.shape[0]
    inner = wkv_ref.shape[2]
    mine = idx_ref[0]
    memory_ref[pl.ds(pl.multiple_of(mine * rows, rows), rows), :] = own_ref[...]
    memory_ref[pl.ds(pl.multiple_of((1 - mine) * rows, rows), rows), :] = recv_ref[...]
    kv_ref[:, 0:inner] = dot(memory_ref[...], wkv_ref[0]).astype(bf16)
    kv_ref[:, inner : 2 * inner] = dot(memory_ref[...], wkv_ref[1]).astype(bf16)


def cross_forward_kernel(
    chunk,
    idx_ref,
    own_ref,
    recv_ref,
    before_ref,
    before_recv_ref,
    gain_ref,
    wo_ref,
    wo_pair_ref,
    wq_ref,
    kv_ref,
    segc_ref,
    segm_ref,
    after_ref,
    normed_ref,
    query_ref,
    ctx_ref,
    prob_ref,
):
    mine = idx_ref[0] == chunk
    rows = own_ref.shape[0]
    inner = wq_ref.shape[1]
    gain = gain_ref[1:2, :].astype(f32)
    after_ref[...] = dot(before_ref[...], wo_ref[...]) + dot(before_recv_ref[...], wo_pair_ref[...])
    for at in range(0, rows, block):
        part = slice(at, at + block)
        values = pick(mine, own_ref[part, :], recv_ref[part, :]).astype(f32) + after_ref[part, :]
        after_ref[part, :] = values
        normed_ref[part, :] = (values * rms_scale(values) * gain).astype(bf16)
    query_ref[...] = dot(normed_ref[...], wq_ref[...]).astype(bf16)
    masks = []
    for at in range(0, rows, block):
        allowed = segc_ref[chunk * rows + at : chunk * rows + at + block, :] == segm_ref[...]
        masks.append(jnp.where(allowed, 0.0, masked_score))
    for pair in range(0, inner, 2 * head_size):
        keys2 = kv_ref[:, pair : pair + 128]
        values_e, values_o = even_odd(kv_ref[:, inner + pair : inner + pair + 128])
        for number, at in enumerate(range(0, rows, block)):
            query_e, query_o = even_odd(query_ref[at : at + block, pair : pair + 128])
            context = jnp.zeros((block, 128), f32)
            for head, query, values in (
                (pair // head_size, query_e, values_e),
                (pair // head_size + 1, query_o, values_o),
            ):
                probs = softmax(dot_rt(query, keys2) + masks[number])
                prob_ref[head, at : at + block, :] = probs
                context = context + dot(probs, values)
            ctx_ref[at : at + block, pair : pair + 128] = context.astype(bf16)


def ffn_kernel(
    chunk,
    idx_ref,
    after_self_ref,
    before_ref,
    before_recv_ref,
    cot_ref,
    cot_recv_ref,
    gain_ref,
    wo_ref,
    wo_pair_ref,
    win_ref,
    wout_ref,
    after_ref,
    normed_ref,
    hidden_ref,
    grads_ref,
    back_ref,
    cot_scr,
):
    mine = idx_ref[0] == chunk
    rows = after_self_ref.shape[0]
    units = win_ref.shape[2]
    gain = gain_ref[2:3, :].astype(f32)
    after_ref[...] = dot(before_ref[...], wo_ref[...]) + dot(before_recv_ref[...], wo_pair_ref[...])
    for at in range(0, rows, block):
        part = slice(at, at + block)
        values = after_self_ref[part, :] + after_ref[part, :]
        after_ref[part, :] = values
        normed_ref[part, :] = (values * rms_scale(values) * gain).astype(bf16)
        cot_scr[part, :] = pick(mine, cot_ref[part, :], cot_recv_ref[part, :])
    wide = 256
    for at in range(0, units, wide):
        cols = slice(at, at + wide)
        gate = dot(normed_ref[...], win_ref[0, :, cols])
        upward = dot(normed_ref[...], win_ref[1, :, cols])
        grad = dot_rt(cot_scr[...], wout_ref[cols, :])
        square = gate * gate
        bend = jnp.tanh(gelu_root * gate * (1.0 + gelu_cubic * square))
        half = 0.5 * (1.0 + bend)
        gelu = gate * half
        slope = half + 0.5 * gelu_root * gate * (1.0 - bend * bend) * (1.0 + 3.0 * gelu_cubic * square)
        hidden_ref[:, cols] = (gelu * upward).astype(bf16)
        grads_ref[:, cols] = (grad * upward * slope).astype(bf16)
        grads_ref[:, units + at : units + at + wide] = (grad * gelu).astype(bf16)
    back_ref[...] = (
        dot_rt(grads_ref[:, 0:units], win_ref[0]) + dot_rt(grads_ref[:, units:], win_ref[1])
    ).astype(bf16)


def down_kernel(idx_ref, first_ref, second_ref, wout_ref, out_ref):
    out_ref[...] = dot(pick(idx_ref[0] == 0, second_ref[...], first_ref[...]), wout_ref[...]).astype(bf16)


def final_kernel(idx_ref, hid_a, hid_b, after_a, after_b, recv_ref, wout_ref, out_ref):
    mine = idx_ref[0] == 0
    own = dot(pick(mine, hid_a[...], hid_b[...]), wout_ref[...])
    out_ref[...] = (pick(mine, after_a[...], after_b[...]) + (own + recv_ref[...].astype(f32))).astype(bf16)


def turn_rows(values, place_ref, order, at):
    turned = jnp.transpose(values)
    size = turned.shape[0] // len(order)
    for number, position in enumerate(order):
        place_ref[position * size : (position + 1) * size, at : at + values.shape[0]] = turned[
            number * size : (number + 1) * size
        ]


def write_grads(bit_ref, turned_ref, right, send_ref, keep_ref, at):
    rows = send_ref.shape[0]
    mine = bit_ref[1]
    cols = slice(at, at + right.shape[1])
    keep_ref[:, cols] = dot(turned_ref[pl.ds(pl.multiple_of(mine * rows, rows), rows), :], right).astype(bf16)
    send_ref[:, cols] = dot(turned_ref[pl.ds(pl.multiple_of((1 - mine) * rows, rows), rows), :], right).astype(bf16)


def ffn_grads_kernel(
    orders,
    idx_ref,
    normed_a,
    normed_b,
    grads_a,
    grads_b,
    hidden_a,
    hidden_b,
    cot_ref,
    cot_recv_ref,
    send_first,
    keep_first,
    send_second,
    keep_second,
    turned,
    turned_two,
    turned_three,
):
    rows = normed_a.shape[0]
    mine = idx_ref[0] == 0
    units = hidden_a.shape[1]
    cut = send_first.shape[1]
    turn_rows(normed_a[...], turned, orders[0], 0)
    turn_rows(normed_b[...], turned, orders[0], rows)
    turn_rows(normed_a[...], turned_two, orders[1], 0)
    turn_rows(normed_b[...], turned_two, orders[1], rows)
    turn_rows(pick(mine, cot_ref[...], cot_recv_ref[...]), turned_three, orders[1], 0)
    turn_rows(pick(mine, cot_recv_ref[...], cot_ref[...]), turned_three, orders[1], rows)
    both = jnp.concatenate([grads_a[...], grads_b[...]], axis=0)
    write_grads(idx_ref, turned, both[:, :cut], send_first, keep_first, 0)
    write_grads(idx_ref, turned_two, both[:, cut:], send_second, keep_second, 0)
    hidden = jnp.concatenate([hidden_a[...], hidden_b[...]], axis=0)
    write_grads(idx_ref, turned_three, hidden, send_second, keep_second, 2 * units - cut)


def attend_back(query_rows, prob_ref, score_ref, grad_ref, key_of, value_of, dq_ref, inner, reach):
    for pair in range(0, inner, 2 * head_size):
        keys_e, keys_o = even_odd(key_of(pair))
        values2 = value_of(pair)
        for at in range(0, query_rows, block):
            keys = reach(at)
            grad_e, grad_o = even_odd(grad_ref[at : at + block, pair : pair + 128])
            total = jnp.zeros((block, 128), f32)
            for head, grad, key in (
                (pair // head_size, grad_e, keys_e),
                (pair // head_size + 1, grad_o, keys_o),
            ):
                probs = prob_ref[head, at : at + block, 0:keys].astype(f32)
                grad_probs = dot_rt(grad, values2[0:keys])
                delta = jnp.sum(probs * grad_probs, axis=-1, keepdims=True) / jnp.sum(
                    probs, axis=-1, keepdims=True
                )
                scores = (probs * (grad_probs - delta)).astype(bf16)
                score_ref[head, at : at + block, 0:keys] = scores
                total = total + dot(scores, key[0:keys])
            dq_ref[at : at + block, pair : pair + 128] = total.astype(bf16)


def cross_back_kernel(
    chunk,
    idx_ref,
    after_ref,
    back_ref,
    back_recv_ref,
    cot_ref,
    cot_recv_ref,
    gain_ref,
    wo_ref,
    wq_ref,
    kv_ref,
    prob_ref,
    grad_ref,
    sent_ref,
    dctx_ref,
    dq_ref,
    score_ref,
    out_ref,
    gain_out_ref,
):
    mine = idx_ref[0] == chunk
    rows = after_ref.shape[0]
    inner = wq_ref.shape[1]
    gain = gain_ref[2:3, :].astype(f32)
    gain_total = jnp.zeros((8, gain.shape[1]), f32)
    for at in range(0, rows, block):
        part = slice(at, at + block)
        incoming = back_ref[part, :].astype(f32) + back_recv_ref[part, :].astype(f32)
        back, gain_terms = norm_back(after_ref[part, :], gain, incoming)
        total = pick(mine, cot_ref[part, :], cot_recv_ref[part, :]).astype(f32) + back
        grad_ref[part, :] = total
        sent_ref[part, :] = total.astype(bf16)
        gain_total = gain_total + jnp.sum(gain_terms.reshape(block // 8, 8, -1), axis=0)
    gain_out_ref[...] = pick(mine, gain_total, jnp.zeros_like(gain_total))
    dctx_ref[...] = dot_rt(sent_ref[...], wo_ref[...]).astype(bf16)
    attend_back(
        rows,
        prob_ref,
        score_ref,
        dctx_ref,
        lambda pair: kv_ref[:, pair : pair + 128],
        lambda pair: kv_ref[:, inner + pair : inner + pair + 128],
        dq_ref,
        inner,
        lambda at: kv_ref.shape[0],
    )
    out_ref[...] = dot_rt(dq_ref[...], wq_ref[...]).astype(bf16)


def cross_grads_kernel(
    order,
    idx_ref,
    normed_a,
    normed_b,
    dq_a,
    dq_b,
    query_a,
    query_b,
    score_a,
    score_b,
    prob_a,
    prob_b,
    dctx_a,
    dctx_b,
    ctx_a,
    ctx_b,
    sent_a,
    sent_b,
    memory_ref,
    wkv_ref,
    send_ref,
    keep_ref,
    memory_send_ref,
    memory_keep_ref,
    turned,
    turned_two,
    turned_three,
    dkv,
):
    rows = normed_a.shape[0]
    inner = dq_a.shape[1]
    for pair in range(0, inner, 2 * head_size):
        keys = jnp.zeros((dkv.shape[0], 128), f32)
        values = jnp.zeros((dkv.shape[0], 128), f32)
        for score, prob, query, dctx in ((score_a, prob_a, query_a, dctx_a), (score_b, prob_b, query_b, dctx_b)):
            cols = slice(pair, pair + 128)
            for number, (query_half, grad_half) in enumerate(
                zip(even_odd(query[:, cols]), even_odd(dctx[:, cols]), strict=True)
            ):
                head = pair // head_size + number
                keys = keys + dot_lt(score[head], query_half)
                values = values + dot_lt(prob[head], grad_half)
        dkv[:, pair : pair + 128] = keys.astype(bf16)
        dkv[:, inner + pair : inner + pair + 128] = values.astype(bf16)
    mine = idx_ref[0]
    other = pl.ds(pl.multiple_of((1 - mine) * rows, rows), rows)
    own = pl.ds(pl.multiple_of(mine * rows, rows), rows)
    memory_send_ref[...] = (
        dot_rt(dkv[other, 0:inner], wkv_ref[0]) + dot_rt(dkv[other, inner:], wkv_ref[1])
    ).astype(bf16)
    memory_keep_ref[...] = dot_rt(dkv[own, 0:inner], wkv_ref[0]) + dot_rt(dkv[own, inner:], wkv_ref[1])
    turn_rows(normed_a[...], turned, order, 0)
    turn_rows(normed_b[...], turned, order, rows)
    both = jnp.concatenate([dq_a[...], dq_b[...]], axis=0)
    write_grads(idx_ref, turned, both, send_ref, keep_ref, 0)
    turn_rows(memory_ref[...], turned_two, order, 0)
    write_grads(idx_ref, turned_two, dkv[...], send_ref, keep_ref, inner)
    turn_rows(sent_a[...], turned_three, order, 0)
    turn_rows(sent_b[...], turned_three, order, rows)
    both = jnp.concatenate([ctx_a[...], ctx_b[...]], axis=0)
    write_grads(idx_ref, turned_three, both, send_ref, keep_ref, 3 * inner)


def self_back_kernel(
    chunk,
    idx_ref,
    after_ref,
    back_ref,
    back_recv_ref,
    cross_ref,
    gain_ref,
    wo_ref,
    qkv_ref,
    prob_ref,
    grad_ref,
    sent_ref,
    dctx_ref,
    dq_ref,
    score_ref,
    gain_out_ref,
):
    mine = idx_ref[0] == chunk
    rows = after_ref.shape[0]
    inner = wo_ref.shape[0]
    gain = gain_ref[1:2, :].astype(f32)
    gain_total = jnp.zeros((8, gain.shape[1]), f32)
    for at in range(0, rows, block):
        part = slice(at, at + block)
        incoming = back_ref[part, :].astype(f32) + back_recv_ref[part, :].astype(f32)
        back, gain_terms = norm_back(after_ref[part, :], gain, incoming)
        total = cross_ref[part, :] + back
        grad_ref[part, :] = total
        sent_ref[part, :] = total.astype(bf16)
        gain_total = gain_total + jnp.sum(gain_terms.reshape(block // 8, 8, -1), axis=0)
    gain_out_ref[...] = pick(mine, gain_total, jnp.zeros_like(gain_total))
    dctx_ref[...] = dot_rt(sent_ref[...], wo_ref[...]).astype(bf16)
    end = (chunk + 1) * rows
    attend_back(
        rows,
        prob_ref,
        score_ref,
        dctx_ref,
        lambda pair: qkv_ref[0:end, inner + pair : inner + pair + 128],
        lambda pair: qkv_ref[0:end, 2 * inner + pair : 2 * inner + pair + 128],
        dq_ref,
        inner,
        lambda at: chunk * rows + at + block,
    )


def self_grads_kernel(
    order,
    idx_ref,
    normed_a,
    normed_b,
    dq_a,
    dq_b,
    qkv_ref,
    score_a,
    score_b,
    prob_a,
    prob_b,
    dctx_a,
    dctx_b,
    ctx_a,
    ctx_b,
    sent_a,
    sent_b,
    send_ref,
    keep_ref,
    dqkv_ref,
    turned,
    turned_two,
):
    rows = normed_a.shape[0]
    inner = dq_a.shape[1]
    for pair in range(0, inner, 2 * head_size):
        for at in range(0, 2 * rows, block):
            keys = jnp.zeros((block, 128), f32)
            values = jnp.zeros((block, 128), f32)
            cols = slice(pair, pair + 128)
            span = slice(at, at + block)
            for base, score, prob, dctx in ((0, score_a, prob_a, dctx_a), (rows, score_b, prob_b, dctx_b)):
                if at >= base + rows:
                    continue
                low = max(at - base, 0)
                for number, (query_half, grad_half) in enumerate(
                    zip(even_odd(qkv_ref[base + low : base + rows, cols]), even_odd(dctx[low:rows, cols]), strict=True)
                ):
                    head = pair // head_size + number
                    keys = keys + dot_lt(score[head, low:rows, span], query_half)
                    values = values + dot_lt(prob[head, low:rows, span], grad_half)
            dqkv_ref[span, inner + pair : inner + pair + 128] = keys.astype(bf16)
            dqkv_ref[span, 2 * inner + pair : 2 * inner + pair + 128] = values.astype(bf16)
    dqkv_ref[0:rows, 0:inner] = dq_a[...]
    dqkv_ref[rows : 2 * rows, 0:inner] = dq_b[...]
    turn_rows(normed_a[...], turned, order, 0)
    turn_rows(normed_b[...], turned, order, rows)
    write_grads(idx_ref, turned, dqkv_ref[...], send_ref, keep_ref, 0)
    turn_rows(sent_a[...], turned_two, order, 0)
    turn_rows(sent_b[...], turned_two, order, rows)
    both = jnp.concatenate([ctx_a[...], ctx_b[...]], axis=0)
    write_grads(idx_ref, turned_two, both, send_ref, keep_ref, 3 * inner)


def diagonals(values):
    wide = jnp.concatenate([values, jnp.zeros_like(values)], axis=1)
    total = wide[0:8]
    for at in range(8, block, 8):
        total = total + pltpu.roll(wide[at : at + 8], 2 * block - at, 1)
    row = lax.broadcasted_iota(jnp.int32, total.shape, 0)
    for bit in (1, 2, 4):
        total = jnp.where((row & bit) != 0, pltpu.roll(total, 2 * block - bit, 1), total)
    return jnp.sum(total, axis=0, keepdims=True)


def self_input_kernel(
    idx_ref,
    dqkv_ref,
    own_ref,
    recv_ref,
    wq_ref,
    wkv_ref,
    score_a,
    score_b,
    hot_ref,
    two_a,
    two_b,
    three_a,
    three_b,
    send_ref,
    keep_ref,
    small_ref,
    line,
):
    rows = own_ref.shape[0]
    inner = wq_ref.shape[1]
    mine = idx_ref[0]
    gain_total = jnp.zeros((8, own_ref.shape[1]), f32)
    for which, values_ref in ((1 - mine, recv_ref), (mine, own_ref)):
        span = pl.ds(pl.multiple_of(which * rows, rows), rows)
        grad = (
            dot_rt(dqkv_ref[span, 0:inner], wq_ref[...])
            + dot_rt(dqkv_ref[span, inner : 2 * inner], wkv_ref[0])
            + dot_rt(dqkv_ref[span, 2 * inner :], wkv_ref[1])
        )
        if values_ref is recv_ref:
            send_ref[0:rows, :] = grad.astype(bf16)
        else:
            keep_ref[...] = grad
        values = values_ref[...].astype(f32)
        terms = grad * values * rms_scale(values)
        gain_total = gain_total + jnp.sum(terms.reshape(rows // 8, 8, -1), axis=0)
    heads = score_a.shape[0]
    count = 2 * rows // block
    line[...] = jnp.zeros_like(line)
    for head in range(heads):
        for step in range(count):
            total = jnp.zeros((block, block), f32)
            for at in range(step, count):
                col = (at - step) * block
                score = score_a if at * block < rows else score_b
                row = at * block % rows
                total = total + score[head, row : row + block, col : col + block].astype(f32)
            line[head : head + 1, step * 2 * block : (step + 1) * 2 * block] = diagonals(total)
    bias = lax.dot_general(
        line[...], hot_ref[...], (((1,), (1,)), ((), ())), precision=lax.Precision.HIGHEST, preferred_element_type=f32
    )
    buckets = hot_ref.shape[0]
    small_ref[...] = jnp.zeros_like(small_ref)
    small_ref[0:1, :] = jnp.sum(gain_total, axis=0, keepdims=True)
    small_ref[1:2, :] = jnp.sum(two_a[...] + two_b[...], axis=0, keepdims=True)
    small_ref[2:3, :] = jnp.sum(three_a[...] + three_b[...], axis=0, keepdims=True)
    small_ref[8:16, 0:buckets] = pick(mine == 0, bias, jnp.zeros_like(bias))
    small_ref[8:16, 128 : 128 + buckets] = pick(mine == 1, bias, jnp.zeros_like(bias))
    high = small_ref[...].astype(bf16)
    send_ref[rows : rows + 16, :] = high
    send_ref[rows + 16 :, :] = (small_ref[...] - high.astype(f32)).astype(bf16)


def input_grad_kernel(idx_ref, own_ref, keep_ref, recv_ref, grad_a, grad_b, gain_ref, out_ref):
    mine = idx_ref[0] == 0
    gain = gain_ref[0:1, :].astype(f32)
    for at in range(0, own_ref.shape[0], block):
        part = slice(at, at + block)
        incoming = keep_ref[part, :] + recv_ref[part, :].astype(f32)
        back, _ = norm_back(own_ref[part, :].astype(f32), gain, incoming)
        out_ref[part, :] = pick(mine, grad_a[part, :], grad_b[part, :]) + back


def halve_kernel(slot, idx_ref, keep_ref, got_ref, send_out, keep_out):
    rows = send_out.shape[0]
    mine = idx_ref[slot]
    other = pl.ds(pl.multiple_of((1 - mine) * rows, 16), rows)
    own = pl.ds(pl.multiple_of(mine * rows, 16), rows)
    send_out[...] = (keep_ref[other, :].astype(f32) + got_ref[other, :].astype(f32)).astype(bf16)
    keep_out[...] = (keep_ref[own, :].astype(f32) + got_ref[own, :].astype(f32)).astype(bf16)


def split_small(values):
    high = values.astype(bf16)
    return jnp.concatenate([high, (values - high.astype(f32)).astype(bf16)], axis=1)


def join_small(parts):
    width = parts.shape[1] // 2
    return parts[:, :width].astype(f32) + parts[:, width:].astype(f32)


def add_kernel(idx_ref, first_ref, second_ref, out_ref):
    out_ref[...] = split_small(join_small(first_ref[...]) + join_small(second_ref[...]))


def add_first_kernel(idx_ref, own_ref, got_ref, out_ref):
    rows = own_ref.shape[0]
    at = got_ref.shape[0] - 2 * rows
    got = got_ref[at : at + rows, :].astype(f32) + got_ref[at + rows :, :].astype(f32)
    out_ref[...] = split_small(join_small(split_small(own_ref[...])) + got)


def halve_small_kernel(slot, has_small, idx_ref, keep_ref, got_ref, *refs):
    send_out, keep_out = refs[-2:]
    count = 16
    rows = send_out.shape[0] - count
    mine = idx_ref[slot]
    other = pl.ds(pl.multiple_of((1 - mine) * rows, 16), rows)
    own = pl.ds(pl.multiple_of(mine * rows, 16), rows)
    send_out[0:rows, :] = (keep_ref[other, :].astype(f32) + got_ref[other, :].astype(f32)).astype(bf16)
    keep_out[0:rows, :] = (keep_ref[own, :].astype(f32) + got_ref[own, :].astype(f32)).astype(bf16)
    if has_small:
        small = split_small(join_small(keep_ref[2 * rows :, :]) + join_small(got_ref[2 * rows :, :]))
    else:
        small = split_small(join_small(refs[0][...]) + join_small(refs[1][...]))
    send_out[rows:, :] = small
    keep_out[rows:, :] = small


def finish_small_kernel(idx_ref, keep_ref, got_ref, out_ref):
    rows = keep_ref.shape[0] - 16
    out_ref[...] = split_small(join_small(keep_ref[rows:, :]) + join_small(got_ref[rows:, :]))


def last_small_kernel(idx_ref, *refs):
    *parts, gain_out, bias_out = refs
    at = parts[0].shape[0] - 16
    total = join_small(parts[0][at:, :])
    for part in parts[1:]:
        total = total + join_small(part[at:, :])
    heads, buckets = bias_out.shape[0] // 2, bias_out.shape[1]
    gain_out[...] = total[0:3, :]
    bias_out[0:heads, :] = total[8 : 8 + heads, 0:buckets]
    bias_out[heads:, :] = total[8 : 8 + heads, 128 : 128 + buckets]


def memory_add_kernel(idx_ref, keep_ref, got_ref, out_ref):
    out_ref[...] = keep_ref[...] + got_ref[...].astype(f32)


def finish_kernel(idx_ref, *refs):
    count = next(at for at, ref in enumerate(refs) if ref.dtype == f32)
    left = refs[-1].shape[0]
    starts = [0]
    for keep_ref in refs[0:count:2]:
        starts.append(starts[-1] + keep_ref.shape[1])

    def pieces(low, high):
        for number, start in enumerate(starts[:-1]):
            at, end = max(low, start), min(high, starts[number + 1])
            if at < end:
                cols = slice(at - start, end - start)
                keep = refs[2 * number][0:left, cols].astype(f32)
                yield at - low, end - low, keep + refs[2 * number + 1][0:left, cols].astype(f32)

    at = 0
    for out in refs[count:]:
        for values in [out] if len(out.shape) == 2 else [out.at[n] for n in range(out.shape[0])]:
            for low, high, total in pieces(at, at + values.shape[1]):
                values[:, low:high] = total
            at += values.shape[1]


def flip(values, bit, size):
    return lax.ppermute(settled(values), "dp", [(at, at ^ bit) for at in range(size)])


def swap(values):
    return lax.ppermute(settled(values), "mp", [(0, 1), (1, 0)])


def halving_plans(size, width):
    bits = [1 << at for at in range(size.bit_length() - 1)]
    if (width // size) % 16:
        return (bits[::-1], [0]), (bits[::-1], [0])
    plans = []
    for steps in (bits, bits[:1] + bits[2:] + bits[1:2]):
        order = [sum(((at // bit) % 2) * (size >> (step + 1)) for step, bit in enumerate(steps)) for at in range(size)]
        plans.append((steps, order))
    return plans


def body(
    hidden_in,
    memory,
    cotangent,
    self_query,
    self_keyval,
    self_output,
    cross_query,
    cross_keyval,
    cross_output,
    ffn_input,
    ffn_output,
    norm_gains,
    rel_bias,
    dec_segments,
    mem_segments,
    rel_bucket,
):
    dp = lax.axis_size("dp")
    position = lax.axis_index("dp")
    half = lax.axis_index("mp")
    own = hidden_in[0]
    rows, width = own.shape
    length = 2 * rows
    buckets, heads = rel_bias.shape
    inner = self_query.shape[1]
    units = ffn_output.shape[0]
    memory_own = memory[0]
    cot = cotangent[0]
    (steps, order), (ffn_steps, ffn_order) = halving_plans(dp, width)
    quarter = [position % 2, (position // 2) % 2]
    idx = jnp.stack([half] + [(position // bit) % 2 for bit in steps] + quarter).astype(jnp.int32)
    order_token = [idx]

    def run(group):
        if not group.stages:
            return []
        values = group.call(order_token[0])
        order_token[0] = lax.optimization_barrier((idx, values[-1]))[0]
        return values

    def single(name, kernel, outs, args, **options):
        group = Group(name)
        group.add(kernel, outs, args, **options)
        return run(group)

    places = steps

    class Scatter:
        def __init__(self, steps, send, keep):
            self.steps, self.keep, self.at, self.extra = steps, keep, 0, 0
            self.got = flip(send, self.steps[0], dp)

        def halve(self, group, *small):
            self.at += 1
            keep = settled(self.keep)
            cut, bit = (keep.shape[0] - self.extra) // 2, self.steps[self.at]
            if small or self.extra:
                kernel = functools.partial(halve_small_kernel, 1 + places.index(bit), self.extra > 0)
                self.extra = 16
                shape = ((cut + 16, keep.shape[1]), bf16)
                self.out, self.keep = group.add(kernel, [shape] * 2, [keep, self.got, *small])
            elif cut % 16 == 0:
                kernel = functools.partial(halve_kernel, 1 + places.index(bit))
                self.out, self.keep = group.add(kernel, [((cut, keep.shape[1]), bf16)] * 2, [keep, self.got])
            else:
                mine = ((position // bit) % 2) * cut
                take = functools.partial(lax.dynamic_slice_in_dim, slice_size=cut, axis=0)
                total = [(take(keep, at).astype(f32) + take(self.got, at).astype(f32)) for at in (cut - mine, mine)]
                self.out, self.keep = [values.astype(bf16) for values in total]

        def send(self):
            self.got = flip(self.out, self.steps[self.at], dp)

        def step(self, name, *small):
            group = Group(name)
            self.halve(group, *small)
            run(group)
            self.send()

        def total(self):
            while self.at < len(self.steps) - 1:
                self.step("halve")
            return settled(self.keep), self.got

    def together(name, *sums):
        group = Group(name)
        for item in sums:
            item.halve(group)
        run(group)
        for item in sums:
            item.send()

    def finish(group, sums, widths):
        left = width // dp
        shapes = [((left, w), f32) if n == 1 else ((n, left, w), f32) for n, w in widths]
        if left % 16 == 0:
            return group.add(finish_kernel, shapes, sums)
        total = jnp.concatenate([k.astype(f32) + g.astype(f32) for k, g in zip(sums[::2], sums[1::2], strict=True)], axis=1)
        outs, at = [], 0
        for n, w in widths:
            outs.append(total[:, at : at + n * w])
            at += n * w
        return [o if n == 1 else jnp.stack(jnp.split(o, n, axis=1)) for o, (n, w) in zip(outs, widths, strict=True)]

    recv = swap(own)
    piece = inner // 4
    spot = (position % 4) * piece
    cut = functools.partial(lax.dynamic_slice_in_dim, start_index=spot, slice_size=piece, axis=0)
    weight_own = swap(jnp.concatenate([cut(self_output), cut(cross_output)]))

    def after(values, made):
        return lax.optimization_barrier((values, settled(made)))[0]


    count = length // block
    lane = np.arange(2 * block)
    spot = np.arange(count)[:, None] * block + np.where(lane < block, -lane, 2 * block - lane)[None]
    spot = np.clip(spot, 0, length - 1).reshape(-1).astype(np.int32)
    firsts = jnp.sum((rel_bucket[None, :] < jnp.arange(buckets + 1, dtype=jnp.int32)[:, None]).astype(jnp.int32), axis=1)
    hot = ((spot[None] >= firsts[:-1, None]) & (spot[None] < firsts[1:, None])).astype(f32)
    line = jnp.einsum("bh,bs->hs", rel_bias, hot.astype(bf16), preferred_element_type=f32)
    line = jnp.pad(line, ((0, 8 - heads), (0, 0)))
    seg_col = dec_segments.reshape(length, 1)
    group = Group("self_project")
    (table,) = group.add(bias_kernel, [((heads, block, length), bf16)], [line])
    projected = [((rows, width), bf16), ((rows, 3 * inner), bf16)]
    weights = [norm_gains, self_query, self_keyval]
    normed_own, qkv_own = group.add(self_project_kernel, projected, [own] + weights)
    run(group)
    memory_recv = swap(after(memory_own, normed_own))

    def self_attend(group, chunk):
        return group.add(
            functools.partial(self_attend_kernel, chunk),
            [((rows, inner), bf16), ((heads, rows, (chunk + 1) * rows), bf16)],
            [qkv, seg_col, dec_segments, table],
        )

    group = Group("self_forward_a")
    normed_recv, qkv_recv = group.add(self_project_kernel, projected, [recv] + weights)
    normed_one_a, normed_one_b, qkv = group.add(
        self_order_kernel,
        [((rows, width), bf16), ((rows, width), bf16), ((length, 3 * inner), bf16)],
        [normed_own, qkv_own, normed_recv, qkv_recv],
    )
    ctx_one_a, prob_one_a = self_attend(group, 0)
    run(group)
    ctx_one_recv_a = swap(ctx_one_a)
    weight_beside = flip(after(weight_own, ctx_one_a), 2, dp)
    weight_core = flip(after(weight_own, ctx_one_a), 1, dp)
    group = Group("self_forward_b")
    ctx_one_b, prob_one_b = self_attend(group, 1)
    run(group)
    ctx_one_recv_b = swap(ctx_one_b)
    cot_recv = swap(after(cot, ctx_one_b))

    group = Group("memory_keyval")
    memory_all, kv = group.add(
        memory_kernel,
        [((length, width), bf16), ((length, 2 * inner), bf16)],
        [memory_own, memory_recv, cross_keyval],
    )
    run(group)
    weight_beside_core = flip(after(weight_beside, ctx_one_b), 1, dp)
    def cross_forward(group, chunk, before, before_recv):
        return group.add(
            functools.partial(cross_forward_kernel, chunk),
            [
                ((rows, width), f32),
                ((rows, width), bf16),
                ((rows, inner), bf16),
                ((rows, inner), bf16),
                ((heads, rows, length), bf16),
            ],
            [
                own,
                recv,
                before,
                before_recv,
                norm_gains,
                self_output,
                self_output_pair,
                cross_query,
                kv,
                seg_col,
                mem_segments,
            ],
        )

    group = Group("cross_forward_a")
    self_output_pair, cross_output_pair = group.add(
        functools.partial(weights_kernel, len(steps) + 1),
        [((inner, width), bf16), ((inner, width), bf16)],
        [weight_own, weight_beside, weight_core, weight_beside_core],
    )
    after_self_a, normed_two_a, query_two_a, ctx_two_a, prob_two_a = cross_forward(group, 0, ctx_one_a, ctx_one_recv_a)
    run(group)
    ctx_two_recv_a = swap(ctx_two_a)
    group = Group("cross_forward_b")
    after_self_b, normed_two_b, query_two_b, ctx_two_b, prob_two_b = cross_forward(group, 1, ctx_one_b, ctx_one_recv_b)
    run(group)
    ctx_two_recv_b = swap(ctx_two_b)

    def ffn(group, chunk, after_self, before, before_recv):
        return group.add(
            functools.partial(ffn_kernel, chunk),
            [
                ((rows, width), f32),
                ((rows, width), bf16),
                ((rows, units), bf16),
                ((rows, 2 * units), bf16),
                ((rows, width), bf16),
            ],
            [
                after_self,
                before,
                before_recv,
                cot,
                cot_recv,
                norm_gains,
                cross_output,
                cross_output_pair,
                ffn_input,
                ffn_output,
            ],
            scratch=[pltpu.VMEM((rows, width), bf16)],
        )

    group = Group("ffn_a")
    after_cross_a, normed_three_a, hidden_a, gate_grads_a, back_three_a = ffn(
        group, 0, after_self_a, ctx_two_a, ctx_two_recv_a
    )
    run(group)
    back_three_recv_a = swap(back_three_a)
    group = Group("ffn_b")
    after_cross_b, normed_three_b, hidden_b, gate_grads_b, back_three_b = ffn(
        group, 1, after_self_b, ctx_two_b, ctx_two_recv_b
    )
    first_send, first_keep, second_send, second_keep = group.add(
        functools.partial(ffn_grads_kernel, [order, ffn_order]),
        [((width // 2, 3 * units // 2), bf16)] * 4,
        [
            normed_three_a,
            normed_three_b,
            gate_grads_a,
            gate_grads_b,
            hidden_a,
            hidden_b,
            cot,
            cot_recv,
        ],
        scratch=[pltpu.VMEM((width, length), bf16)] * 3,
        flops=2 * length * width * units * 3,
    )
    run(group)
    back_three_recv_b = swap(back_three_b)
    ffn_sums = [Scatter(steps, first_send, first_keep), Scatter(ffn_steps, second_send, second_keep)]

    def cross_back(group, chunk, after, back, back_recv, prob):
        return group.add(
            functools.partial(cross_back_kernel, chunk),
            [
                ((rows, width), f32),
                ((rows, width), bf16),
                ((rows, inner), bf16),
                ((rows, inner), bf16),
                ((heads, rows, length), bf16),
                ((rows, width), bf16),
                ((8, width), f32),
            ],
            [after, back, back_recv, cot, cot_recv, norm_gains, cross_output, cross_query, kv, prob],
            flops=2 * rows * width * inner * 4,
        )

    group = Group("cross_back_a")
    grad_cross_a, sent_two_a, dctx_two_a, dq_two_a, score_two_a, back_two_a, three_a = cross_back(
        group, 0, after_cross_a, back_three_a, back_three_recv_a, prob_two_a
    )
    run(group)
    back_two_recv_a = swap(back_two_a)
    together("halve_ffn_one", *ffn_sums)
    group = Group("cross_back_b")
    grad_cross_b, sent_two_b, dctx_two_b, dq_two_b, score_two_b, back_two_b, three_b = cross_back(
        group, 1, after_cross_b, back_three_b, back_three_recv_b, prob_two_b
    )
    run(group)
    back_two_recv_b = swap(back_two_b)
    group = Group("self_back_a")
    cross_send, cross_keep, memory_send, memory_keep = group.add(
        functools.partial(cross_grads_kernel, order),
        [
            ((width // 2, 4 * inner), bf16),
            ((width // 2, 4 * inner), bf16),
            ((rows, width), bf16),
            ((rows, width), f32),
        ],
        [
            normed_two_a,
            normed_two_b,
            dq_two_a,
            dq_two_b,
            query_two_a,
            query_two_b,
            score_two_a,
            score_two_b,
            prob_two_a,
            prob_two_b,
            dctx_two_a,
            dctx_two_b,
            ctx_two_a,
            ctx_two_b,
            sent_two_a,
            sent_two_b,
            memory_all,
            cross_keyval,
        ],
        scratch=[pltpu.VMEM((width, length), bf16)] * 3 + [pltpu.VMEM((length, 2 * inner), bf16)],
        flops=2 * length * width * inner * 8,
    )

    def self_back(group, chunk, after, back, back_recv, grad_cross, prob):
        end = (chunk + 1) * rows
        return group.add(
            functools.partial(self_back_kernel, chunk),
            [
                ((rows, width), f32),
                ((rows, width), bf16),
                ((rows, inner), bf16),
                ((rows, inner), bf16),
                ((heads, rows, end), bf16),
                ((8, width), f32),
            ],
            [after, back, back_recv, grad_cross, norm_gains, self_output, qkv, prob],
            flops=2 * rows * width * inner * 3,
        )

    grad_self_a, sent_one_a, dctx_one_a, dq_one_a, score_one_a, two_a = self_back(
        group, 0, after_self_a, back_two_a, back_two_recv_a, grad_cross_a, prob_one_a
    )
    run(group)
    cross_sum = Scatter(steps, cross_send, cross_keep)
    memory_recv_grad = swap(memory_send)
    group = Group("self_back_b")
    grad_self_b, sent_one_b, dctx_one_b, dq_one_b, score_one_b, two_b = self_back(
        group, 1, after_self_b, back_two_b, back_two_recv_b, grad_cross_b, prob_one_b
    )

    self_send, self_keep, dqkv = group.add(
        functools.partial(self_grads_kernel, order),
        [((width // 2, 4 * inner), bf16), ((width // 2, 4 * inner), bf16), ((length, 3 * inner), bf16)],
        [
            normed_one_a,
            normed_one_b,
            dq_one_a,
            dq_one_b,
            qkv,
            score_one_a,
            score_one_b,
            prob_one_a,
            prob_one_b,
            dctx_one_a,
            dctx_one_b,
            ctx_one_a,
            ctx_one_b,
            sent_one_a,
            sent_one_b,
        ],
        scratch=[pltpu.VMEM((width, length), bf16)] * 2,
        flops=2 * length * width * inner * 6,
    )
    run(group)
    self_sum = Scatter(steps, self_send, self_keep)
    together("halve_ffn_two", *ffn_sums)
    cross_sum.step("halve_cross_one")
    group = Group("self_input")
    back_one_send, back_one_keep, small_part = group.add(
        self_input_kernel,
        [((rows + 32, width), bf16), ((rows, width), f32), ((16, width), f32)],
        [
            dqkv,
            own,
            recv,
            self_query,
            self_keyval,
            score_one_a,
            score_one_b,
            hot,
            two_a,
            two_b,
            three_a,
            three_b,
        ],
        scratch=[pltpu.VMEM((8, 2 * length), f32)],
    )
    run(group)
    back_one_recv = swap(back_one_send)
    self_sum.step("halve_self_one")
    cross_sum.step("halve_cross_two")
    group = Group("input_grad")
    (grad_input,) = group.add(
        input_grad_kernel,
        [((rows, width), f32)],
        [own, back_one_keep, back_one_recv, grad_self_a, grad_self_b, norm_gains],
    )
    pair = ((16, 2 * width), bf16)
    (small,) = group.add(add_first_kernel, [pair], [small_part, back_one_recv])
    (out_send,) = group.add(down_kernel, [((rows, width), bf16)], [hidden_a, hidden_b, ffn_output])
    run(group)
    out_recv = swap(out_send)
    small_got = flip(small, 1, dp)
    together("halve_ffn_three", *ffn_sums)
    (small,) = single("small_add", add_kernel, [pair], [settled(small), small_got])
    small_got = flip(small, 2, dp)
    cross_sum.step("halve_cross_three")
    carried = steps == [1, 2, 4, 8] and 2 * width == 4 * inner
    if carried:
        self_sum.step("halve_self_two", small, small_got)
    else:
        for bit in sorted(steps)[2:]:
            (small,) = single("small_add", add_kernel, [pair], [settled(small), small_got])
            small_got = flip(small, bit, dp)
        (small,) = single("small_add", add_kernel, [pair], [small, small_got])
        self_sum.step("halve_self_two")
    widths = [(1, inner), (2, inner), (1, inner)]
    group = Group("final")
    (output,) = group.add(
        final_kernel,
        [((rows, width), bf16)],
        [hidden_a, hidden_b, after_cross_a, after_cross_b, out_recv, ffn_output],
    )
    (grad_memory,) = group.add(memory_add_kernel, [((rows, width), f32)], [memory_keep, memory_recv_grad])
    grads_cross = finish(group, cross_sum.total(), widths)
    grads_ffn = finish(group, [part for item in ffn_sums for part in item.total()], [(2, units), (1, units)])
    run(group)
    self_sum.step("halve_self_three")
    group = Group("finish_self")
    rest = self_sum.total()
    grads_self = finish(group, rest, widths)
    small_outs = [((3, width), f32), ((2 * heads, buckets), f32)]
    gains, bias = group.add(last_small_kernel, small_outs, [*rest] if carried else [small])
    run(group)
    grads_ffn, grads_cross, grads_self = [[settled(g) for g in grads] for grads in (grads_ffn, grads_cross, grads_self)]
    return (
        settled(output)[None],
        settled(grad_input)[None],
        settled(grad_memory)[None],
        *grads_self[:-1],
        grads_self[-1].T,
        *grads_cross[:-1],
        grads_cross[-1].T,
        *grads_ffn[:-1],
        grads_ffn[-1].T,
        settled(gains),
        settled(bias).T,
    )


def solution(mesh):
    in_specs = (
        P("dp", "mp", None),
        P("dp", "mp", None),
        P("dp", "mp", None),
        P(None, "mp"),
        P(None, None, "mp"),
        P("mp", None),
        P(None, "mp"),
        P(None, None, "mp"),
        P("mp", None),
        P(None, None, "mp"),
        P("mp", None),
        P(),
        P(None, "mp"),
        P("dp", None),
        P("dp", None),
        P(),
    )
    out_specs = (
        P("dp", "mp", None),
        P("dp", "mp", None),
        P("dp", "mp", None),
        P("dp", "mp"),
        P(None, "dp", "mp"),
        P("mp", "dp"),
        P("dp", "mp"),
        P(None, "dp", "mp"),
        P("mp", "dp"),
        P(None, "dp", "mp"),
        P("mp", "dp"),
        P(),
        P(),
    )
    return jax.shard_map(body, mesh=mesh, in_specs=in_specs, out_specs=out_specs, check_vma=False)
```

```python
import functools

import jax
import jax.numpy as jnp
import numpy as np
from jax import lax
from jax.experimental import pallas as pl
from jax.experimental.pallas import tpu as pltpu
from jax.sharding import PartitionSpec as P

epsilon = 1e-06
masked_score = -1e30
gelu_root = float(np.sqrt(2.0 / np.pi))
gelu_cubic = 0.044715
block = 128
head_size = 64
f32 = jnp.float32
bf16 = jnp.bfloat16


def dot(left, right):
    return lax.dot_general(left, right, (((1,), (0,)), ((), ())), preferred_element_type=f32)


def dot_rt(left, right):
    return lax.dot_general(left, right, (((1,), (1,)), ((), ())), preferred_element_type=f32)


def dot_lt(left, right):
    return lax.dot_general(left, right, (((0,), (0,)), ((), ())), preferred_element_type=f32)


def pick(flag, first, second):
    return jnp.where(flag, first, second)


def even_odd(values):
    lane = lax.broadcasted_iota(jnp.int32, values.shape, 1)
    zero = jnp.zeros_like(values)
    return jnp.where(lane < head_size, values, zero), jnp.where(lane < head_size, zero, values)


def rms_scale(values):
    return lax.rsqrt(jnp.mean(values * values, axis=-1, keepdims=True) + epsilon)


def norm_back(values, gain, grad):
    scale = rms_scale(values)
    scaled = grad * gain
    inner = jnp.mean(values * scaled, axis=-1, keepdims=True)
    back = scale * scaled - values * (scale * scale * scale * inner)
    return back, grad * values * scale


def softmax(scores):
    top = jnp.max(scores, axis=-1, keepdims=True)
    weights = jnp.exp(scores - top)
    total = jnp.sum(weights, axis=-1, keepdims=True)
    return (weights * (1.0 / total)).astype(bf16)


times = {"memory_keyval": 10.0, "ffn_b": 10.0, "cross_back_a": 60.0, "cross_back_b": 60.0, "self_back_b": 2.5, "halve_ffn_two": 6.0, "halve_cross_two": 10.0, "final": 15.0}


class Made:
    def __init__(self, shape, dtype):
        self.shape, self.dtype, self.value = shape, dtype, None


def settled(arg):
    return arg.value if isinstance(arg, Made) and arg.value is not None else arg


class Group:
    def __init__(self, name, cost=0):
        self.name, self.cost, self.stages, self.inputs = name, cost, [], []

    def add(self, kernel, outs, args, scratch=(), flops=0):
        made = [Made(shape, dtype) for shape, dtype in outs]
        args = [settled(arg) for arg in args]
        self.stages.append((kernel, list(args), made, list(scratch)))
        self.cost += flops
        for arg in args:
            if not isinstance(arg, Made) and not any(arg is known for known in self.inputs):
                self.inputs.append(arg)
        return made

    def call(self, idx):
        made = [out for stage in self.stages for out in stage[2]]
        scratch = [item for stage in self.stages for item in stage[3]]

        def kernel(idx_ref, *refs):
            ins, refs = refs[: len(self.inputs)], refs[len(self.inputs) :]
            outs, spare = refs[: len(made)], list(refs[len(made) :])
            known = [(value, ref) for value, ref in zip(self.inputs + made, ins + outs, strict=True)]
            for body, args, stage_outs, stage_scratch in self.stages:
                taken = [next(ref for value, ref in known if value is item) for item in args + stage_outs]
                body(idx_ref, *taken, *[spare.pop(0) for _ in stage_scratch])

        out_shape = [jax.ShapeDtypeStruct(out.shape, out.dtype) for out in made]
        moved = sum(x.size * x.dtype.itemsize for x in self.inputs + out_shape)
        values = pl.pallas_call(
            kernel,
            name=self.name,
            out_shape=out_shape,
            in_specs=[pl.BlockSpec(memory_space=pltpu.SMEM)]
            + [pl.BlockSpec(memory_space=pltpu.VMEM)] * len(self.inputs),
            out_specs=[pl.BlockSpec(memory_space=pltpu.VMEM)] * len(made),
            scratch_shapes=scratch,
            compiler_params=pltpu.CompilerParams(vmem_limit_bytes=8 << 20),
            cost_estimate=pl.CostEstimate(flops=int(times.get(self.name, 0.01) * 1.15e9), transcendentals=0, bytes_accessed=1024),
        )(idx, *self.inputs)
        for out, value in zip(made, values, strict=True):
            out.value = value
        return values


def bias_kernel(idx_ref, line_ref, table_ref):
    heads = table_ref.shape[0]
    count = table_ref.shape[2] // block
    for head in range(heads):
        for step in range(count):
            line = line_ref[head : head + 1, step * 2 * block : (step + 1) * 2 * block]
            wide = jnp.broadcast_to(line, (block, 2 * block))
            turned = pltpu.roll(wide, 0, 1, stride=1, stride_axis=0)
            at = (count - 1 - step) * block
            table_ref[head, :, at : at + block] = turned[:, :block].astype(bf16)


def self_project_kernel(idx_ref, values_ref, gain_ref, wq_ref, wkv_ref, normed_ref, qkv_ref):
    inner = wq_ref.shape[1]
    gain = gain_ref[0:1, :].astype(f32)
    for at in range(0, values_ref.shape[0], block):
        values = values_ref[at : at + block, :].astype(f32)
        normed_ref[at : at + block, :] = (values * rms_scale(values) * gain).astype(bf16)
    qkv_ref[:, 0:inner] = dot(normed_ref[...], wq_ref[...]).astype(bf16)
    qkv_ref[:, inner : 2 * inner] = dot(normed_ref[...], wkv_ref[0]).astype(bf16)
    qkv_ref[:, 2 * inner :] = dot(normed_ref[...], wkv_ref[1]).astype(bf16)


def self_order_kernel(idx_ref, normed_own, qkv_own, normed_recv, qkv_recv, normed_a, normed_b, qkv_ref):
    mine = idx_ref[0] == 0
    rows = normed_own.shape[0]
    normed_a[...] = pick(mine, normed_own[...], normed_recv[...])
    normed_b[...] = pick(mine, normed_recv[...], normed_own[...])
    qkv_ref[0:rows, :] = pick(mine, qkv_own[...], qkv_recv[...])
    qkv_ref[rows:, :] = pick(mine, qkv_recv[...], qkv_own[...])


def self_attend_kernel(chunk, idx_ref, qkv_ref, segc_ref, segr_ref, table_ref, ctx_ref, prob_ref):
    rows, inner = ctx_ref.shape
    base = chunk * rows
    total = table_ref.shape[2]
    masks = []
    for at in range(0, rows, block):
        keys = base + at + block
        allowed = segc_ref[base + at : keys, :] == segr_ref[:, 0:keys]
        row = lax.broadcasted_iota(jnp.int32, (block, keys), 0) + (base + at)
        col = lax.broadcasted_iota(jnp.int32, (block, keys), 1)
        masks.append(jnp.where(allowed & (row >= col), 0.0, masked_score))
    for pair in range(0, inner, 2 * head_size):
        keys2 = qkv_ref[0 : base + rows, inner + pair : inner + pair + 128]
        values_e, values_o = even_odd(qkv_ref[0 : base + rows, 2 * inner + pair : 2 * inner + pair + 128])
        for number, at in enumerate(range(0, rows, block)):
            keys = base + at + block
            query_e, query_o = even_odd(qkv_ref[base + at : keys, pair : pair + 128])
            context = jnp.zeros((block, 128), f32)
            for head, query, values in (
                (pair // head_size, query_e, values_e),
                (pair // head_size + 1, query_o, values_o),
            ):
                scores = dot_rt(query, keys2[0:keys]) + table_ref[head, :, total - keys :].astype(f32)
                probs = softmax(scores + masks[number])
                prob_ref[head, at : at + block, 0:keys] = probs
                context = context + dot(probs, values[0:keys])
            ctx_ref[at : at + block, pair : pair + 128] = context.astype(bf16)


def weights_kernel(quarter_at, idx_ref, own_ref, beside_ref, own_core, beside_core, *outs):
    rows = outs[0].shape[0] // 4
    low, high = idx_ref[quarter_at], idx_ref[quarter_at + 1]
    for number, out_ref in enumerate(outs):
        part = slice(number * rows, (number + 1) * rows)
        for ref, at in (
            (own_ref, 2 * high + low),
            (beside_ref, 2 * (1 - high) + low),
            (own_core, 2 * high + (1 - low)),
            (beside_core, 2 * (1 - high) + (1 - low)),
        ):
            out_ref[pl.ds(pl.multiple_of(at * rows, 16), rows), :] = ref[part, :]


def memory_kernel(idx_ref, own_ref, recv_ref, wkv_ref, memory_ref, kv_ref):
    rows = own_ref.shape[0]
    inner = wkv_ref.shape[2]
    mine = idx_ref[0]
    memory_ref[pl.ds(pl.multiple_of(mine * rows, rows), rows), :] = own_ref[...]
    memory_ref[pl.ds(pl.multiple_of((1 - mine) * rows, rows), rows), :] = recv_ref[...]
    kv_ref[:, 0:inner] = dot(memory_ref[...], wkv_ref[0]).astype(bf16)
    kv_ref[:, inner : 2 * inner] = dot(memory_ref[...], wkv_ref[1]).astype(bf16)


def cross_forward_kernel(
    chunk,
    idx_ref,
    own_ref,
    recv_ref,
    before_ref,
    before_recv_ref,
    gain_ref,
    wo_ref,
    wo_pair_ref,
    wq_ref,
    kv_ref,
    segc_ref,
    segm_ref,
    after_ref,
    normed_ref,
    query_ref,
    ctx_ref,
    prob_ref,
):
    mine = idx_ref[0] == chunk
    rows = own_ref.shape[0]
    inner = wq_ref.shape[1]
    gain = gain_ref[1:2, :].astype(f32)
    after_ref[...] = dot(before_ref[...], wo_ref[...]) + dot(before_recv_ref[...], wo_pair_ref[...])
    for at in range(0, rows, block):
        part = slice(at, at + block)
        values = pick(mine, own_ref[part, :], recv_ref[part, :]).astype(f32) + after_ref[part, :]
        after_ref[part, :] = values
        normed_ref[part, :] = (values * rms_scale(values) * gain).astype(bf16)
    query_ref[...] = dot(normed_ref[...], wq_ref[...]).astype(bf16)
    masks = []
    for at in range(0, rows, block):
        allowed = segc_ref[chunk * rows + at : chunk * rows + at + block, :] == segm_ref[...]
        masks.append(jnp.where(allowed, 0.0, masked_score))
    for pair in range(0, inner, 2 * head_size):
        keys2 = kv_ref[:, pair : pair + 128]
        values_e, values_o = even_odd(kv_ref[:, inner + pair : inner + pair + 128])
        for number, at in enumerate(range(0, rows, block)):
            query_e, query_o = even_odd(query_ref[at : at + block, pair : pair + 128])
            context = jnp.zeros((block, 128), f32)
            for head, query, values in (
                (pair // head_size, query_e, values_e),
                (pair // head_size + 1, query_o, values_o),
            ):
                probs = softmax(dot_rt(query, keys2) + masks[number])
                prob_ref[head, at : at + block, :] = probs
                context = context + dot(probs, values)
            ctx_ref[at : at + block, pair : pair + 128] = context.astype(bf16)


def ffn_kernel(
    chunk,
    idx_ref,
    after_self_ref,
    before_ref,
    before_recv_ref,
    cot_ref,
    cot_recv_ref,
    gain_ref,
    wo_ref,
    wo_pair_ref,
    win_ref,
    wout_ref,
    after_ref,
    normed_ref,
    hidden_ref,
    grads_ref,
    back_ref,
    cot_scr,
):
    mine = idx_ref[0] == chunk
    rows = after_self_ref.shape[0]
    units = win_ref.shape[2]
    gain = gain_ref[2:3, :].astype(f32)
    after_ref[...] = dot(before_ref[...], wo_ref[...]) + dot(before_recv_ref[...], wo_pair_ref[...])
    for at in range(0, rows, block):
        part = slice(at, at + block)
        values = after_self_ref[part, :] + after_ref[part, :]
        after_ref[part, :] = values
        normed_ref[part, :] = (values * rms_scale(values) * gain).astype(bf16)
        cot_scr[part, :] = pick(mine, cot_ref[part, :], cot_recv_ref[part, :])
    wide = 256
    for at in range(0, units, wide):
        cols = slice(at, at + wide)
        gate = dot(normed_ref[...], win_ref[0, :, cols])
        upward = dot(normed_ref[...], win_ref[1, :, cols])
        grad = dot_rt(cot_scr[...], wout_ref[cols, :])
        square = gate * gate
        bend = jnp.tanh(gelu_root * gate * (1.0 + gelu_cubic * square))
        half = 0.5 * (1.0 + bend)
        gelu = gate * half
        slope = half + 0.5 * gelu_root * gate * (1.0 - bend * bend) * (1.0 + 3.0 * gelu_cubic * square)
        hidden_ref[:, cols] = (gelu * upward).astype(bf16)
        grads_ref[:, cols] = (grad * upward * slope).astype(bf16)
        grads_ref[:, units + at : units + at + wide] = (grad * gelu).astype(bf16)
    back_ref[...] = (
        dot_rt(grads_ref[:, 0:units], win_ref[0]) + dot_rt(grads_ref[:, units:], win_ref[1])
    ).astype(bf16)


def down_kernel(idx_ref, first_ref, second_ref, wout_ref, memory_ref, out_ref):
    rows = first_ref.shape[0]
    hidden = pick(idx_ref[0] == 0, second_ref[...], first_ref[...])
    out_ref[0:rows, :] = dot(hidden, wout_ref[...]).astype(bf16)
    out_ref[rows:, :] = memory_ref[...]


def final_kernel(idx_ref, hid_a, hid_b, after_a, after_b, recv_ref, wout_ref, out_ref):
    mine = idx_ref[0] == 0
    own = dot(pick(mine, hid_a[...], hid_b[...]), wout_ref[...])
    out_ref[...] = (pick(mine, after_a[...], after_b[...]) + (own + recv_ref[0 : own.shape[0], :].astype(f32))).astype(bf16)


def turn_rows(values, place_ref, order, at):
    turned = jnp.transpose(values)
    size = turned.shape[0] // len(order)
    for number, position in enumerate(order):
        place_ref[position * size : (position + 1) * size, at : at + values.shape[0]] = turned[
            number * size : (number + 1) * size
        ]


def write_grads(bit_ref, turned_ref, right, send_ref, keep_ref, at):
    rows = send_ref.shape[0]
    mine = bit_ref[1]
    cols = slice(at, at + right.shape[1])
    keep_ref[:, cols] = dot(turned_ref[pl.ds(pl.multiple_of(mine * rows, rows), rows), :], right).astype(bf16)
    send_ref[:, cols] = dot(turned_ref[pl.ds(pl.multiple_of((1 - mine) * rows, rows), rows), :], right).astype(bf16)


def ffn_grads_kernel(
    orders,
    idx_ref,
    normed_a,
    normed_b,
    grads_a,
    grads_b,
    hidden_a,
    hidden_b,
    cot_ref,
    cot_recv_ref,
    send_first,
    keep_first,
    send_second,
    keep_second,
    turned,
    turned_two,
    turned_three,
):
    rows = normed_a.shape[0]
    mine = idx_ref[0] == 0
    units = hidden_a.shape[1]
    cut = send_first.shape[1]
    turn_rows(normed_a[...], turned, orders[0], 0)
    turn_rows(normed_b[...], turned, orders[0], rows)
    turn_rows(normed_a[...], turned_two, orders[1], 0)
    turn_rows(normed_b[...], turned_two, orders[1], rows)
    turn_rows(pick(mine, cot_ref[...], cot_recv_ref[...]), turned_three, orders[1], 0)
    turn_rows(pick(mine, cot_recv_ref[...], cot_ref[...]), turned_three, orders[1], rows)
    both = jnp.concatenate([grads_a[...], grads_b[...]], axis=0)
    write_grads(idx_ref, turned, both[:, :cut], send_first, keep_first, 0)
    write_grads(idx_ref, turned_two, both[:, cut:], send_second, keep_second, 0)
    hidden = jnp.concatenate([hidden_a[...], hidden_b[...]], axis=0)
    write_grads(idx_ref, turned_three, hidden, send_second, keep_second, 2 * units - cut)


def attend_back(query_rows, prob_ref, score_ref, grad_ref, key_of, value_of, dq_ref, inner, reach):
    for pair in range(0, inner, 2 * head_size):
        keys_e, keys_o = even_odd(key_of(pair))
        values2 = value_of(pair)
        for at in range(0, query_rows, block):
            keys = reach(at)
            grad_e, grad_o = even_odd(grad_ref[at : at + block, pair : pair + 128])
            total = jnp.zeros((block, 128), f32)
            for head, grad, key in (
                (pair // head_size, grad_e, keys_e),
                (pair // head_size + 1, grad_o, keys_o),
            ):
                probs = prob_ref[head, at : at + block, 0:keys].astype(f32)
                grad_probs = dot_rt(grad, values2[0:keys])
                delta = jnp.sum(probs * grad_probs, axis=-1, keepdims=True) / jnp.sum(
                    probs, axis=-1, keepdims=True
                )
                scores = (probs * (grad_probs - delta)).astype(bf16)
                score_ref[head, at : at + block, 0:keys] = scores
                total = total + dot(scores, key[0:keys])
            dq_ref[at : at + block, pair : pair + 128] = total.astype(bf16)


def cross_back_kernel(
    chunk,
    idx_ref,
    after_ref,
    back_ref,
    back_recv_ref,
    cot_ref,
    cot_recv_ref,
    gain_ref,
    wo_ref,
    wq_ref,
    kv_ref,
    prob_ref,
    grad_ref,
    sent_ref,
    dctx_ref,
    dq_ref,
    score_ref,
    out_ref,
    gain_out_ref,
):
    mine = idx_ref[0] == chunk
    rows = after_ref.shape[0]
    inner = wq_ref.shape[1]
    gain = gain_ref[2:3, :].astype(f32)
    gain_total = jnp.zeros((8, gain.shape[1]), f32)
    for at in range(0, rows, block):
        part = slice(at, at + block)
        incoming = back_ref[part, :].astype(f32) + back_recv_ref[part, :].astype(f32)
        back, gain_terms = norm_back(after_ref[part, :], gain, incoming)
        total = pick(mine, cot_ref[part, :], cot_recv_ref[part, :]).astype(f32) + back
        grad_ref[part, :] = total
        sent_ref[part, :] = total.astype(bf16)
        gain_total = gain_total + jnp.sum(gain_terms.reshape(block // 8, 8, -1), axis=0)
    gain_out_ref[...] = pick(mine, gain_total, jnp.zeros_like(gain_total))
    dctx_ref[...] = dot_rt(sent_ref[...], wo_ref[...]).astype(bf16)
    attend_back(
        rows,
        prob_ref,
        score_ref,
        dctx_ref,
        lambda pair: kv_ref[:, pair : pair + 128],
        lambda pair: kv_ref[:, inner + pair : inner + pair + 128],
        dq_ref,
        inner,
        lambda at: kv_ref.shape[0],
    )
    out_ref[...] = dot_rt(dq_ref[...], wq_ref[...]).astype(bf16)


def cross_grads_kernel(
    order,
    idx_ref,
    normed_a,
    normed_b,
    dq_a,
    dq_b,
    query_a,
    query_b,
    score_a,
    score_b,
    prob_a,
    prob_b,
    dctx_a,
    dctx_b,
    ctx_a,
    ctx_b,
    sent_a,
    sent_b,
    memory_ref,
    wkv_ref,
    send_ref,
    keep_ref,
    memory_send_ref,
    memory_keep_ref,
    turned,
    turned_two,
    turned_three,
    dkv,
):
    rows = normed_a.shape[0]
    inner = dq_a.shape[1]
    for pair in range(0, inner, 2 * head_size):
        keys = jnp.zeros((dkv.shape[0], 128), f32)
        values = jnp.zeros((dkv.shape[0], 128), f32)
        for score, prob, query, dctx in ((score_a, prob_a, query_a, dctx_a), (score_b, prob_b, query_b, dctx_b)):
            cols = slice(pair, pair + 128)
            for number, (query_half, grad_half) in enumerate(
                zip(even_odd(query[:, cols]), even_odd(dctx[:, cols]), strict=True)
            ):
                head = pair // head_size + number
                keys = keys + dot_lt(score[head], query_half)
                values = values + dot_lt(prob[head], grad_half)
        dkv[:, pair : pair + 128] = keys.astype(bf16)
        dkv[:, inner + pair : inner + pair + 128] = values.astype(bf16)
    mine = idx_ref[0]
    other = pl.ds(pl.multiple_of((1 - mine) * rows, rows), rows)
    own = pl.ds(pl.multiple_of(mine * rows, rows), rows)
    memory_send_ref[...] = (
        dot_rt(dkv[other, 0:inner], wkv_ref[0]) + dot_rt(dkv[other, inner:], wkv_ref[1])
    ).astype(bf16)
    memory_keep_ref[...] = dot_rt(dkv[own, 0:inner], wkv_ref[0]) + dot_rt(dkv[own, inner:], wkv_ref[1])
    turn_rows(normed_a[...], turned, order, 0)
    turn_rows(normed_b[...], turned, order, rows)
    both = jnp.concatenate([dq_a[...], dq_b[...]], axis=0)
    write_grads(idx_ref, turned, both, send_ref, keep_ref, 0)
    turn_rows(memory_ref[...], turned_two, order, 0)
    write_grads(idx_ref, turned_two, dkv[...], send_ref, keep_ref, inner)
    turn_rows(sent_a[...], turned_three, order, 0)
    turn_rows(sent_b[...], turned_three, order, rows)
    both = jnp.concatenate([ctx_a[...], ctx_b[...]], axis=0)
    write_grads(idx_ref, turned_three, both, send_ref, keep_ref, 3 * inner)


def self_back_kernel(
    chunk,
    idx_ref,
    after_ref,
    back_ref,
    back_recv_ref,
    cross_ref,
    gain_ref,
    wo_ref,
    qkv_ref,
    prob_ref,
    grad_ref,
    sent_ref,
    dctx_ref,
    dq_ref,
    score_ref,
    gain_out_ref,
):
    mine = idx_ref[0] == chunk
    rows = after_ref.shape[0]
    inner = wo_ref.shape[0]
    gain = gain_ref[1:2, :].astype(f32)
    gain_total = jnp.zeros((8, gain.shape[1]), f32)
    for at in range(0, rows, block):
        part = slice(at, at + block)
        incoming = back_ref[part, :].astype(f32) + back_recv_ref[part, :].astype(f32)
        back, gain_terms = norm_back(after_ref[part, :], gain, incoming)
        total = cross_ref[part, :] + back
        grad_ref[part, :] = total
        sent_ref[part, :] = total.astype(bf16)
        gain_total = gain_total + jnp.sum(gain_terms.reshape(block // 8, 8, -1), axis=0)
    gain_out_ref[...] = pick(mine, gain_total, jnp.zeros_like(gain_total))
    dctx_ref[...] = dot_rt(sent_ref[...], wo_ref[...]).astype(bf16)
    end = (chunk + 1) * rows
    attend_back(
        rows,
        prob_ref,
        score_ref,
        dctx_ref,
        lambda pair: qkv_ref[0:end, inner + pair : inner + pair + 128],
        lambda pair: qkv_ref[0:end, 2 * inner + pair : 2 * inner + pair + 128],
        dq_ref,
        inner,
        lambda at: chunk * rows + at + block,
    )


def self_grads_kernel(
    order,
    idx_ref,
    normed_a,
    normed_b,
    dq_a,
    dq_b,
    qkv_ref,
    score_a,
    score_b,
    prob_a,
    prob_b,
    dctx_a,
    dctx_b,
    ctx_a,
    ctx_b,
    sent_a,
    sent_b,
    send_ref,
    keep_ref,
    dqkv_ref,
    turned,
    turned_two,
):
    rows = normed_a.shape[0]
    inner = dq_a.shape[1]
    for pair in range(0, inner, 2 * head_size):
        for at in range(0, 2 * rows, block):
            keys = jnp.zeros((block, 128), f32)
            values = jnp.zeros((block, 128), f32)
            cols = slice(pair, pair + 128)
            span = slice(at, at + block)
            for base, score, prob, dctx in ((0, score_a, prob_a, dctx_a), (rows, score_b, prob_b, dctx_b)):
                if at >= base + rows:
                    continue
                low = max(at - base, 0)
                for number, (query_half, grad_half) in enumerate(
                    zip(even_odd(qkv_ref[base + low : base + rows, cols]), even_odd(dctx[low:rows, cols]), strict=True)
                ):
                    head = pair // head_size + number
                    keys = keys + dot_lt(score[head, low:rows, span], query_half)
                    values = values + dot_lt(prob[head, low:rows, span], grad_half)
            dqkv_ref[span, inner + pair : inner + pair + 128] = keys.astype(bf16)
            dqkv_ref[span, 2 * inner + pair : 2 * inner + pair + 128] = values.astype(bf16)
    dqkv_ref[0:rows, 0:inner] = dq_a[...]
    dqkv_ref[rows : 2 * rows, 0:inner] = dq_b[...]
    turn_rows(normed_a[...], turned, order, 0)
    turn_rows(normed_b[...], turned, order, rows)
    write_grads(idx_ref, turned, dqkv_ref[...], send_ref, keep_ref, 0)
    turn_rows(sent_a[...], turned_two, order, 0)
    turn_rows(sent_b[...], turned_two, order, rows)
    both = jnp.concatenate([ctx_a[...], ctx_b[...]], axis=0)
    write_grads(idx_ref, turned_two, both, send_ref, keep_ref, 3 * inner)


def diagonals(values):
    wide = jnp.concatenate([values, jnp.zeros_like(values)], axis=1)
    total = wide[0:8]
    for at in range(8, block, 8):
        total = total + pltpu.roll(wide[at : at + 8], 2 * block - at, 1)
    row = lax.broadcasted_iota(jnp.int32, total.shape, 0)
    for bit in (1, 2, 4):
        total = jnp.where((row & bit) != 0, pltpu.roll(total, 2 * block - bit, 1), total)
    return jnp.sum(total, axis=0, keepdims=True)


def self_input_kernel(
    idx_ref,
    dqkv_ref,
    own_ref,
    recv_ref,
    wq_ref,
    wkv_ref,
    score_a,
    score_b,
    hot_ref,
    two_a,
    two_b,
    three_a,
    three_b,
    send_ref,
    keep_ref,
    small_ref,
    line,
):
    rows = own_ref.shape[0]
    inner = wq_ref.shape[1]
    mine = idx_ref[0]
    gain_total = jnp.zeros((8, own_ref.shape[1]), f32)
    for which, values_ref in ((1 - mine, recv_ref), (mine, own_ref)):
        span = pl.ds(pl.multiple_of(which * rows, rows), rows)
        grad = (
            dot_rt(dqkv_ref[span, 0:inner], wq_ref[...])
            + dot_rt(dqkv_ref[span, inner : 2 * inner], wkv_ref[0])
            + dot_rt(dqkv_ref[span, 2 * inner :], wkv_ref[1])
        )
        if values_ref is recv_ref:
            send_ref[0:rows, :] = grad.astype(bf16)
        else:
            keep_ref[...] = grad
        values = values_ref[...].astype(f32)
        terms = grad * values * rms_scale(values)
        gain_total = gain_total + jnp.sum(terms.reshape(rows // 8, 8, -1), axis=0)
    heads = score_a.shape[0]
    count = 2 * rows // block
    line[...] = jnp.zeros_like(line)
    for head in range(heads):
        for step in range(count):
            total = jnp.zeros((block, block), f32)
            for at in range(step, count):
                col = (at - step) * block
                score = score_a if at * block < rows else score_b
                row = at * block % rows
                total = total + score[head, row : row + block, col : col + block].astype(f32)
            line[head : head + 1, step * 2 * block : (step + 1) * 2 * block] = diagonals(total)
    bias = lax.dot_general(
        line[...], hot_ref[...], (((1,), (1,)), ((), ())), precision=lax.Precision.HIGHEST, preferred_element_type=f32
    )
    buckets = hot_ref.shape[0]
    small_ref[...] = jnp.zeros_like(small_ref)
    small_ref[0:1, :] = jnp.sum(gain_total, axis=0, keepdims=True)
    small_ref[1:2, :] = jnp.sum(two_a[...] + two_b[...], axis=0, keepdims=True)
    small_ref[2:3, :] = jnp.sum(three_a[...] + three_b[...], axis=0, keepdims=True)
    small_ref[8:16, 0:buckets] = pick(mine == 0, bias, jnp.zeros_like(bias))
    small_ref[8:16, 128 : 128 + buckets] = pick(mine == 1, bias, jnp.zeros_like(bias))
    high = small_ref[...].astype(bf16)
    send_ref[rows : rows + 16, :] = high
    send_ref[rows + 16 :, :] = (small_ref[...] - high.astype(f32)).astype(bf16)


def input_grad_kernel(idx_ref, own_ref, keep_ref, recv_ref, grad_a, grad_b, gain_ref, out_ref):
    mine = idx_ref[0] == 0
    gain = gain_ref[0:1, :].astype(f32)
    for at in range(0, own_ref.shape[0], block):
        part = slice(at, at + block)
        incoming = keep_ref[part, :] + recv_ref[part, :].astype(f32)
        back, _ = norm_back(own_ref[part, :].astype(f32), gain, incoming)
        out_ref[part, :] = pick(mine, grad_a[part, :], grad_b[part, :]) + back


def halve_kernel(slot, idx_ref, keep_ref, got_ref, send_out, keep_out):
    rows = send_out.shape[0]
    mine = idx_ref[slot]
    other = pl.ds(pl.multiple_of((1 - mine) * rows, 16), rows)
    own = pl.ds(pl.multiple_of(mine * rows, 16), rows)
    send_out[...] = (keep_ref[other, :].astype(f32) + got_ref[other, :].astype(f32)).astype(bf16)
    keep_out[...] = (keep_ref[own, :].astype(f32) + got_ref[own, :].astype(f32)).astype(bf16)


def split_small(values):
    high = values.astype(bf16)
    return jnp.concatenate([high, (values - high.astype(f32)).astype(bf16)], axis=1)


def join_small(parts):
    width = parts.shape[1] // 2
    return parts[:, :width].astype(f32) + parts[:, width:].astype(f32)


def add_kernel(idx_ref, first_ref, second_ref, out_ref):
    out_ref[...] = split_small(join_small(first_ref[...]) + join_small(second_ref[...]))


def add_first_kernel(idx_ref, own_ref, got_ref, out_ref):
    rows = own_ref.shape[0]
    at = got_ref.shape[0] - 2 * rows
    got = got_ref[at : at + rows, :].astype(f32) + got_ref[at + rows :, :].astype(f32)
    out_ref[...] = split_small(join_small(split_small(own_ref[...])) + got)


def halve_small_kernel(slot, has_small, idx_ref, keep_ref, got_ref, *refs):
    send_out, keep_out = refs[-2:]
    count = 16
    rows = send_out.shape[0] - count
    mine = idx_ref[slot]
    other = pl.ds(pl.multiple_of((1 - mine) * rows, 16), rows)
    own = pl.ds(pl.multiple_of(mine * rows, 16), rows)
    send_out[0:rows, :] = (keep_ref[other, :].astype(f32) + got_ref[other, :].astype(f32)).astype(bf16)
    keep_out[0:rows, :] = (keep_ref[own, :].astype(f32) + got_ref[own, :].astype(f32)).astype(bf16)
    if has_small:
        small = split_small(join_small(keep_ref[2 * rows :, :]) + join_small(got_ref[2 * rows :, :]))
    else:
        small = split_small(join_small(refs[0][...]) + join_small(refs[1][...]))
    send_out[rows:, :] = small
    keep_out[rows:, :] = small


def finish_small_kernel(idx_ref, keep_ref, got_ref, out_ref):
    rows = keep_ref.shape[0] - 16
    out_ref[...] = split_small(join_small(keep_ref[rows:, :]) + join_small(got_ref[rows:, :]))


def last_small_kernel(idx_ref, *refs):
    *parts, gain_out, bias_out = refs
    at = parts[0].shape[0] - 16
    total = join_small(parts[0][at:, :])
    for part in parts[1:]:
        total = total + join_small(part[at:, :])
    heads, buckets = bias_out.shape[0] // 2, bias_out.shape[1]
    gain_out[...] = total[0:3, :]
    bias_out[0:heads, :] = total[8 : 8 + heads, 0:buckets]
    bias_out[heads:, :] = total[8 : 8 + heads, 128 : 128 + buckets]


def memory_add_kernel(idx_ref, keep_ref, got_ref, out_ref):
    out_ref[...] = keep_ref[...] + got_ref[keep_ref.shape[0] :, :].astype(f32)


def finish_kernel(idx_ref, *refs):
    count = next(at for at, ref in enumerate(refs) if ref.dtype == f32)
    left = refs[-1].shape[0]
    starts = [0]
    for keep_ref in refs[0:count:2]:
        starts.append(starts[-1] + keep_ref.shape[1])

    def pieces(low, high):
        for number, start in enumerate(starts[:-1]):
            at, end = max(low, start), min(high, starts[number + 1])
            if at < end:
                cols = slice(at - start, end - start)
                keep = refs[2 * number][0:left, cols].astype(f32)
                yield at - low, end - low, keep + refs[2 * number + 1][0:left, cols].astype(f32)

    at = 0
    for out in refs[count:]:
        for values in [out] if len(out.shape) == 2 else [out.at[n] for n in range(out.shape[0])]:
            for low, high, total in pieces(at, at + values.shape[1]):
                values[:, low:high] = total
            at += values.shape[1]


def flip(values, bit, size):
    return lax.ppermute(settled(values), "dp", [(at, at ^ bit) for at in range(size)])


def swap(values):
    return lax.ppermute(settled(values), "mp", [(0, 1), (1, 0)])


def halving_plans(size, width):
    bits = [1 << at for at in range(size.bit_length() - 1)]
    if (width // size) % 16:
        return (bits[::-1], [0]), (bits[::-1], [0])
    plans = []
    for steps in (bits, bits[:1] + bits[2:] + bits[1:2]):
        order = [sum(((at // bit) % 2) * (size >> (step + 1)) for step, bit in enumerate(steps)) for at in range(size)]
        plans.append((steps, order))
    return plans


def body(
    hidden_in,
    memory,
    cotangent,
    self_query,
    self_keyval,
    self_output,
    cross_query,
    cross_keyval,
    cross_output,
    ffn_input,
    ffn_output,
    norm_gains,
    rel_bias,
    dec_segments,
    mem_segments,
    rel_bucket,
):
    dp = lax.axis_size("dp")
    position = lax.axis_index("dp")
    half = lax.axis_index("mp")
    own = hidden_in[0]
    rows, width = own.shape
    length = 2 * rows
    buckets, heads = rel_bias.shape
    inner = self_query.shape[1]
    units = ffn_output.shape[0]
    memory_own = memory[0]
    cot = cotangent[0]
    (steps, order), (ffn_steps, ffn_order) = halving_plans(dp, width)
    quarter = [position % 2, (position // 2) % 2]
    idx = jnp.stack([half] + [(position // bit) % 2 for bit in steps] + quarter).astype(jnp.int32)
    order_token = [idx]

    def run(group):
        if not group.stages:
            return []
        values = group.call(order_token[0])
        order_token[0] = lax.optimization_barrier((idx, values[-1]))[0]
        return values

    def single(name, kernel, outs, args, **options):
        group = Group(name)
        group.add(kernel, outs, args, **options)
        return run(group)

    places = steps

    class Scatter:
        def __init__(self, steps, send, keep):
            self.steps, self.keep, self.at, self.extra = steps, keep, 0, 0
            self.got = flip(send, self.steps[0], dp)

        def halve(self, group, *small):
            self.at += 1
            keep = settled(self.keep)
            cut, bit = (keep.shape[0] - self.extra) // 2, self.steps[self.at]
            if small or self.extra:
                kernel = functools.partial(halve_small_kernel, 1 + places.index(bit), self.extra > 0)
                self.extra = 16
                shape = ((cut + 16, keep.shape[1]), bf16)
                self.out, self.keep = group.add(kernel, [shape] * 2, [keep, self.got, *small])
            elif cut % 16 == 0:
                kernel = functools.partial(halve_kernel, 1 + places.index(bit))
                self.out, self.keep = group.add(kernel, [((cut, keep.shape[1]), bf16)] * 2, [keep, self.got])
            else:
                mine = ((position // bit) % 2) * cut
                take = functools.partial(lax.dynamic_slice_in_dim, slice_size=cut, axis=0)
                total = [(take(keep, at).astype(f32) + take(self.got, at).astype(f32)) for at in (cut - mine, mine)]
                self.out, self.keep = [values.astype(bf16) for values in total]

        def send(self):
            self.got = flip(self.out, self.steps[self.at], dp)

        def step(self, name, *small):
            group = Group(name)
            self.halve(group, *small)
            run(group)
            self.send()

        def total(self):
            while self.at < len(self.steps) - 1:
                self.step("halve")
            return settled(self.keep), self.got

    def together(name, *sums):
        group = Group(name)
        for item in sums:
            item.halve(group)
        run(group)
        for item in sums:
            item.send()

    def finish(group, sums, widths):
        left = width // dp
        shapes = [((left, w), f32) if n == 1 else ((n, left, w), f32) for n, w in widths]
        if left % 16 == 0:
            return group.add(finish_kernel, shapes, sums)
        total = jnp.concatenate([k.astype(f32) + g.astype(f32) for k, g in zip(sums[::2], sums[1::2], strict=True)], axis=1)
        outs, at = [], 0
        for n, w in widths:
            outs.append(total[:, at : at + n * w])
            at += n * w
        return [o if n == 1 else jnp.stack(jnp.split(o, n, axis=1)) for o, (n, w) in zip(outs, widths, strict=True)]

    recv = swap(own)
    piece = inner // 4
    spot = (position % 4) * piece
    cut = functools.partial(lax.dynamic_slice_in_dim, start_index=spot, slice_size=piece, axis=0)
    weight_own = swap(jnp.concatenate([cut(self_output), cut(cross_output)]))

    def after(values, made):
        return lax.optimization_barrier((values, settled(made)))[0]


    count = length // block
    lane = np.arange(2 * block)
    spot = np.arange(count)[:, None] * block + np.where(lane < block, -lane, 2 * block - lane)[None]
    spot = np.clip(spot, 0, length - 1).reshape(-1).astype(np.int32)
    firsts = jnp.sum((rel_bucket[None, :] < jnp.arange(buckets + 1, dtype=jnp.int32)[:, None]).astype(jnp.int32), axis=1)
    hot = ((spot[None] >= firsts[:-1, None]) & (spot[None] < firsts[1:, None])).astype(f32)
    line = jnp.einsum("bh,bs->hs", rel_bias, hot.astype(bf16), preferred_element_type=f32)
    line = jnp.pad(line, ((0, 8 - heads), (0, 0)))
    seg_col = dec_segments.reshape(length, 1)
    group = Group("self_project")
    (table,) = group.add(bias_kernel, [((heads, block, length), bf16)], [line])
    projected = [((rows, width), bf16), ((rows, 3 * inner), bf16)]
    weights = [norm_gains, self_query, self_keyval]
    normed_own, qkv_own = group.add(self_project_kernel, projected, [own] + weights)
    run(group)
    memory_recv = swap(after(memory_own, normed_own))

    def self_attend(group, chunk):
        return group.add(
            functools.partial(self_attend_kernel, chunk),
            [((rows, inner), bf16), ((heads, rows, (chunk + 1) * rows), bf16)],
            [qkv, seg_col, dec_segments, table],
        )

    group = Group("self_forward_a")
    normed_recv, qkv_recv = group.add(self_project_kernel, projected, [recv] + weights)
    normed_one_a, normed_one_b, qkv = group.add(
        self_order_kernel,
        [((rows, width), bf16), ((rows, width), bf16), ((length, 3 * inner), bf16)],
        [normed_own, qkv_own, normed_recv, qkv_recv],
    )
    ctx_one_a, prob_one_a = self_attend(group, 0)
    run(group)
    ctx_one_recv_a = swap(ctx_one_a)
    weight_beside = flip(after(weight_own, ctx_one_a), 2, dp)
    weight_core = flip(after(weight_own, ctx_one_a), 1, dp)
    group = Group("self_forward_b")
    ctx_one_b, prob_one_b = self_attend(group, 1)
    run(group)
    ctx_one_recv_b = swap(ctx_one_b)
    cot_recv = swap(after(cot, ctx_one_b))

    group = Group("memory_keyval")
    memory_all, kv = group.add(
        memory_kernel,
        [((length, width), bf16), ((length, 2 * inner), bf16)],
        [memory_own, memory_recv, cross_keyval],
    )
    run(group)
    weight_beside_core = flip(after(weight_beside, ctx_one_b), 1, dp)
    def cross_forward(group, chunk, before, before_recv):
        return group.add(
            functools.partial(cross_forward_kernel, chunk),
            [
                ((rows, width), f32),
                ((rows, width), bf16),
                ((rows, inner), bf16),
                ((rows, inner), bf16),
                ((heads, rows, length), bf16),
            ],
            [
                own,
                recv,
                before,
                before_recv,
                norm_gains,
                self_output,
                self_output_pair,
                cross_query,
                kv,
                seg_col,
                mem_segments,
            ],
        )

    group = Group("cross_forward_a")
    self_output_pair, cross_output_pair = group.add(
        functools.partial(weights_kernel, len(steps) + 1),
        [((inner, width), bf16), ((inner, width), bf16)],
        [weight_own, weight_beside, weight_core, weight_beside_core],
    )
    after_self_a, normed_two_a, query_two_a, ctx_two_a, prob_two_a = cross_forward(group, 0, ctx_one_a, ctx_one_recv_a)
    run(group)
    ctx_two_recv_a = swap(ctx_two_a)
    group = Group("cross_forward_b")
    after_self_b, normed_two_b, query_two_b, ctx_two_b, prob_two_b = cross_forward(group, 1, ctx_one_b, ctx_one_recv_b)
    run(group)
    ctx_two_recv_b = swap(ctx_two_b)

    def ffn(group, chunk, after_self, before, before_recv):
        return group.add(
            functools.partial(ffn_kernel, chunk),
            [
                ((rows, width), f32),
                ((rows, width), bf16),
                ((rows, units), bf16),
                ((rows, 2 * units), bf16),
                ((rows, width), bf16),
            ],
            [
                after_self,
                before,
                before_recv,
                cot,
                cot_recv,
                norm_gains,
                cross_output,
                cross_output_pair,
                ffn_input,
                ffn_output,
            ],
            scratch=[pltpu.VMEM((rows, width), bf16)],
        )

    group = Group("ffn_a")
    after_cross_a, normed_three_a, hidden_a, gate_grads_a, back_three_a = ffn(
        group, 0, after_self_a, ctx_two_a, ctx_two_recv_a
    )
    run(group)
    back_three_recv_a = swap(back_three_a)
    group = Group("ffn_b")
    after_cross_b, normed_three_b, hidden_b, gate_grads_b, back_three_b = ffn(
        group, 1, after_self_b, ctx_two_b, ctx_two_recv_b
    )
    first_send, first_keep, second_send, second_keep = group.add(
        functools.partial(ffn_grads_kernel, [order, ffn_order]),
        [((width // 2, 3 * units // 2), bf16)] * 4,
        [
            normed_three_a,
            normed_three_b,
            gate_grads_a,
            gate_grads_b,
            hidden_a,
            hidden_b,
            cot,
            cot_recv,
        ],
        scratch=[pltpu.VMEM((width, length), bf16)] * 3,
        flops=2 * length * width * units * 3,
    )
    run(group)
    back_three_recv_b = swap(back_three_b)
    ffn_sums = [Scatter(steps, first_send, first_keep), Scatter(ffn_steps, second_send, second_keep)]

    def cross_back(group, chunk, after, back, back_recv, prob):
        return group.add(
            functools.partial(cross_back_kernel, chunk),
            [
                ((rows, width), f32),
                ((rows, width), bf16),
                ((rows, inner), bf16),
                ((rows, inner), bf16),
                ((heads, rows, length), bf16),
                ((rows, width), bf16),
                ((8, width), f32),
            ],
            [after, back, back_recv, cot, cot_recv, norm_gains, cross_output, cross_query, kv, prob],
            flops=2 * rows * width * inner * 4,
        )

    group = Group("cross_back_a")
    grad_cross_a, sent_two_a, dctx_two_a, dq_two_a, score_two_a, back_two_a, three_a = cross_back(
        group, 0, after_cross_a, back_three_a, back_three_recv_a, prob_two_a
    )
    run(group)
    back_two_recv_a = swap(back_two_a)
    together("halve_ffn_one", *ffn_sums)
    group = Group("cross_back_b")
    grad_cross_b, sent_two_b, dctx_two_b, dq_two_b, score_two_b, back_two_b, three_b = cross_back(
        group, 1, after_cross_b, back_three_b, back_three_recv_b, prob_two_b
    )
    run(group)
    back_two_recv_b = swap(back_two_b)
    group = Group("self_back_a")
    cross_send, cross_keep, memory_send, memory_keep = group.add(
        functools.partial(cross_grads_kernel, order),
        [
            ((width // 2, 4 * inner), bf16),
            ((width // 2, 4 * inner), bf16),
            ((rows, width), bf16),
            ((rows, width), f32),
        ],
        [
            normed_two_a,
            normed_two_b,
            dq_two_a,
            dq_two_b,
            query_two_a,
            query_two_b,
            score_two_a,
            score_two_b,
            prob_two_a,
            prob_two_b,
            dctx_two_a,
            dctx_two_b,
            ctx_two_a,
            ctx_two_b,
            sent_two_a,
            sent_two_b,
            memory_all,
            cross_keyval,
        ],
        scratch=[pltpu.VMEM((width, length), bf16)] * 3 + [pltpu.VMEM((length, 2 * inner), bf16)],
        flops=2 * length * width * inner * 8,
    )

    def self_back(group, chunk, after, back, back_recv, grad_cross, prob):
        end = (chunk + 1) * rows
        return group.add(
            functools.partial(self_back_kernel, chunk),
            [
                ((rows, width), f32),
                ((rows, width), bf16),
                ((rows, inner), bf16),
                ((rows, inner), bf16),
                ((heads, rows, end), bf16),
                ((8, width), f32),
            ],
            [after, back, back_recv, grad_cross, norm_gains, self_output, qkv, prob],
            flops=2 * rows * width * inner * 3,
        )

    grad_self_a, sent_one_a, dctx_one_a, dq_one_a, score_one_a, two_a = self_back(
        group, 0, after_self_a, back_two_a, back_two_recv_a, grad_cross_a, prob_one_a
    )
    run(group)
    cross_sum = Scatter(steps, cross_send, cross_keep)
    group = Group("self_back_b")
    grad_self_b, sent_one_b, dctx_one_b, dq_one_b, score_one_b, two_b = self_back(
        group, 1, after_self_b, back_two_b, back_two_recv_b, grad_cross_b, prob_one_b
    )

    self_send, self_keep, dqkv = group.add(
        functools.partial(self_grads_kernel, order),
        [((width // 2, 4 * inner), bf16), ((width // 2, 4 * inner), bf16), ((length, 3 * inner), bf16)],
        [
            normed_one_a,
            normed_one_b,
            dq_one_a,
            dq_one_b,
            qkv,
            score_one_a,
            score_one_b,
            prob_one_a,
            prob_one_b,
            dctx_one_a,
            dctx_one_b,
            ctx_one_a,
            ctx_one_b,
            sent_one_a,
            sent_one_b,
        ],
        scratch=[pltpu.VMEM((width, length), bf16)] * 2,
        flops=2 * length * width * inner * 6,
    )
    run(group)
    self_sum = Scatter(steps, self_send, self_keep)
    together("halve_ffn_two", *ffn_sums)
    cross_sum.step("halve_cross_one")
    group = Group("self_input")
    back_one_send, back_one_keep, small_part = group.add(
        self_input_kernel,
        [((rows + 32, width), bf16), ((rows, width), f32), ((16, width), f32)],
        [
            dqkv,
            own,
            recv,
            self_query,
            self_keyval,
            score_one_a,
            score_one_b,
            hot,
            two_a,
            two_b,
            three_a,
            three_b,
        ],
        scratch=[pltpu.VMEM((8, 2 * length), f32)],
    )
    run(group)
    back_one_recv = swap(back_one_send)
    self_sum.step("halve_self_one")
    cross_sum.step("halve_cross_two")
    group = Group("input_grad")
    (grad_input,) = group.add(
        input_grad_kernel,
        [((rows, width), f32)],
        [own, back_one_keep, back_one_recv, grad_self_a, grad_self_b, norm_gains],
    )
    pair = ((16, 2 * width), bf16)
    (small,) = group.add(add_first_kernel, [pair], [small_part, back_one_recv])
    run(group)
    small_got = flip(small, 1, dp)
    together("halve_ffn_three", *ffn_sums)
    (small,) = single("small_add", add_kernel, [pair], [settled(small), small_got])
    small_got = flip(small, 2, dp)
    cross_sum.step("halve_cross_three")
    carried = steps == [1, 2, 4, 8] and 2 * width == 4 * inner
    if carried:
        group = Group("halve_self_two")
        self_sum.halve(group, small, small_got)
    else:
        for bit in sorted(steps)[2:]:
            (small,) = single("small_add", add_kernel, [pair], [settled(small), small_got])
            small_got = flip(small, bit, dp)
        (small,) = single("small_add", add_kernel, [pair], [small, small_got])
        group = Group("halve_self_two")
        self_sum.halve(group)
    (out_send,) = group.add(down_kernel, [((length, width), bf16)], [hidden_a, hidden_b, ffn_output, memory_send])
    run(group)
    self_sum.send()
    out_recv = swap(out_send)
    self_sum.step("halve_self_three")
    widths = [(1, inner), (2, inner), (1, inner)]
    group = Group("final")
    (output,) = group.add(
        final_kernel,
        [((rows, width), bf16)],
        [hidden_a, hidden_b, after_cross_a, after_cross_b, out_recv, ffn_output],
    )
    (grad_memory,) = group.add(memory_add_kernel, [((rows, width), f32)], [memory_keep, out_recv])
    grads_cross = finish(group, cross_sum.total(), widths)
    grads_ffn = finish(group, [part for item in ffn_sums for part in item.total()], [(2, units), (1, units)])
    run(group)
    group = Group("finish_self")
    rest = self_sum.total()
    grads_self = finish(group, rest, widths)
    small_outs = [((3, width), f32), ((2 * heads, buckets), f32)]
    gains, bias = group.add(last_small_kernel, small_outs, [*rest] if carried else [small])
    run(group)
    grads_ffn, grads_cross, grads_self = [[settled(g) for g in grads] for grads in (grads_ffn, grads_cross, grads_self)]
    return (
        settled(output)[None],
        settled(grad_input)[None],
        settled(grad_memory)[None],
        *grads_self[:-1],
        grads_self[-1].T,
        *grads_cross[:-1],
        grads_cross[-1].T,
        *grads_ffn[:-1],
        grads_ffn[-1].T,
        settled(gains),
        settled(bias).T,
    )


def solution(mesh):
    in_specs = (
        P("dp", "mp", None),
        P("dp", "mp", None),
        P("dp", "mp", None),
        P(None, "mp"),
        P(None, None, "mp"),
        P("mp", None),
        P(None, "mp"),
        P(None, None, "mp"),
        P("mp", None),
        P(None, None, "mp"),
        P("mp", None),
        P(),
        P(None, "mp"),
        P("dp", None),
        P("dp", None),
        P(),
    )
    out_specs = (
        P("dp", "mp", None),
        P("dp", "mp", None),
        P("dp", "mp", None),
        P("dp", "mp"),
        P(None, "dp", "mp"),
        P("mp", "dp"),
        P("dp", "mp"),
        P(None, "dp", "mp"),
        P("mp", "dp"),
        P(None, "dp", "mp"),
        P("mp", "dp"),
        P(),
        P(),
    )
    return jax.shard_map(body, mesh=mesh, in_specs=in_specs, out_specs=out_specs, check_vma=False)
```

```python
import functools

import jax
import jax.numpy as jnp
import numpy as np
from jax import lax
from jax.experimental import pallas as pl
from jax.experimental.pallas import tpu as pltpu
from jax.sharding import PartitionSpec as P

epsilon = 1e-06
masked_score = -1e30
gelu_root = float(np.sqrt(2.0 / np.pi))
gelu_cubic = 0.044715
block = 128
head_size = 64
f32 = jnp.float32
bf16 = jnp.bfloat16


def dot(left, right):
    return lax.dot_general(left, right, (((1,), (0,)), ((), ())), preferred_element_type=f32)


def dot_rt(left, right):
    return lax.dot_general(left, right, (((1,), (1,)), ((), ())), preferred_element_type=f32)


def dot_lt(left, right):
    return lax.dot_general(left, right, (((0,), (0,)), ((), ())), preferred_element_type=f32)


def pick(flag, first, second):
    return jnp.where(flag, first, second)


def even_odd(values):
    lane = lax.broadcasted_iota(jnp.int32, values.shape, 1)
    zero = jnp.zeros_like(values)
    return jnp.where(lane < head_size, values, zero), jnp.where(lane < head_size, zero, values)


def rms_scale(values):
    return lax.rsqrt(jnp.mean(values * values, axis=-1, keepdims=True) + epsilon)


def norm_back(values, gain, grad):
    scale = rms_scale(values)
    scaled = grad * gain
    inner = jnp.mean(values * scaled, axis=-1, keepdims=True)
    back = scale * scaled - values * (scale * scale * scale * inner)
    return back, grad * values * scale


def softmax(scores):
    top = jnp.max(scores, axis=-1, keepdims=True)
    weights = jnp.exp(scores - top)
    total = jnp.sum(weights, axis=-1, keepdims=True)
    return (weights * (1.0 / total)).astype(bf16)


times = {"memory_keyval": 10.0, "ffn_b": 10.0, "cross_back_a": 60.0, "cross_back_b": 60.0, "self_back_b": 2.5, "halve_ffn_two": 6.0, "halve_cross_two": 10.0, "final": 15.0}


class Made:
    def __init__(self, shape, dtype):
        self.shape, self.dtype, self.value = shape, dtype, None


def settled(arg):
    return arg.value if isinstance(arg, Made) and arg.value is not None else arg


class Group:
    def __init__(self, name, cost=0):
        self.name, self.cost, self.stages, self.inputs = name, cost, [], []

    def add(self, kernel, outs, args, scratch=(), flops=0):
        made = [Made(shape, dtype) for shape, dtype in outs]
        args = [settled(arg) for arg in args]
        self.stages.append((kernel, list(args), made, list(scratch)))
        self.cost += flops
        for arg in args:
            if not isinstance(arg, Made) and not any(arg is known for known in self.inputs):
                self.inputs.append(arg)
        return made

    def call(self, idx):
        made = [out for stage in self.stages for out in stage[2]]
        scratch = [item for stage in self.stages for item in stage[3]]

        def kernel(idx_ref, *refs):
            ins, refs = refs[: len(self.inputs)], refs[len(self.inputs) :]
            outs, spare = refs[: len(made)], list(refs[len(made) :])
            known = [(value, ref) for value, ref in zip(self.inputs + made, ins + outs, strict=True)]
            for body, args, stage_outs, stage_scratch in self.stages:
                taken = [next(ref for value, ref in known if value is item) for item in args + stage_outs]
                body(idx_ref, *taken, *[spare.pop(0) for _ in stage_scratch])

        out_shape = [jax.ShapeDtypeStruct(out.shape, out.dtype) for out in made]
        moved = sum(x.size * x.dtype.itemsize for x in self.inputs + out_shape)
        values = pl.pallas_call(
            kernel,
            name=self.name,
            out_shape=out_shape,
            in_specs=[pl.BlockSpec(memory_space=pltpu.SMEM)]
            + [pl.BlockSpec(memory_space=pltpu.VMEM)] * len(self.inputs),
            out_specs=[pl.BlockSpec(memory_space=pltpu.VMEM)] * len(made),
            scratch_shapes=scratch,
            compiler_params=pltpu.CompilerParams(vmem_limit_bytes=8 << 20),
            cost_estimate=pl.CostEstimate(flops=int(times.get(self.name, 0.01) * 1.15e9), transcendentals=0, bytes_accessed=1024),
        )(idx, *self.inputs)
        for out, value in zip(made, values, strict=True):
            out.value = value
        return values


def bias_kernel(idx_ref, line_ref, table_ref):
    heads = table_ref.shape[0]
    count = table_ref.shape[2] // block
    for head in range(heads):
        for step in range(count):
            line = line_ref[head : head + 1, step * 2 * block : (step + 1) * 2 * block]
            wide = jnp.broadcast_to(line, (block, 2 * block))
            turned = pltpu.roll(wide, 0, 1, stride=1, stride_axis=0)
            at = (count - 1 - step) * block
            table_ref[head, :, at : at + block] = turned[:, :block].astype(bf16)


def self_project_kernel(idx_ref, values_ref, gain_ref, wq_ref, wkv_ref, normed_ref, qkv_ref):
    inner = wq_ref.shape[1]
    gain = gain_ref[0:1, :].astype(f32)
    for at in range(0, values_ref.shape[0], block):
        values = values_ref[at : at + block, :].astype(f32)
        normed_ref[at : at + block, :] = (values * rms_scale(values) * gain).astype(bf16)
    qkv_ref[:, 0:inner] = dot(normed_ref[...], wq_ref[...]).astype(bf16)
    qkv_ref[:, inner : 2 * inner] = dot(normed_ref[...], wkv_ref[0]).astype(bf16)
    qkv_ref[:, 2 * inner :] = dot(normed_ref[...], wkv_ref[1]).astype(bf16)


def self_order_kernel(idx_ref, normed_own, qkv_own, normed_recv, qkv_recv, normed_a, normed_b, qkv_ref):
    mine = idx_ref[0] == 0
    rows = normed_own.shape[0]
    normed_a[...] = pick(mine, normed_own[...], normed_recv[...])
    normed_b[...] = pick(mine, normed_recv[...], normed_own[...])
    qkv_ref[0:rows, :] = pick(mine, qkv_own[...], qkv_recv[...])
    qkv_ref[rows:, :] = pick(mine, qkv_recv[...], qkv_own[...])


def self_attend_kernel(chunk, idx_ref, qkv_ref, segc_ref, segr_ref, table_ref, ctx_ref, prob_ref):
    rows, inner = ctx_ref.shape
    base = chunk * rows
    total = table_ref.shape[2]
    masks = []
    for at in range(0, rows, block):
        keys = base + at + block
        allowed = segc_ref[base + at : keys, :] == segr_ref[:, 0:keys]
        row = lax.broadcasted_iota(jnp.int32, (block, keys), 0) + (base + at)
        col = lax.broadcasted_iota(jnp.int32, (block, keys), 1)
        masks.append(jnp.where(allowed & (row >= col), 0.0, masked_score))
    for pair in range(0, inner, 2 * head_size):
        keys2 = qkv_ref[0 : base + rows, inner + pair : inner + pair + 128]
        values_e, values_o = even_odd(qkv_ref[0 : base + rows, 2 * inner + pair : 2 * inner + pair + 128])
        for number, at in enumerate(range(0, rows, block)):
            keys = base + at + block
            query_e, query_o = even_odd(qkv_ref[base + at : keys, pair : pair + 128])
            context = jnp.zeros((block, 128), f32)
            for head, query, values in (
                (pair // head_size, query_e, values_e),
                (pair // head_size + 1, query_o, values_o),
            ):
                scores = dot_rt(query, keys2[0:keys]) + table_ref[head, :, total - keys :].astype(f32)
                probs = softmax(scores + masks[number])
                prob_ref[head, at : at + block, 0:keys] = probs
                context = context + dot(probs, values[0:keys])
            ctx_ref[at : at + block, pair : pair + 128] = context.astype(bf16)


def weights_kernel(quarter_at, idx_ref, own_ref, beside_ref, own_core, beside_core, *outs):
    rows = outs[0].shape[0] // 4
    low, high = idx_ref[quarter_at], idx_ref[quarter_at + 1]
    for number, out_ref in enumerate(outs):
        part = slice(number * rows, (number + 1) * rows)
        for ref, at in (
            (own_ref, 2 * high + low),
            (beside_ref, 2 * (1 - high) + low),
            (own_core, 2 * high + (1 - low)),
            (beside_core, 2 * (1 - high) + (1 - low)),
        ):
            out_ref[pl.ds(pl.multiple_of(at * rows, 16), rows), :] = ref[part, :]


def memory_kernel(idx_ref, own_ref, recv_ref, wkv_ref, memory_ref, kv_ref):
    rows = own_ref.shape[0]
    inner = wkv_ref.shape[2]
    mine = idx_ref[0]
    memory_ref[pl.ds(pl.multiple_of(mine * rows, rows), rows), :] = own_ref[...]
    memory_ref[pl.ds(pl.multiple_of((1 - mine) * rows, rows), rows), :] = recv_ref[...]
    kv_ref[:, 0:inner] = dot(memory_ref[...], wkv_ref[0]).astype(bf16)
    kv_ref[:, inner : 2 * inner] = dot(memory_ref[...], wkv_ref[1]).astype(bf16)


def cross_forward_kernel(
    chunk,
    idx_ref,
    own_ref,
    recv_ref,
    before_ref,
    before_recv_ref,
    gain_ref,
    wo_ref,
    wo_pair_ref,
    wq_ref,
    kv_ref,
    segc_ref,
    segm_ref,
    after_ref,
    normed_ref,
    query_ref,
    ctx_ref,
    prob_ref,
):
    mine = idx_ref[0] == chunk
    rows = own_ref.shape[0]
    inner = wq_ref.shape[1]
    gain = gain_ref[1:2, :].astype(f32)
    after_ref[...] = dot(before_ref[...], wo_ref[...]) + dot(before_recv_ref[...], wo_pair_ref[...])
    for at in range(0, rows, block):
        part = slice(at, at + block)
        values = pick(mine, own_ref[part, :], recv_ref[part, :]).astype(f32) + after_ref[part, :]
        after_ref[part, :] = values
        normed_ref[part, :] = (values * rms_scale(values) * gain).astype(bf16)
    query_ref[...] = dot(normed_ref[...], wq_ref[...]).astype(bf16)
    masks = []
    for at in range(0, rows, block):
        allowed = segc_ref[chunk * rows + at : chunk * rows + at + block, :] == segm_ref[...]
        masks.append(jnp.where(allowed, 0.0, masked_score))
    for pair in range(0, inner, 2 * head_size):
        keys2 = kv_ref[:, pair : pair + 128]
        values_e, values_o = even_odd(kv_ref[:, inner + pair : inner + pair + 128])
        for number, at in enumerate(range(0, rows, block)):
            query_e, query_o = even_odd(query_ref[at : at + block, pair : pair + 128])
            context = jnp.zeros((block, 128), f32)
            for head, query, values in (
                (pair // head_size, query_e, values_e),
                (pair // head_size + 1, query_o, values_o),
            ):
                probs = softmax(dot_rt(query, keys2) + masks[number])
                prob_ref[head, at : at + block, :] = probs
                context = context + dot(probs, values)
            ctx_ref[at : at + block, pair : pair + 128] = context.astype(bf16)


def ffn_kernel(
    chunk,
    idx_ref,
    after_self_ref,
    before_ref,
    before_recv_ref,
    cot_ref,
    cot_recv_ref,
    gain_ref,
    wo_ref,
    wo_pair_ref,
    win_ref,
    wout_ref,
    after_ref,
    normed_ref,
    hidden_ref,
    grads_ref,
    back_ref,
    cot_scr,
):
    mine = idx_ref[0] == chunk
    rows = after_self_ref.shape[0]
    units = win_ref.shape[2]
    gain = gain_ref[2:3, :].astype(f32)
    after_ref[...] = dot(before_ref[...], wo_ref[...]) + dot(before_recv_ref[...], wo_pair_ref[...])
    for at in range(0, rows, block):
        part = slice(at, at + block)
        values = after_self_ref[part, :] + after_ref[part, :]
        after_ref[part, :] = values
        normed_ref[part, :] = (values * rms_scale(values) * gain).astype(bf16)
        cot_scr[part, :] = pick(mine, cot_ref[part, :], cot_recv_ref[part, :])
    wide = 256
    for at in range(0, units, wide):
        cols = slice(at, at + wide)
        gate = dot(normed_ref[...], win_ref[0, :, cols])
        upward = dot(normed_ref[...], win_ref[1, :, cols])
        grad = dot_rt(cot_scr[...], wout_ref[cols, :])
        square = gate * gate
        bend = jnp.tanh(gelu_root * gate * (1.0 + gelu_cubic * square))
        half = 0.5 * (1.0 + bend)
        gelu = gate * half
        slope = half + 0.5 * gelu_root * gate * (1.0 - bend * bend) * (1.0 + 3.0 * gelu_cubic * square)
        hidden_ref[:, cols] = (gelu * upward).astype(bf16)
        grads_ref[:, cols] = (grad * upward * slope).astype(bf16)
        grads_ref[:, units + at : units + at + wide] = (grad * gelu).astype(bf16)
    back_ref[...] = (
        dot_rt(grads_ref[:, 0:units], win_ref[0]) + dot_rt(grads_ref[:, units:], win_ref[1])
    ).astype(bf16)


def down_kernel(idx_ref, first_ref, second_ref, wout_ref, out_ref):
    hidden = pick(idx_ref[0] == 0, second_ref[...], first_ref[...])
    out_ref[...] = dot(hidden, wout_ref[...]).astype(bf16)


def join_kernel(idx_ref, first_ref, second_ref, out_ref):
    rows = first_ref.shape[0]
    out_ref[0:rows, :] = first_ref[...]
    out_ref[rows:, :] = second_ref[...]


def final_kernel(idx_ref, hid_a, hid_b, after_a, after_b, recv_ref, wout_ref, out_ref):
    mine = idx_ref[0] == 0
    own = dot(pick(mine, hid_a[...], hid_b[...]), wout_ref[...])
    out_ref[...] = (pick(mine, after_a[...], after_b[...]) + (own + recv_ref[0 : own.shape[0], :].astype(f32))).astype(bf16)


def turn_rows(values, place_ref, order, at):
    turned = jnp.transpose(values)
    size = turned.shape[0] // len(order)
    for number, position in enumerate(order):
        place_ref[position * size : (position + 1) * size, at : at + values.shape[0]] = turned[
            number * size : (number + 1) * size
        ]


def write_grads(bit_ref, turned_ref, right, send_ref, keep_ref, at):
    rows = send_ref.shape[0]
    mine = bit_ref[1]
    cols = slice(at, at + right.shape[1])
    keep_ref[:, cols] = dot(turned_ref[pl.ds(pl.multiple_of(mine * rows, rows), rows), :], right).astype(bf16)
    send_ref[:, cols] = dot(turned_ref[pl.ds(pl.multiple_of((1 - mine) * rows, rows), rows), :], right).astype(bf16)


def ffn_grads_kernel(
    orders,
    idx_ref,
    normed_a,
    normed_b,
    grads_a,
    grads_b,
    hidden_a,
    hidden_b,
    cot_ref,
    cot_recv_ref,
    send_first,
    keep_first,
    send_second,
    keep_second,
    turned,
    turned_two,
    turned_three,
):
    rows = normed_a.shape[0]
    mine = idx_ref[0] == 0
    units = hidden_a.shape[1]
    cut = send_first.shape[1]
    turn_rows(normed_a[...], turned, orders[0], 0)
    turn_rows(normed_b[...], turned, orders[0], rows)
    turn_rows(normed_a[...], turned_two, orders[1], 0)
    turn_rows(normed_b[...], turned_two, orders[1], rows)
    turn_rows(pick(mine, cot_ref[...], cot_recv_ref[...]), turned_three, orders[1], 0)
    turn_rows(pick(mine, cot_recv_ref[...], cot_ref[...]), turned_three, orders[1], rows)
    both = jnp.concatenate([grads_a[...], grads_b[...]], axis=0)
    write_grads(idx_ref, turned, both[:, :cut], send_first, keep_first, 0)
    write_grads(idx_ref, turned_two, both[:, cut:], send_second, keep_second, 0)
    hidden = jnp.concatenate([hidden_a[...], hidden_b[...]], axis=0)
    write_grads(idx_ref, turned_three, hidden, send_second, keep_second, 2 * units - cut)


def attend_back(query_rows, prob_ref, score_ref, grad_ref, key_of, value_of, dq_ref, inner, reach):
    for pair in range(0, inner, 2 * head_size):
        keys_e, keys_o = even_odd(key_of(pair))
        values2 = value_of(pair)
        for at in range(0, query_rows, block):
            keys = reach(at)
            grad_e, grad_o = even_odd(grad_ref[at : at + block, pair : pair + 128])
            total = jnp.zeros((block, 128), f32)
            for head, grad, key in (
                (pair // head_size, grad_e, keys_e),
                (pair // head_size + 1, grad_o, keys_o),
            ):
                probs = prob_ref[head, at : at + block, 0:keys].astype(f32)
                grad_probs = dot_rt(grad, values2[0:keys])
                delta = jnp.sum(probs * grad_probs, axis=-1, keepdims=True) / jnp.sum(
                    probs, axis=-1, keepdims=True
                )
                scores = (probs * (grad_probs - delta)).astype(bf16)
                score_ref[head, at : at + block, 0:keys] = scores
                total = total + dot(scores, key[0:keys])
            dq_ref[at : at + block, pair : pair + 128] = total.astype(bf16)


def cross_back_kernel(
    chunk,
    idx_ref,
    after_ref,
    back_ref,
    back_recv_ref,
    cot_ref,
    cot_recv_ref,
    gain_ref,
    wo_ref,
    wq_ref,
    kv_ref,
    prob_ref,
    grad_ref,
    sent_ref,
    dctx_ref,
    dq_ref,
    score_ref,
    out_ref,
    gain_out_ref,
):
    mine = idx_ref[0] == chunk
    rows = after_ref.shape[0]
    inner = wq_ref.shape[1]
    gain = gain_ref[2:3, :].astype(f32)
    gain_total = jnp.zeros((8, gain.shape[1]), f32)
    for at in range(0, rows, block):
        part = slice(at, at + block)
        incoming = back_ref[part, :].astype(f32) + back_recv_ref[part, :].astype(f32)
        back, gain_terms = norm_back(after_ref[part, :], gain, incoming)
        total = pick(mine, cot_ref[part, :], cot_recv_ref[part, :]).astype(f32) + back
        grad_ref[part, :] = total
        sent_ref[part, :] = total.astype(bf16)
        gain_total = gain_total + jnp.sum(gain_terms.reshape(block // 8, 8, -1), axis=0)
    gain_out_ref[...] = pick(mine, gain_total, jnp.zeros_like(gain_total))
    dctx_ref[...] = dot_rt(sent_ref[...], wo_ref[...]).astype(bf16)
    attend_back(
        rows,
        prob_ref,
        score_ref,
        dctx_ref,
        lambda pair: kv_ref[:, pair : pair + 128],
        lambda pair: kv_ref[:, inner + pair : inner + pair + 128],
        dq_ref,
        inner,
        lambda at: kv_ref.shape[0],
    )
    out_ref[...] = dot_rt(dq_ref[...], wq_ref[...]).astype(bf16)


def cross_grads_kernel(
    order,
    idx_ref,
    normed_a,
    normed_b,
    dq_a,
    dq_b,
    query_a,
    query_b,
    score_a,
    score_b,
    prob_a,
    prob_b,
    dctx_a,
    dctx_b,
    ctx_a,
    ctx_b,
    sent_a,
    sent_b,
    memory_ref,
    wkv_ref,
    send_ref,
    keep_ref,
    memory_send_ref,
    memory_keep_ref,
    turned,
    turned_two,
    turned_three,
    dkv,
):
    rows = normed_a.shape[0]
    inner = dq_a.shape[1]
    for pair in range(0, inner, 2 * head_size):
        keys = jnp.zeros((dkv.shape[0], 128), f32)
        values = jnp.zeros((dkv.shape[0], 128), f32)
        for score, prob, query, dctx in ((score_a, prob_a, query_a, dctx_a), (score_b, prob_b, query_b, dctx_b)):
            cols = slice(pair, pair + 128)
            for number, (query_half, grad_half) in enumerate(
                zip(even_odd(query[:, cols]), even_odd(dctx[:, cols]), strict=True)
            ):
                head = pair // head_size + number
                keys = keys + dot_lt(score[head], query_half)
                values = values + dot_lt(prob[head], grad_half)
        dkv[:, pair : pair + 128] = keys.astype(bf16)
        dkv[:, inner + pair : inner + pair + 128] = values.astype(bf16)
    mine = idx_ref[0]
    other = pl.ds(pl.multiple_of((1 - mine) * rows, rows), rows)
    own = pl.ds(pl.multiple_of(mine * rows, rows), rows)
    memory_send_ref[...] = (
        dot_rt(dkv[other, 0:inner], wkv_ref[0]) + dot_rt(dkv[other, inner:], wkv_ref[1])
    ).astype(bf16)
    memory_keep_ref[...] = dot_rt(dkv[own, 0:inner], wkv_ref[0]) + dot_rt(dkv[own, inner:], wkv_ref[1])
    turn_rows(normed_a[...], turned, order, 0)
    turn_rows(normed_b[...], turned, order, rows)
    both = jnp.concatenate([dq_a[...], dq_b[...]], axis=0)
    write_grads(idx_ref, turned, both, send_ref, keep_ref, 0)
    turn_rows(memory_ref[...], turned_two, order, 0)
    write_grads(idx_ref, turned_two, dkv[...], send_ref, keep_ref, inner)
    turn_rows(sent_a[...], turned_three, order, 0)
    turn_rows(sent_b[...], turned_three, order, rows)
    both = jnp.concatenate([ctx_a[...], ctx_b[...]], axis=0)
    write_grads(idx_ref, turned_three, both, send_ref, keep_ref, 3 * inner)


def self_back_kernel(
    chunk,
    idx_ref,
    after_ref,
    back_ref,
    back_recv_ref,
    cross_ref,
    gain_ref,
    wo_ref,
    qkv_ref,
    prob_ref,
    grad_ref,
    sent_ref,
    dctx_ref,
    dq_ref,
    score_ref,
    gain_out_ref,
):
    mine = idx_ref[0] == chunk
    rows = after_ref.shape[0]
    inner = wo_ref.shape[0]
    gain = gain_ref[1:2, :].astype(f32)
    gain_total = jnp.zeros((8, gain.shape[1]), f32)
    for at in range(0, rows, block):
        part = slice(at, at + block)
        incoming = back_ref[part, :].astype(f32) + back_recv_ref[part, :].astype(f32)
        back, gain_terms = norm_back(after_ref[part, :], gain, incoming)
        total = cross_ref[part, :] + back
        grad_ref[part, :] = total
        sent_ref[part, :] = total.astype(bf16)
        gain_total = gain_total + jnp.sum(gain_terms.reshape(block // 8, 8, -1), axis=0)
    gain_out_ref[...] = pick(mine, gain_total, jnp.zeros_like(gain_total))
    dctx_ref[...] = dot_rt(sent_ref[...], wo_ref[...]).astype(bf16)
    end = (chunk + 1) * rows
    attend_back(
        rows,
        prob_ref,
        score_ref,
        dctx_ref,
        lambda pair: qkv_ref[0:end, inner + pair : inner + pair + 128],
        lambda pair: qkv_ref[0:end, 2 * inner + pair : 2 * inner + pair + 128],
        dq_ref,
        inner,
        lambda at: chunk * rows + at + block,
    )


def self_grads_kernel(
    order,
    idx_ref,
    normed_a,
    normed_b,
    dq_a,
    dq_b,
    qkv_ref,
    score_a,
    score_b,
    prob_a,
    prob_b,
    dctx_a,
    dctx_b,
    ctx_a,
    ctx_b,
    sent_a,
    sent_b,
    send_ref,
    keep_ref,
    dqkv_ref,
    turned,
    turned_two,
):
    rows = normed_a.shape[0]
    inner = dq_a.shape[1]
    for pair in range(0, inner, 2 * head_size):
        for at in range(0, 2 * rows, block):
            keys = jnp.zeros((block, 128), f32)
            values = jnp.zeros((block, 128), f32)
            cols = slice(pair, pair + 128)
            span = slice(at, at + block)
            for base, score, prob, dctx in ((0, score_a, prob_a, dctx_a), (rows, score_b, prob_b, dctx_b)):
                if at >= base + rows:
                    continue
                low = max(at - base, 0)
                for number, (query_half, grad_half) in enumerate(
                    zip(even_odd(qkv_ref[base + low : base + rows, cols]), even_odd(dctx[low:rows, cols]), strict=True)
                ):
                    head = pair // head_size + number
                    keys = keys + dot_lt(score[head, low:rows, span], query_half)
                    values = values + dot_lt(prob[head, low:rows, span], grad_half)
            dqkv_ref[span, inner + pair : inner + pair + 128] = keys.astype(bf16)
            dqkv_ref[span, 2 * inner + pair : 2 * inner + pair + 128] = values.astype(bf16)
    dqkv_ref[0:rows, 0:inner] = dq_a[...]
    dqkv_ref[rows : 2 * rows, 0:inner] = dq_b[...]
    turn_rows(normed_a[...], turned, order, 0)
    turn_rows(normed_b[...], turned, order, rows)
    write_grads(idx_ref, turned, dqkv_ref[...], send_ref, keep_ref, 0)
    turn_rows(sent_a[...], turned_two, order, 0)
    turn_rows(sent_b[...], turned_two, order, rows)
    both = jnp.concatenate([ctx_a[...], ctx_b[...]], axis=0)
    write_grads(idx_ref, turned_two, both, send_ref, keep_ref, 3 * inner)


def diagonals(values):
    wide = jnp.concatenate([values, jnp.zeros_like(values)], axis=1)
    total = wide[0:8]
    for at in range(8, block, 8):
        total = total + pltpu.roll(wide[at : at + 8], 2 * block - at, 1)
    row = lax.broadcasted_iota(jnp.int32, total.shape, 0)
    for bit in (1, 2, 4):
        total = jnp.where((row & bit) != 0, pltpu.roll(total, 2 * block - bit, 1), total)
    return jnp.sum(total, axis=0, keepdims=True)


def self_input_kernel(
    idx_ref,
    dqkv_ref,
    own_ref,
    recv_ref,
    wq_ref,
    wkv_ref,
    score_a,
    score_b,
    hot_ref,
    two_a,
    two_b,
    three_a,
    three_b,
    send_ref,
    keep_ref,
    small_ref,
    line,
):
    rows = own_ref.shape[0]
    inner = wq_ref.shape[1]
    mine = idx_ref[0]
    gain_total = jnp.zeros((8, own_ref.shape[1]), f32)
    for which, values_ref in ((1 - mine, recv_ref), (mine, own_ref)):
        span = pl.ds(pl.multiple_of(which * rows, rows), rows)
        grad = (
            dot_rt(dqkv_ref[span, 0:inner], wq_ref[...])
            + dot_rt(dqkv_ref[span, inner : 2 * inner], wkv_ref[0])
            + dot_rt(dqkv_ref[span, 2 * inner :], wkv_ref[1])
        )
        if values_ref is recv_ref:
            send_ref[0:rows, :] = grad.astype(bf16)
        else:
            keep_ref[...] = grad
        values = values_ref[...].astype(f32)
        terms = grad * values * rms_scale(values)
        gain_total = gain_total + jnp.sum(terms.reshape(rows // 8, 8, -1), axis=0)
    heads = score_a.shape[0]
    count = 2 * rows // block
    line[...] = jnp.zeros_like(line)
    for head in range(heads):
        for step in range(count):
            total = jnp.zeros((block, block), f32)
            for at in range(step, count):
                col = (at - step) * block
                score = score_a if at * block < rows else score_b
                row = at * block % rows
                total = total + score[head, row : row + block, col : col + block].astype(f32)
            line[head : head + 1, step * 2 * block : (step + 1) * 2 * block] = diagonals(total)
    bias = lax.dot_general(
        line[...], hot_ref[...], (((1,), (1,)), ((), ())), precision=lax.Precision.HIGHEST, preferred_element_type=f32
    )
    buckets = hot_ref.shape[0]
    small_ref[...] = jnp.zeros_like(small_ref)
    small_ref[0:1, :] = jnp.sum(gain_total, axis=0, keepdims=True)
    small_ref[1:2, :] = jnp.sum(two_a[...] + two_b[...], axis=0, keepdims=True)
    small_ref[2:3, :] = jnp.sum(three_a[...] + three_b[...], axis=0, keepdims=True)
    small_ref[8:16, 0:buckets] = pick(mine == 0, bias, jnp.zeros_like(bias))
    small_ref[8:16, 128 : 128 + buckets] = pick(mine == 1, bias, jnp.zeros_like(bias))
    high = small_ref[...].astype(bf16)
    send_ref[rows : rows + 16, :] = high
    send_ref[rows + 16 :, :] = (small_ref[...] - high.astype(f32)).astype(bf16)


def input_grad_kernel(idx_ref, own_ref, keep_ref, recv_ref, grad_a, grad_b, gain_ref, out_ref):
    mine = idx_ref[0] == 0
    gain = gain_ref[0:1, :].astype(f32)
    for at in range(0, own_ref.shape[0], block):
        part = slice(at, at + block)
        incoming = keep_ref[part, :] + recv_ref[part, :].astype(f32)
        back, _ = norm_back(own_ref[part, :].astype(f32), gain, incoming)
        out_ref[part, :] = pick(mine, grad_a[part, :], grad_b[part, :]) + back


def halve_kernel(slot, idx_ref, keep_ref, got_ref, send_out, keep_out):
    rows = send_out.shape[0]
    mine = idx_ref[slot]
    other = pl.ds(pl.multiple_of((1 - mine) * rows, 16), rows)
    own = pl.ds(pl.multiple_of(mine * rows, 16), rows)
    send_out[...] = (keep_ref[other, :].astype(f32) + got_ref[other, :].astype(f32)).astype(bf16)
    keep_out[...] = (keep_ref[own, :].astype(f32) + got_ref[own, :].astype(f32)).astype(bf16)


def split_small(values):
    high = values.astype(bf16)
    return jnp.concatenate([high, (values - high.astype(f32)).astype(bf16)], axis=1)


def join_small(parts):
    width = parts.shape[1] // 2
    return parts[:, :width].astype(f32) + parts[:, width:].astype(f32)


def add_kernel(idx_ref, first_ref, second_ref, out_ref):
    out_ref[...] = split_small(join_small(first_ref[...]) + join_small(second_ref[...]))


def add_first_kernel(idx_ref, own_ref, got_ref, out_ref):
    rows = own_ref.shape[0]
    at = got_ref.shape[0] - 2 * rows
    got = got_ref[at : at + rows, :].astype(f32) + got_ref[at + rows :, :].astype(f32)
    out_ref[...] = split_small(join_small(split_small(own_ref[...])) + got)


def halve_small_kernel(slot, has_small, idx_ref, keep_ref, got_ref, *refs):
    send_out, keep_out = refs[-2:]
    count = 16
    rows = send_out.shape[0] - count
    mine = idx_ref[slot]
    other = pl.ds(pl.multiple_of((1 - mine) * rows, 16), rows)
    own = pl.ds(pl.multiple_of(mine * rows, 16), rows)
    send_out[0:rows, :] = (keep_ref[other, :].astype(f32) + got_ref[other, :].astype(f32)).astype(bf16)
    keep_out[0:rows, :] = (keep_ref[own, :].astype(f32) + got_ref[own, :].astype(f32)).astype(bf16)
    if has_small:
        small = split_small(join_small(keep_ref[2 * rows :, :]) + join_small(got_ref[2 * rows :, :]))
    else:
        small = split_small(join_small(refs[0][...]) + join_small(refs[1][...]))
    send_out[rows:, :] = small
    keep_out[rows:, :] = small


def finish_small_kernel(idx_ref, keep_ref, got_ref, out_ref):
    rows = keep_ref.shape[0] - 16
    out_ref[...] = split_small(join_small(keep_ref[rows:, :]) + join_small(got_ref[rows:, :]))


def last_small_kernel(idx_ref, *refs):
    *parts, gain_out, bias_out = refs
    at = parts[0].shape[0] - 16
    total = join_small(parts[0][at:, :])
    for part in parts[1:]:
        total = total + join_small(part[at:, :])
    heads, buckets = bias_out.shape[0] // 2, bias_out.shape[1]
    gain_out[...] = total[0:3, :]
    bias_out[0:heads, :] = total[8 : 8 + heads, 0:buckets]
    bias_out[heads:, :] = total[8 : 8 + heads, 128 : 128 + buckets]


def memory_add_kernel(idx_ref, keep_ref, got_ref, out_ref):
    out_ref[...] = keep_ref[...] + got_ref[keep_ref.shape[0] :, :].astype(f32)


def finish_kernel(idx_ref, *refs):
    count = next(at for at, ref in enumerate(refs) if ref.dtype == f32)
    left = refs[-1].shape[0]
    starts = [0]
    for keep_ref in refs[0:count:2]:
        starts.append(starts[-1] + keep_ref.shape[1])

    def pieces(low, high):
        for number, start in enumerate(starts[:-1]):
            at, end = max(low, start), min(high, starts[number + 1])
            if at < end:
                cols = slice(at - start, end - start)
                keep = refs[2 * number][0:left, cols].astype(f32)
                yield at - low, end - low, keep + refs[2 * number + 1][0:left, cols].astype(f32)

    at = 0
    for out in refs[count:]:
        for values in [out] if len(out.shape) == 2 else [out.at[n] for n in range(out.shape[0])]:
            for low, high, total in pieces(at, at + values.shape[1]):
                values[:, low:high] = total
            at += values.shape[1]


def flip(values, bit, size):
    return lax.ppermute(settled(values), "dp", [(at, at ^ bit) for at in range(size)])


def swap(values):
    return lax.ppermute(settled(values), "mp", [(0, 1), (1, 0)])


def halving_plans(size, width):
    bits = [1 << at for at in range(size.bit_length() - 1)]
    if (width // size) % 16:
        return (bits[::-1], [0]), (bits[::-1], [0])
    plans = []
    for steps in (bits, bits[:1] + bits[2:] + bits[1:2]):
        order = [sum(((at // bit) % 2) * (size >> (step + 1)) for step, bit in enumerate(steps)) for at in range(size)]
        plans.append((steps, order))
    return plans


def body(
    hidden_in,
    memory,
    cotangent,
    self_query,
    self_keyval,
    self_output,
    cross_query,
    cross_keyval,
    cross_output,
    ffn_input,
    ffn_output,
    norm_gains,
    rel_bias,
    dec_segments,
    mem_segments,
    rel_bucket,
):
    dp = lax.axis_size("dp")
    position = lax.axis_index("dp")
    half = lax.axis_index("mp")
    own = hidden_in[0]
    rows, width = own.shape
    length = 2 * rows
    buckets, heads = rel_bias.shape
    inner = self_query.shape[1]
    units = ffn_output.shape[0]
    memory_own = memory[0]
    cot = cotangent[0]
    (steps, order), (ffn_steps, ffn_order) = halving_plans(dp, width)
    quarter = [position % 2, (position // 2) % 2]
    idx = jnp.stack([half] + [(position // bit) % 2 for bit in steps] + quarter).astype(jnp.int32)
    order_token = [idx]

    def run(group):
        if not group.stages:
            return []
        values = group.call(order_token[0])
        order_token[0] = lax.optimization_barrier((idx, values[-1]))[0]
        return values

    def single(name, kernel, outs, args, **options):
        group = Group(name)
        group.add(kernel, outs, args, **options)
        return run(group)

    places = steps

    class Scatter:
        def __init__(self, steps, send, keep):
            self.steps, self.keep, self.at, self.extra = steps, keep, 0, 0
            self.got = flip(send, self.steps[0], dp)

        def halve(self, group, *small):
            self.at += 1
            keep = settled(self.keep)
            cut, bit = (keep.shape[0] - self.extra) // 2, self.steps[self.at]
            if small or self.extra:
                kernel = functools.partial(halve_small_kernel, 1 + places.index(bit), self.extra > 0)
                self.extra = 16
                shape = ((cut + 16, keep.shape[1]), bf16)
                self.out, self.keep = group.add(kernel, [shape] * 2, [keep, self.got, *small])
            elif cut % 16 == 0:
                kernel = functools.partial(halve_kernel, 1 + places.index(bit))
                self.out, self.keep = group.add(kernel, [((cut, keep.shape[1]), bf16)] * 2, [keep, self.got])
            else:
                mine = ((position // bit) % 2) * cut
                take = functools.partial(lax.dynamic_slice_in_dim, slice_size=cut, axis=0)
                total = [(take(keep, at).astype(f32) + take(self.got, at).astype(f32)) for at in (cut - mine, mine)]
                self.out, self.keep = [values.astype(bf16) for values in total]

        def send(self):
            self.got = flip(self.out, self.steps[self.at], dp)

        def step(self, name, *small):
            group = Group(name)
            self.halve(group, *small)
            run(group)
            self.send()

        def total(self):
            while self.at < len(self.steps) - 1:
                self.step("halve")
            return settled(self.keep), self.got

    def together(name, *sums):
        group = Group(name)
        for item in sums:
            item.halve(group)
        run(group)
        for item in sums:
            item.send()

    def finish(group, sums, widths):
        left = width // dp
        shapes = [((left, w), f32) if n == 1 else ((n, left, w), f32) for n, w in widths]
        if left % 16 == 0:
            return group.add(finish_kernel, shapes, sums)
        total = jnp.concatenate([k.astype(f32) + g.astype(f32) for k, g in zip(sums[::2], sums[1::2], strict=True)], axis=1)
        outs, at = [], 0
        for n, w in widths:
            outs.append(total[:, at : at + n * w])
            at += n * w
        return [o if n == 1 else jnp.stack(jnp.split(o, n, axis=1)) for o, (n, w) in zip(outs, widths, strict=True)]

    recv = swap(own)
    piece = inner // 4
    spot = (position % 4) * piece
    cut = functools.partial(lax.dynamic_slice_in_dim, start_index=spot, slice_size=piece, axis=0)
    weight_own = swap(jnp.concatenate([cut(self_output), cut(cross_output)]))

    def after(values, made):
        return lax.optimization_barrier((values, settled(made)))[0]


    count = length // block
    lane = np.arange(2 * block)
    spot = np.arange(count)[:, None] * block + np.where(lane < block, -lane, 2 * block - lane)[None]
    spot = np.clip(spot, 0, length - 1).reshape(-1).astype(np.int32)
    firsts = jnp.sum((rel_bucket[None, :] < jnp.arange(buckets + 1, dtype=jnp.int32)[:, None]).astype(jnp.int32), axis=1)
    hot = ((spot[None] >= firsts[:-1, None]) & (spot[None] < firsts[1:, None])).astype(f32)
    line = jnp.einsum("bh,bs->hs", rel_bias, hot.astype(bf16), preferred_element_type=f32)
    line = jnp.pad(line, ((0, 8 - heads), (0, 0)))
    seg_col = dec_segments.reshape(length, 1)
    group = Group("bias_table")
    (table,) = group.add(bias_kernel, [((heads, block, length), bf16)], [line])
    projected = [((rows, width), bf16), ((rows, 3 * inner), bf16)]
    weights = [norm_gains, self_query, self_keyval]
    run(group)
    memory_recv = swap(after(memory_own, table))

    def self_attend(group, chunk):
        return group.add(
            functools.partial(self_attend_kernel, chunk),
            [((rows, inner), bf16), ((heads, rows, (chunk + 1) * rows), bf16)],
            [qkv, seg_col, dec_segments, table],
        )

    group = Group("self_forward_a")
    normed_own, qkv_own = group.add(self_project_kernel, projected, [own] + weights)
    normed_recv, qkv_recv = group.add(self_project_kernel, projected, [recv] + weights)
    normed_one_a, normed_one_b, qkv = group.add(
        self_order_kernel,
        [((rows, width), bf16), ((rows, width), bf16), ((length, 3 * inner), bf16)],
        [normed_own, qkv_own, normed_recv, qkv_recv],
    )
    ctx_one_a, prob_one_a = self_attend(group, 0)
    run(group)
    ctx_one_recv_a = swap(ctx_one_a)
    weight_beside = flip(after(weight_own, ctx_one_a), 2, dp)
    weight_core = flip(after(weight_own, ctx_one_a), 1, dp)
    group = Group("self_forward_b")
    ctx_one_b, prob_one_b = self_attend(group, 1)
    run(group)
    ctx_one_recv_b = swap(ctx_one_b)
    cot_recv = swap(after(cot, ctx_one_b))

    group = Group("memory_keyval")
    memory_all, kv = group.add(
        memory_kernel,
        [((length, width), bf16), ((length, 2 * inner), bf16)],
        [memory_own, memory_recv, cross_keyval],
    )
    run(group)
    weight_beside_core = flip(after(weight_beside, ctx_one_b), 1, dp)
    def cross_forward(group, chunk, before, before_recv):
        return group.add(
            functools.partial(cross_forward_kernel, chunk),
            [
                ((rows, width), f32),
                ((rows, width), bf16),
                ((rows, inner), bf16),
                ((rows, inner), bf16),
                ((heads, rows, length), bf16),
            ],
            [
                own,
                recv,
                before,
                before_recv,
                norm_gains,
                self_output,
                self_output_pair,
                cross_query,
                kv,
                seg_col,
                mem_segments,
            ],
        )

    group = Group("cross_forward_a")
    self_output_pair, cross_output_pair = group.add(
        functools.partial(weights_kernel, len(steps) + 1),
        [((inner, width), bf16), ((inner, width), bf16)],
        [weight_own, weight_beside, weight_core, weight_beside_core],
    )
    after_self_a, normed_two_a, query_two_a, ctx_two_a, prob_two_a = cross_forward(group, 0, ctx_one_a, ctx_one_recv_a)
    run(group)
    ctx_two_recv_a = swap(ctx_two_a)
    group = Group("cross_forward_b")
    after_self_b, normed_two_b, query_two_b, ctx_two_b, prob_two_b = cross_forward(group, 1, ctx_one_b, ctx_one_recv_b)
    run(group)
    ctx_two_recv_b = swap(ctx_two_b)

    def ffn(group, chunk, after_self, before, before_recv):
        return group.add(
            functools.partial(ffn_kernel, chunk),
            [
                ((rows, width), f32),
                ((rows, width), bf16),
                ((rows, units), bf16),
                ((rows, 2 * units), bf16),
                ((rows, width), bf16),
            ],
            [
                after_self,
                before,
                before_recv,
                cot,
                cot_recv,
                norm_gains,
                cross_output,
                cross_output_pair,
                ffn_input,
                ffn_output,
            ],
            scratch=[pltpu.VMEM((rows, width), bf16)],
        )

    group = Group("ffn_a")
    after_cross_a, normed_three_a, hidden_a, gate_grads_a, back_three_a = ffn(
        group, 0, after_self_a, ctx_two_a, ctx_two_recv_a
    )
    run(group)
    back_three_recv_a = swap(back_three_a)
    group = Group("ffn_b")
    after_cross_b, normed_three_b, hidden_b, gate_grads_b, back_three_b = ffn(
        group, 1, after_self_b, ctx_two_b, ctx_two_recv_b
    )
    first_send, first_keep, second_send, second_keep = group.add(
        functools.partial(ffn_grads_kernel, [order, ffn_order]),
        [((width // 2, 3 * units // 2), bf16)] * 4,
        [
            normed_three_a,
            normed_three_b,
            gate_grads_a,
            gate_grads_b,
            hidden_a,
            hidden_b,
            cot,
            cot_recv,
        ],
        scratch=[pltpu.VMEM((width, length), bf16)] * 3,
        flops=2 * length * width * units * 3,
    )
    run(group)
    back_three_recv_b = swap(back_three_b)
    ffn_sums = [Scatter(steps, first_send, first_keep), Scatter(ffn_steps, second_send, second_keep)]

    def cross_back(group, chunk, after, back, back_recv, prob):
        return group.add(
            functools.partial(cross_back_kernel, chunk),
            [
                ((rows, width), f32),
                ((rows, width), bf16),
                ((rows, inner), bf16),
                ((rows, inner), bf16),
                ((heads, rows, length), bf16),
                ((rows, width), bf16),
                ((8, width), f32),
            ],
            [after, back, back_recv, cot, cot_recv, norm_gains, cross_output, cross_query, kv, prob],
            flops=2 * rows * width * inner * 4,
        )

    group = Group("cross_back_a")
    grad_cross_a, sent_two_a, dctx_two_a, dq_two_a, score_two_a, back_two_a, three_a = cross_back(
        group, 0, after_cross_a, back_three_a, back_three_recv_a, prob_two_a
    )
    run(group)
    back_two_recv_a = swap(back_two_a)
    together("halve_ffn_one", *ffn_sums)
    group = Group("cross_back_b")
    grad_cross_b, sent_two_b, dctx_two_b, dq_two_b, score_two_b, back_two_b, three_b = cross_back(
        group, 1, after_cross_b, back_three_b, back_three_recv_b, prob_two_b
    )
    run(group)
    back_two_recv_b = swap(back_two_b)
    group = Group("self_back_a")
    cross_send, cross_keep, memory_send, memory_keep = group.add(
        functools.partial(cross_grads_kernel, order),
        [
            ((width // 2, 4 * inner), bf16),
            ((width // 2, 4 * inner), bf16),
            ((rows, width), bf16),
            ((rows, width), f32),
        ],
        [
            normed_two_a,
            normed_two_b,
            dq_two_a,
            dq_two_b,
            query_two_a,
            query_two_b,
            score_two_a,
            score_two_b,
            prob_two_a,
            prob_two_b,
            dctx_two_a,
            dctx_two_b,
            ctx_two_a,
            ctx_two_b,
            sent_two_a,
            sent_two_b,
            memory_all,
            cross_keyval,
        ],
        scratch=[pltpu.VMEM((width, length), bf16)] * 3 + [pltpu.VMEM((length, 2 * inner), bf16)],
        flops=2 * length * width * inner * 8,
    )

    def self_back(group, chunk, after, back, back_recv, grad_cross, prob):
        end = (chunk + 1) * rows
        return group.add(
            functools.partial(self_back_kernel, chunk),
            [
                ((rows, width), f32),
                ((rows, width), bf16),
                ((rows, inner), bf16),
                ((rows, inner), bf16),
                ((heads, rows, end), bf16),
                ((8, width), f32),
            ],
            [after, back, back_recv, grad_cross, norm_gains, self_output, qkv, prob],
            flops=2 * rows * width * inner * 3,
        )

    grad_self_a, sent_one_a, dctx_one_a, dq_one_a, score_one_a, two_a = self_back(
        group, 0, after_self_a, back_two_a, back_two_recv_a, grad_cross_a, prob_one_a
    )
    run(group)
    cross_sum = Scatter(steps, cross_send, cross_keep)
    group = Group("self_back_b")
    grad_self_b, sent_one_b, dctx_one_b, dq_one_b, score_one_b, two_b = self_back(
        group, 1, after_self_b, back_two_b, back_two_recv_b, grad_cross_b, prob_one_b
    )

    self_send, self_keep, dqkv = group.add(
        functools.partial(self_grads_kernel, order),
        [((width // 2, 4 * inner), bf16), ((width // 2, 4 * inner), bf16), ((length, 3 * inner), bf16)],
        [
            normed_one_a,
            normed_one_b,
            dq_one_a,
            dq_one_b,
            qkv,
            score_one_a,
            score_one_b,
            prob_one_a,
            prob_one_b,
            dctx_one_a,
            dctx_one_b,
            ctx_one_a,
            ctx_one_b,
            sent_one_a,
            sent_one_b,
        ],
        scratch=[pltpu.VMEM((width, length), bf16)] * 2,
        flops=2 * length * width * inner * 6,
    )
    run(group)
    self_sum = Scatter(steps, self_send, self_keep)
    together("halve_ffn_two", *ffn_sums)
    cross_sum.step("halve_cross_one")
    group = Group("self_input")
    back_one_send, back_one_keep, small_part = group.add(
        self_input_kernel,
        [((rows + 32, width), bf16), ((rows, width), f32), ((16, width), f32)],
        [
            dqkv,
            own,
            recv,
            self_query,
            self_keyval,
            score_one_a,
            score_one_b,
            hot,
            two_a,
            two_b,
            three_a,
            three_b,
        ],
        scratch=[pltpu.VMEM((8, 2 * length), f32)],
    )
    run(group)
    back_one_recv = swap(back_one_send)
    self_sum.step("halve_self_one")
    (out_part,) = single("down", down_kernel, [((rows, width), bf16)], [hidden_a, hidden_b, ffn_output])
    cross_sum.step("halve_cross_two")
    group = Group("input_grad")
    (grad_input,) = group.add(
        input_grad_kernel,
        [((rows, width), f32)],
        [own, back_one_keep, back_one_recv, grad_self_a, grad_self_b, norm_gains],
    )
    pair = ((16, 2 * width), bf16)
    (small,) = group.add(add_first_kernel, [pair], [small_part, back_one_recv])
    run(group)
    small_got = flip(small, 1, dp)
    together("halve_ffn_three", *ffn_sums)
    (small,) = single("small_add", add_kernel, [pair], [settled(small), small_got])
    small_got = flip(small, 2, dp)
    cross_sum.step("halve_cross_three")
    carried = steps == [1, 2, 4, 8] and 2 * width == 4 * inner
    if carried:
        group = Group("halve_self_two")
        self_sum.halve(group, small, small_got)
    else:
        for bit in sorted(steps)[2:]:
            (small,) = single("small_add", add_kernel, [pair], [settled(small), small_got])
            small_got = flip(small, bit, dp)
        (small,) = single("small_add", add_kernel, [pair], [small, small_got])
        group = Group("halve_self_two")
        self_sum.halve(group)
    (out_send,) = group.add(join_kernel, [((length, width), bf16)], [out_part, memory_send])
    run(group)
    self_sum.send()
    out_recv = swap(out_send)
    self_sum.step("halve_self_three")
    widths = [(1, inner), (2, inner), (1, inner)]
    group = Group("final")
    (output,) = group.add(
        final_kernel,
        [((rows, width), bf16)],
        [hidden_a, hidden_b, after_cross_a, after_cross_b, out_recv, ffn_output],
    )
    (grad_memory,) = group.add(memory_add_kernel, [((rows, width), f32)], [memory_keep, out_recv])
    grads_cross = finish(group, cross_sum.total(), widths)
    grads_ffn = finish(group, [part for item in ffn_sums for part in item.total()], [(2, units), (1, units)])
    run(group)
    group = Group("finish_self")
    rest = self_sum.total()
    grads_self = finish(group, rest, widths)
    small_outs = [((3, width), f32), ((2 * heads, buckets), f32)]
    gains, bias = group.add(last_small_kernel, small_outs, [*rest] if carried else [small])
    run(group)
    grads_ffn, grads_cross, grads_self = [[settled(g) for g in grads] for grads in (grads_ffn, grads_cross, grads_self)]
    return (
        settled(output)[None],
        settled(grad_input)[None],
        settled(grad_memory)[None],
        *grads_self[:-1],
        grads_self[-1].T,
        *grads_cross[:-1],
        grads_cross[-1].T,
        *grads_ffn[:-1],
        grads_ffn[-1].T,
        settled(gains),
        settled(bias).T,
    )


def solution(mesh):
    in_specs = (
        P("dp", "mp", None),
        P("dp", "mp", None),
        P("dp", "mp", None),
        P(None, "mp"),
        P(None, None, "mp"),
        P("mp", None),
        P(None, "mp"),
        P(None, None, "mp"),
        P("mp", None),
        P(None, None, "mp"),
        P("mp", None),
        P(),
        P(None, "mp"),
        P("dp", None),
        P("dp", None),
        P(),
    )
    out_specs = (
        P("dp", "mp", None),
        P("dp", "mp", None),
        P("dp", "mp", None),
        P("dp", "mp"),
        P(None, "dp", "mp"),
        P("mp", "dp"),
        P("dp", "mp"),
        P(None, "dp", "mp"),
        P("mp", "dp"),
        P(None, "dp", "mp"),
        P("mp", "dp"),
        P(),
        P(),
    )
    return jax.shard_map(body, mesh=mesh, in_specs=in_specs, out_specs=out_specs, check_vma=False)
```

```python
import functools

import jax
import jax.numpy as jnp
import numpy as np
from jax import lax
from jax.experimental import pallas as pl
from jax.experimental.pallas import tpu as pltpu
from jax.sharding import PartitionSpec as P

epsilon = 1e-06
masked_score = -1e30
gelu_root = float(np.sqrt(2.0 / np.pi))
gelu_cubic = 0.044715
block = 128
head_size = 64
f32 = jnp.float32
bf16 = jnp.bfloat16


def dot(left, right):
    return lax.dot_general(left, right, (((1,), (0,)), ((), ())), preferred_element_type=f32)


def dot_rt(left, right):
    return lax.dot_general(left, right, (((1,), (1,)), ((), ())), preferred_element_type=f32)


def dot_lt(left, right):
    return lax.dot_general(left, right, (((0,), (0,)), ((), ())), preferred_element_type=f32)


def pick(flag, first, second):
    return jnp.where(flag, first, second)


def even_odd(values):
    lane = lax.broadcasted_iota(jnp.int32, values.shape, 1)
    zero = jnp.zeros_like(values)
    return jnp.where(lane < head_size, values, zero), jnp.where(lane < head_size, zero, values)


def rms_scale(values):
    return lax.rsqrt(jnp.mean(values * values, axis=-1, keepdims=True) + epsilon)


def norm_back(values, gain, grad):
    scale = rms_scale(values)
    scaled = grad * gain
    inner = jnp.mean(values * scaled, axis=-1, keepdims=True)
    back = scale * scaled - values * (scale * scale * scale * inner)
    return back, grad * values * scale


def softmax(scores):
    top = jnp.max(scores, axis=-1, keepdims=True)
    weights = jnp.exp(scores - top)
    total = jnp.sum(weights, axis=-1, keepdims=True)
    return (weights * (1.0 / total)).astype(bf16)


times = {"memory_keyval": 10.0, "ffn_b": 10.0, "cross_back_a": 60.0, "cross_back_b": 60.0, "self_back_b": 0.01, "halve_ffn_two": 15.0, "halve_cross_two": 10.0, "final": 15.0}


class Made:
    def __init__(self, shape, dtype):
        self.shape, self.dtype, self.value = shape, dtype, None


def settled(arg):
    return arg.value if isinstance(arg, Made) and arg.value is not None else arg


class Group:
    def __init__(self, name, cost=0):
        self.name, self.cost, self.stages, self.inputs = name, cost, [], []

    def add(self, kernel, outs, args, scratch=(), flops=0):
        made = [Made(shape, dtype) for shape, dtype in outs]
        args = [settled(arg) for arg in args]
        self.stages.append((kernel, list(args), made, list(scratch)))
        self.cost += flops
        for arg in args:
            if not isinstance(arg, Made) and not any(arg is known for known in self.inputs):
                self.inputs.append(arg)
        return made

    def call(self, idx):
        made = [out for stage in self.stages for out in stage[2]]
        scratch = [item for stage in self.stages for item in stage[3]]

        def kernel(idx_ref, *refs):
            ins, refs = refs[: len(self.inputs)], refs[len(self.inputs) :]
            outs, spare = refs[: len(made)], list(refs[len(made) :])
            known = [(value, ref) for value, ref in zip(self.inputs + made, ins + outs, strict=True)]
            for body, args, stage_outs, stage_scratch in self.stages:
                taken = [next(ref for value, ref in known if value is item) for item in args + stage_outs]
                body(idx_ref, *taken, *[spare.pop(0) for _ in stage_scratch])

        out_shape = [jax.ShapeDtypeStruct(out.shape, out.dtype) for out in made]
        moved = sum(x.size * x.dtype.itemsize for x in self.inputs + out_shape)
        values = pl.pallas_call(
            kernel,
            name=self.name,
            out_shape=out_shape,
            in_specs=[pl.BlockSpec(memory_space=pltpu.SMEM)]
            + [pl.BlockSpec(memory_space=pltpu.VMEM)] * len(self.inputs),
            out_specs=[pl.BlockSpec(memory_space=pltpu.VMEM)] * len(made),
            scratch_shapes=scratch,
            compiler_params=pltpu.CompilerParams(vmem_limit_bytes=8 << 20),
            cost_estimate=pl.CostEstimate(flops=int(times.get(self.name, 0.01) * 1.15e9), transcendentals=0, bytes_accessed=1024),
        )(idx, *self.inputs)
        for out, value in zip(made, values, strict=True):
            out.value = value
        return values


def bias_kernel(idx_ref, line_ref, table_ref):
    heads = table_ref.shape[0]
    count = table_ref.shape[2] // block
    for head in range(heads):
        for step in range(count):
            line = line_ref[head : head + 1, step * 2 * block : (step + 1) * 2 * block]
            wide = jnp.broadcast_to(line, (block, 2 * block))
            turned = pltpu.roll(wide, 0, 1, stride=1, stride_axis=0)
            at = (count - 1 - step) * block
            table_ref[head, :, at : at + block] = turned[:, :block].astype(bf16)


def self_project_kernel(idx_ref, values_ref, gain_ref, wq_ref, wkv_ref, normed_ref, qkv_ref):
    inner = wq_ref.shape[1]
    gain = gain_ref[0:1, :].astype(f32)
    for at in range(0, values_ref.shape[0], block):
        values = values_ref[at : at + block, :].astype(f32)
        normed_ref[at : at + block, :] = (values * rms_scale(values) * gain).astype(bf16)
    qkv_ref[:, 0:inner] = dot(normed_ref[...], wq_ref[...]).astype(bf16)
    qkv_ref[:, inner : 2 * inner] = dot(normed_ref[...], wkv_ref[0]).astype(bf16)
    qkv_ref[:, 2 * inner :] = dot(normed_ref[...], wkv_ref[1]).astype(bf16)


def self_order_kernel(idx_ref, normed_own, qkv_own, normed_recv, qkv_recv, normed_a, normed_b, qkv_ref):
    mine = idx_ref[0] == 0
    rows = normed_own.shape[0]
    normed_a[...] = pick(mine, normed_own[...], normed_recv[...])
    normed_b[...] = pick(mine, normed_recv[...], normed_own[...])
    qkv_ref[0:rows, :] = pick(mine, qkv_own[...], qkv_recv[...])
    qkv_ref[rows:, :] = pick(mine, qkv_recv[...], qkv_own[...])


def self_attend_kernel(chunk, idx_ref, qkv_ref, segc_ref, segr_ref, table_ref, ctx_ref, prob_ref):
    rows, inner = ctx_ref.shape
    base = chunk * rows
    total = table_ref.shape[2]
    masks = []
    for at in range(0, rows, block):
        keys = base + at + block
        allowed = segc_ref[base + at : keys, :] == segr_ref[:, 0:keys]
        row = lax.broadcasted_iota(jnp.int32, (block, keys), 0) + (base + at)
        col = lax.broadcasted_iota(jnp.int32, (block, keys), 1)
        masks.append(jnp.where(allowed & (row >= col), 0.0, masked_score))
    for pair in range(0, inner, 2 * head_size):
        keys2 = qkv_ref[0 : base + rows, inner + pair : inner + pair + 128]
        values_e, values_o = even_odd(qkv_ref[0 : base + rows, 2 * inner + pair : 2 * inner + pair + 128])
        for number, at in enumerate(range(0, rows, block)):
            keys = base + at + block
            query_e, query_o = even_odd(qkv_ref[base + at : keys, pair : pair + 128])
            context = jnp.zeros((block, 128), f32)
            for head, query, values in (
                (pair // head_size, query_e, values_e),
                (pair // head_size + 1, query_o, values_o),
            ):
                scores = dot_rt(query, keys2[0:keys]) + table_ref[head, :, total - keys :].astype(f32)
                probs = softmax(scores + masks[number])
                prob_ref[head, at : at + block, 0:keys] = probs
                context = context + dot(probs, values[0:keys])
            ctx_ref[at : at + block, pair : pair + 128] = context.astype(bf16)


def weights_kernel(quarter_at, idx_ref, own_ref, beside_ref, own_core, beside_core, *outs):
    rows = outs[0].shape[0] // 4
    low, high = idx_ref[quarter_at], idx_ref[quarter_at + 1]
    for number, out_ref in enumerate(outs):
        part = slice(number * rows, (number + 1) * rows)
        for ref, at in (
            (own_ref, 2 * high + low),
            (beside_ref, 2 * (1 - high) + low),
            (own_core, 2 * high + (1 - low)),
            (beside_core, 2 * (1 - high) + (1 - low)),
        ):
            out_ref[pl.ds(pl.multiple_of(at * rows, 16), rows), :] = ref[part, :]


def memory_kernel(idx_ref, own_ref, recv_ref, wkv_ref, memory_ref, kv_ref):
    rows = own_ref.shape[0]
    inner = wkv_ref.shape[2]
    mine = idx_ref[0]
    memory_ref[pl.ds(pl.multiple_of(mine * rows, rows), rows), :] = own_ref[...]
    memory_ref[pl.ds(pl.multiple_of((1 - mine) * rows, rows), rows), :] = recv_ref[...]
    kv_ref[:, 0:inner] = dot(memory_ref[...], wkv_ref[0]).astype(bf16)
    kv_ref[:, inner : 2 * inner] = dot(memory_ref[...], wkv_ref[1]).astype(bf16)


def cross_forward_kernel(
    chunk,
    idx_ref,
    own_ref,
    recv_ref,
    before_ref,
    before_recv_ref,
    gain_ref,
    wo_ref,
    wo_pair_ref,
    wq_ref,
    kv_ref,
    segc_ref,
    segm_ref,
    after_ref,
    normed_ref,
    query_ref,
    ctx_ref,
    prob_ref,
):
    mine = idx_ref[0] == chunk
    rows = own_ref.shape[0]
    inner = wq_ref.shape[1]
    gain = gain_ref[1:2, :].astype(f32)
    after_ref[...] = dot(before_ref[...], wo_ref[...]) + dot(before_recv_ref[...], wo_pair_ref[...])
    for at in range(0, rows, block):
        part = slice(at, at + block)
        values = pick(mine, own_ref[part, :], recv_ref[part, :]).astype(f32) + after_ref[part, :]
        after_ref[part, :] = values
        normed_ref[part, :] = (values * rms_scale(values) * gain).astype(bf16)
    query_ref[...] = dot(normed_ref[...], wq_ref[...]).astype(bf16)
    masks = []
    for at in range(0, rows, block):
        allowed = segc_ref[chunk * rows + at : chunk * rows + at + block, :] == segm_ref[...]
        masks.append(jnp.where(allowed, 0.0, masked_score))
    for pair in range(0, inner, 2 * head_size):
        keys2 = kv_ref[:, pair : pair + 128]
        values_e, values_o = even_odd(kv_ref[:, inner + pair : inner + pair + 128])
        for number, at in enumerate(range(0, rows, block)):
            query_e, query_o = even_odd(query_ref[at : at + block, pair : pair + 128])
            context = jnp.zeros((block, 128), f32)
            for head, query, values in (
                (pair // head_size, query_e, values_e),
                (pair // head_size + 1, query_o, values_o),
            ):
                probs = softmax(dot_rt(query, keys2) + masks[number])
                prob_ref[head, at : at + block, :] = probs
                context = context + dot(probs, values)
            ctx_ref[at : at + block, pair : pair + 128] = context.astype(bf16)


def ffn_kernel(
    chunk,
    idx_ref,
    after_self_ref,
    before_ref,
    before_recv_ref,
    cot_ref,
    cot_recv_ref,
    gain_ref,
    wo_ref,
    wo_pair_ref,
    win_ref,
    wout_ref,
    after_ref,
    normed_ref,
    hidden_ref,
    grads_ref,
    back_ref,
    cot_scr,
):
    mine = idx_ref[0] == chunk
    rows = after_self_ref.shape[0]
    units = win_ref.shape[2]
    gain = gain_ref[2:3, :].astype(f32)
    after_ref[...] = dot(before_ref[...], wo_ref[...]) + dot(before_recv_ref[...], wo_pair_ref[...])
    for at in range(0, rows, block):
        part = slice(at, at + block)
        values = after_self_ref[part, :] + after_ref[part, :]
        after_ref[part, :] = values
        normed_ref[part, :] = (values * rms_scale(values) * gain).astype(bf16)
        cot_scr[part, :] = pick(mine, cot_ref[part, :], cot_recv_ref[part, :])
    wide = 256
    for at in range(0, units, wide):
        cols = slice(at, at + wide)
        gate = dot(normed_ref[...], win_ref[0, :, cols])
        upward = dot(normed_ref[...], win_ref[1, :, cols])
        grad = dot_rt(cot_scr[...], wout_ref[cols, :])
        square = gate * gate
        bend = jnp.tanh(gelu_root * gate * (1.0 + gelu_cubic * square))
        half = 0.5 * (1.0 + bend)
        gelu = gate * half
        slope = half + 0.5 * gelu_root * gate * (1.0 - bend * bend) * (1.0 + 3.0 * gelu_cubic * square)
        hidden_ref[:, cols] = (gelu * upward).astype(bf16)
        grads_ref[:, cols] = (grad * upward * slope).astype(bf16)
        grads_ref[:, units + at : units + at + wide] = (grad * gelu).astype(bf16)
    back_ref[...] = (
        dot_rt(grads_ref[:, 0:units], win_ref[0]) + dot_rt(grads_ref[:, units:], win_ref[1])
    ).astype(bf16)


def down_kernel(idx_ref, first_ref, second_ref, wout_ref, out_ref):
    hidden = pick(idx_ref[0] == 0, second_ref[...], first_ref[...])
    out_ref[...] = dot(hidden, wout_ref[...]).astype(bf16)


def join_kernel(idx_ref, first_ref, second_ref, out_ref):
    rows = first_ref.shape[0]
    out_ref[0:rows, :] = first_ref[...]
    out_ref[rows:, :] = second_ref[...]


def final_kernel(idx_ref, hid_a, hid_b, after_a, after_b, recv_ref, wout_ref, out_ref):
    mine = idx_ref[0] == 0
    own = dot(pick(mine, hid_a[...], hid_b[...]), wout_ref[...])
    out_ref[...] = (pick(mine, after_a[...], after_b[...]) + (own + recv_ref[0 : own.shape[0], :].astype(f32))).astype(bf16)


def turn_rows(values, place_ref, order, at):
    turned = jnp.transpose(values)
    size = turned.shape[0] // len(order)
    for number, position in enumerate(order):
        place_ref[position * size : (position + 1) * size, at : at + values.shape[0]] = turned[
            number * size : (number + 1) * size
        ]


def write_grads(bit_ref, turned_ref, right, send_ref, keep_ref, at):
    rows = send_ref.shape[0]
    mine = bit_ref[1]
    cols = slice(at, at + right.shape[1])
    keep_ref[:, cols] = dot(turned_ref[pl.ds(pl.multiple_of(mine * rows, rows), rows), :], right).astype(bf16)
    send_ref[:, cols] = dot(turned_ref[pl.ds(pl.multiple_of((1 - mine) * rows, rows), rows), :], right).astype(bf16)


def ffn_grads_kernel(
    orders,
    idx_ref,
    normed_a,
    normed_b,
    grads_a,
    grads_b,
    hidden_a,
    hidden_b,
    cot_ref,
    cot_recv_ref,
    send_first,
    keep_first,
    send_second,
    keep_second,
    turned,
    turned_two,
    turned_three,
):
    rows = normed_a.shape[0]
    mine = idx_ref[0] == 0
    units = hidden_a.shape[1]
    cut = send_first.shape[1]
    turn_rows(normed_a[...], turned, orders[0], 0)
    turn_rows(normed_b[...], turned, orders[0], rows)
    turn_rows(normed_a[...], turned_two, orders[1], 0)
    turn_rows(normed_b[...], turned_two, orders[1], rows)
    turn_rows(pick(mine, cot_ref[...], cot_recv_ref[...]), turned_three, orders[1], 0)
    turn_rows(pick(mine, cot_recv_ref[...], cot_ref[...]), turned_three, orders[1], rows)
    both = jnp.concatenate([grads_a[...], grads_b[...]], axis=0)
    write_grads(idx_ref, turned, both[:, :cut], send_first, keep_first, 0)
    write_grads(idx_ref, turned_two, both[:, cut:], send_second, keep_second, 0)
    hidden = jnp.concatenate([hidden_a[...], hidden_b[...]], axis=0)
    write_grads(idx_ref, turned_three, hidden, send_second, keep_second, 2 * units - cut)


def attend_back(query_rows, prob_ref, score_ref, grad_ref, key_of, value_of, dq_ref, inner, reach):
    for pair in range(0, inner, 2 * head_size):
        keys_e, keys_o = even_odd(key_of(pair))
        values2 = value_of(pair)
        for at in range(0, query_rows, block):
            keys = reach(at)
            grad_e, grad_o = even_odd(grad_ref[at : at + block, pair : pair + 128])
            total = jnp.zeros((block, 128), f32)
            for head, grad, key in (
                (pair // head_size, grad_e, keys_e),
                (pair // head_size + 1, grad_o, keys_o),
            ):
                probs = prob_ref[head, at : at + block, 0:keys].astype(f32)
                grad_probs = dot_rt(grad, values2[0:keys])
                delta = jnp.sum(probs * grad_probs, axis=-1, keepdims=True) / jnp.sum(
                    probs, axis=-1, keepdims=True
                )
                scores = (probs * (grad_probs - delta)).astype(bf16)
                score_ref[head, at : at + block, 0:keys] = scores
                total = total + dot(scores, key[0:keys])
            dq_ref[at : at + block, pair : pair + 128] = total.astype(bf16)


def cross_back_kernel(
    chunk,
    idx_ref,
    after_ref,
    back_ref,
    back_recv_ref,
    cot_ref,
    cot_recv_ref,
    gain_ref,
    wo_ref,
    wq_ref,
    kv_ref,
    prob_ref,
    grad_ref,
    sent_ref,
    dctx_ref,
    dq_ref,
    score_ref,
    out_ref,
    gain_out_ref,
):
    mine = idx_ref[0] == chunk
    rows = after_ref.shape[0]
    inner = wq_ref.shape[1]
    gain = gain_ref[2:3, :].astype(f32)
    gain_total = jnp.zeros((8, gain.shape[1]), f32)
    for at in range(0, rows, block):
        part = slice(at, at + block)
        incoming = back_ref[part, :].astype(f32) + back_recv_ref[part, :].astype(f32)
        back, gain_terms = norm_back(after_ref[part, :], gain, incoming)
        total = pick(mine, cot_ref[part, :], cot_recv_ref[part, :]).astype(f32) + back
        grad_ref[part, :] = total
        sent_ref[part, :] = total.astype(bf16)
        gain_total = gain_total + jnp.sum(gain_terms.reshape(block // 8, 8, -1), axis=0)
    gain_out_ref[...] = pick(mine, gain_total, jnp.zeros_like(gain_total))
    dctx_ref[...] = dot_rt(sent_ref[...], wo_ref[...]).astype(bf16)
    attend_back(
        rows,
        prob_ref,
        score_ref,
        dctx_ref,
        lambda pair: kv_ref[:, pair : pair + 128],
        lambda pair: kv_ref[:, inner + pair : inner + pair + 128],
        dq_ref,
        inner,
        lambda at: kv_ref.shape[0],
    )
    out_ref[...] = dot_rt(dq_ref[...], wq_ref[...]).astype(bf16)


def cross_grads_kernel(
    order,
    idx_ref,
    normed_a,
    normed_b,
    dq_a,
    dq_b,
    query_a,
    query_b,
    score_a,
    score_b,
    prob_a,
    prob_b,
    dctx_a,
    dctx_b,
    ctx_a,
    ctx_b,
    sent_a,
    sent_b,
    memory_ref,
    wkv_ref,
    send_ref,
    keep_ref,
    memory_send_ref,
    memory_keep_ref,
    turned,
    turned_two,
    turned_three,
    dkv,
):
    rows = normed_a.shape[0]
    inner = dq_a.shape[1]
    for pair in range(0, inner, 2 * head_size):
        keys = jnp.zeros((dkv.shape[0], 128), f32)
        values = jnp.zeros((dkv.shape[0], 128), f32)
        for score, prob, query, dctx in ((score_a, prob_a, query_a, dctx_a), (score_b, prob_b, query_b, dctx_b)):
            cols = slice(pair, pair + 128)
            for number, (query_half, grad_half) in enumerate(
                zip(even_odd(query[:, cols]), even_odd(dctx[:, cols]), strict=True)
            ):
                head = pair // head_size + number
                keys = keys + dot_lt(score[head], query_half)
                values = values + dot_lt(prob[head], grad_half)
        dkv[:, pair : pair + 128] = keys.astype(bf16)
        dkv[:, inner + pair : inner + pair + 128] = values.astype(bf16)
    mine = idx_ref[0]
    other = pl.ds(pl.multiple_of((1 - mine) * rows, rows), rows)
    own = pl.ds(pl.multiple_of(mine * rows, rows), rows)
    memory_send_ref[...] = (
        dot_rt(dkv[other, 0:inner], wkv_ref[0]) + dot_rt(dkv[other, inner:], wkv_ref[1])
    ).astype(bf16)
    memory_keep_ref[...] = dot_rt(dkv[own, 0:inner], wkv_ref[0]) + dot_rt(dkv[own, inner:], wkv_ref[1])
    turn_rows(normed_a[...], turned, order, 0)
    turn_rows(normed_b[...], turned, order, rows)
    both = jnp.concatenate([dq_a[...], dq_b[...]], axis=0)
    write_grads(idx_ref, turned, both, send_ref, keep_ref, 0)
    turn_rows(memory_ref[...], turned_two, order, 0)
    write_grads(idx_ref, turned_two, dkv[...], send_ref, keep_ref, inner)
    turn_rows(sent_a[...], turned_three, order, 0)
    turn_rows(sent_b[...], turned_three, order, rows)
    both = jnp.concatenate([ctx_a[...], ctx_b[...]], axis=0)
    write_grads(idx_ref, turned_three, both, send_ref, keep_ref, 3 * inner)


def self_back_kernel(
    chunk,
    idx_ref,
    after_ref,
    back_ref,
    back_recv_ref,
    cross_ref,
    gain_ref,
    wo_ref,
    qkv_ref,
    prob_ref,
    grad_ref,
    sent_ref,
    dctx_ref,
    dq_ref,
    score_ref,
    gain_out_ref,
):
    mine = idx_ref[0] == chunk
    rows = after_ref.shape[0]
    inner = wo_ref.shape[0]
    gain = gain_ref[1:2, :].astype(f32)
    gain_total = jnp.zeros((8, gain.shape[1]), f32)
    for at in range(0, rows, block):
        part = slice(at, at + block)
        incoming = back_ref[part, :].astype(f32) + back_recv_ref[part, :].astype(f32)
        back, gain_terms = norm_back(after_ref[part, :], gain, incoming)
        total = cross_ref[part, :] + back
        grad_ref[part, :] = total
        sent_ref[part, :] = total.astype(bf16)
        gain_total = gain_total + jnp.sum(gain_terms.reshape(block // 8, 8, -1), axis=0)
    gain_out_ref[...] = pick(mine, gain_total, jnp.zeros_like(gain_total))
    dctx_ref[...] = dot_rt(sent_ref[...], wo_ref[...]).astype(bf16)
    end = (chunk + 1) * rows
    attend_back(
        rows,
        prob_ref,
        score_ref,
        dctx_ref,
        lambda pair: qkv_ref[0:end, inner + pair : inner + pair + 128],
        lambda pair: qkv_ref[0:end, 2 * inner + pair : 2 * inner + pair + 128],
        dq_ref,
        inner,
        lambda at: chunk * rows + at + block,
    )


def self_grads_kernel(
    order,
    idx_ref,
    normed_a,
    normed_b,
    dq_a,
    dq_b,
    qkv_ref,
    score_a,
    score_b,
    prob_a,
    prob_b,
    dctx_a,
    dctx_b,
    ctx_a,
    ctx_b,
    sent_a,
    sent_b,
    send_ref,
    keep_ref,
    dqkv_ref,
    turned,
    turned_two,
):
    rows = normed_a.shape[0]
    inner = dq_a.shape[1]
    for pair in range(0, inner, 2 * head_size):
        for at in range(0, 2 * rows, block):
            keys = jnp.zeros((block, 128), f32)
            values = jnp.zeros((block, 128), f32)
            cols = slice(pair, pair + 128)
            span = slice(at, at + block)
            for base, score, prob, dctx in ((0, score_a, prob_a, dctx_a), (rows, score_b, prob_b, dctx_b)):
                if at >= base + rows:
                    continue
                low = max(at - base, 0)
                for number, (query_half, grad_half) in enumerate(
                    zip(even_odd(qkv_ref[base + low : base + rows, cols]), even_odd(dctx[low:rows, cols]), strict=True)
                ):
                    head = pair // head_size + number
                    keys = keys + dot_lt(score[head, low:rows, span], query_half)
                    values = values + dot_lt(prob[head, low:rows, span], grad_half)
            dqkv_ref[span, inner + pair : inner + pair + 128] = keys.astype(bf16)
            dqkv_ref[span, 2 * inner + pair : 2 * inner + pair + 128] = values.astype(bf16)
    dqkv_ref[0:rows, 0:inner] = dq_a[...]
    dqkv_ref[rows : 2 * rows, 0:inner] = dq_b[...]
    turn_rows(normed_a[...], turned, order, 0)
    turn_rows(normed_b[...], turned, order, rows)
    write_grads(idx_ref, turned, dqkv_ref[...], send_ref, keep_ref, 0)
    turn_rows(sent_a[...], turned_two, order, 0)
    turn_rows(sent_b[...], turned_two, order, rows)
    both = jnp.concatenate([ctx_a[...], ctx_b[...]], axis=0)
    write_grads(idx_ref, turned_two, both, send_ref, keep_ref, 3 * inner)


def diagonals(values):
    wide = jnp.concatenate([values, jnp.zeros_like(values)], axis=1)
    total = wide[0:8]
    for at in range(8, block, 8):
        total = total + pltpu.roll(wide[at : at + 8], 2 * block - at, 1)
    row = lax.broadcasted_iota(jnp.int32, total.shape, 0)
    for bit in (1, 2, 4):
        total = jnp.where((row & bit) != 0, pltpu.roll(total, 2 * block - bit, 1), total)
    return jnp.sum(total, axis=0, keepdims=True)


def self_input_kernel(
    idx_ref,
    dqkv_ref,
    own_ref,
    recv_ref,
    wq_ref,
    wkv_ref,
    score_a,
    score_b,
    hot_ref,
    two_a,
    two_b,
    three_a,
    three_b,
    send_ref,
    keep_ref,
    small_ref,
    line,
):
    rows = own_ref.shape[0]
    inner = wq_ref.shape[1]
    mine = idx_ref[0]
    gain_total = jnp.zeros((8, own_ref.shape[1]), f32)
    for which, values_ref in ((1 - mine, recv_ref), (mine, own_ref)):
        span = pl.ds(pl.multiple_of(which * rows, rows), rows)
        grad = (
            dot_rt(dqkv_ref[span, 0:inner], wq_ref[...])
            + dot_rt(dqkv_ref[span, inner : 2 * inner], wkv_ref[0])
            + dot_rt(dqkv_ref[span, 2 * inner :], wkv_ref[1])
        )
        if values_ref is recv_ref:
            send_ref[0:rows, :] = grad.astype(bf16)
        else:
            keep_ref[...] = grad
        values = values_ref[...].astype(f32)
        terms = grad * values * rms_scale(values)
        gain_total = gain_total + jnp.sum(terms.reshape(rows // 8, 8, -1), axis=0)
    heads = score_a.shape[0]
    count = 2 * rows // block
    line[...] = jnp.zeros_like(line)
    for head in range(heads):
        for step in range(count):
            total = jnp.zeros((block, block), f32)
            for at in range(step, count):
                col = (at - step) * block
                score = score_a if at * block < rows else score_b
                row = at * block % rows
                total = total + score[head, row : row + block, col : col + block].astype(f32)
            line[head : head + 1, step * 2 * block : (step + 1) * 2 * block] = diagonals(total)
    bias = lax.dot_general(
        line[...], hot_ref[...], (((1,), (1,)), ((), ())), precision=lax.Precision.HIGHEST, preferred_element_type=f32
    )
    buckets = hot_ref.shape[0]
    small_ref[...] = jnp.zeros_like(small_ref)
    small_ref[0:1, :] = jnp.sum(gain_total, axis=0, keepdims=True)
    small_ref[1:2, :] = jnp.sum(two_a[...] + two_b[...], axis=0, keepdims=True)
    small_ref[2:3, :] = jnp.sum(three_a[...] + three_b[...], axis=0, keepdims=True)
    small_ref[8:16, 0:buckets] = pick(mine == 0, bias, jnp.zeros_like(bias))
    small_ref[8:16, 128 : 128 + buckets] = pick(mine == 1, bias, jnp.zeros_like(bias))
    high = small_ref[...].astype(bf16)
    send_ref[rows : rows + 16, :] = high
    send_ref[rows + 16 :, :] = (small_ref[...] - high.astype(f32)).astype(bf16)


def input_grad_kernel(idx_ref, own_ref, keep_ref, recv_ref, grad_a, grad_b, gain_ref, out_ref):
    mine = idx_ref[0] == 0
    gain = gain_ref[0:1, :].astype(f32)
    for at in range(0, own_ref.shape[0], block):
        part = slice(at, at + block)
        incoming = keep_ref[part, :] + recv_ref[part, :].astype(f32)
        back, _ = norm_back(own_ref[part, :].astype(f32), gain, incoming)
        out_ref[part, :] = pick(mine, grad_a[part, :], grad_b[part, :]) + back


def halve_kernel(slot, idx_ref, keep_ref, got_ref, send_out, keep_out):
    rows = send_out.shape[0]
    mine = idx_ref[slot]
    other = pl.ds(pl.multiple_of((1 - mine) * rows, 16), rows)
    own = pl.ds(pl.multiple_of(mine * rows, 16), rows)
    send_out[...] = (keep_ref[other, :].astype(f32) + got_ref[other, :].astype(f32)).astype(bf16)
    keep_out[...] = (keep_ref[own, :].astype(f32) + got_ref[own, :].astype(f32)).astype(bf16)


def split_small(values):
    high = values.astype(bf16)
    return jnp.concatenate([high, (values - high.astype(f32)).astype(bf16)], axis=1)


def join_small(parts):
    width = parts.shape[1] // 2
    return parts[:, :width].astype(f32) + parts[:, width:].astype(f32)


def add_kernel(idx_ref, first_ref, second_ref, out_ref):
    out_ref[...] = split_small(join_small(first_ref[...]) + join_small(second_ref[...]))


def add_first_kernel(idx_ref, own_ref, got_ref, out_ref):
    rows = own_ref.shape[0]
    at = got_ref.shape[0] - 2 * rows
    got = got_ref[at : at + rows, :].astype(f32) + got_ref[at + rows :, :].astype(f32)
    out_ref[...] = split_small(join_small(split_small(own_ref[...])) + got)


def halve_small_kernel(slot, has_small, idx_ref, keep_ref, got_ref, *refs):
    send_out, keep_out = refs[-2:]
    count = 16
    rows = send_out.shape[0] - count
    mine = idx_ref[slot]
    other = pl.ds(pl.multiple_of((1 - mine) * rows, 16), rows)
    own = pl.ds(pl.multiple_of(mine * rows, 16), rows)
    send_out[0:rows, :] = (keep_ref[other, :].astype(f32) + got_ref[other, :].astype(f32)).astype(bf16)
    keep_out[0:rows, :] = (keep_ref[own, :].astype(f32) + got_ref[own, :].astype(f32)).astype(bf16)
    if has_small:
        small = split_small(join_small(keep_ref[2 * rows :, :]) + join_small(got_ref[2 * rows :, :]))
    else:
        small = split_small(join_small(refs[0][...]) + join_small(refs[1][...]))
    send_out[rows:, :] = small
    keep_out[rows:, :] = small


def finish_small_kernel(idx_ref, keep_ref, got_ref, out_ref):
    rows = keep_ref.shape[0] - 16
    out_ref[...] = split_small(join_small(keep_ref[rows:, :]) + join_small(got_ref[rows:, :]))


def last_small_kernel(idx_ref, *refs):
    *parts, gain_out, bias_out = refs
    at = parts[0].shape[0] - 16
    total = join_small(parts[0][at:, :])
    for part in parts[1:]:
        total = total + join_small(part[at:, :])
    heads, buckets = bias_out.shape[0] // 2, bias_out.shape[1]
    gain_out[...] = total[0:3, :]
    bias_out[0:heads, :] = total[8 : 8 + heads, 0:buckets]
    bias_out[heads:, :] = total[8 : 8 + heads, 128 : 128 + buckets]


def memory_add_kernel(idx_ref, keep_ref, got_ref, out_ref):
    out_ref[...] = keep_ref[...] + got_ref[keep_ref.shape[0] :, :].astype(f32)


def finish_kernel(idx_ref, *refs):
    count = next(at for at, ref in enumerate(refs) if ref.dtype == f32)
    left = refs[-1].shape[0]
    starts = [0]
    for keep_ref in refs[0:count:2]:
        starts.append(starts[-1] + keep_ref.shape[1])

    def pieces(low, high):
        for number, start in enumerate(starts[:-1]):
            at, end = max(low, start), min(high, starts[number + 1])
            if at < end:
                cols = slice(at - start, end - start)
                keep = refs[2 * number][0:left, cols].astype(f32)
                yield at - low, end - low, keep + refs[2 * number + 1][0:left, cols].astype(f32)

    at = 0
    for out in refs[count:]:
        for values in [out] if len(out.shape) == 2 else [out.at[n] for n in range(out.shape[0])]:
            for low, high, total in pieces(at, at + values.shape[1]):
                values[:, low:high] = total
            at += values.shape[1]


def flip(values, bit, size):
    return lax.ppermute(settled(values), "dp", [(at, at ^ bit) for at in range(size)])


def swap(values):
    return lax.ppermute(settled(values), "mp", [(0, 1), (1, 0)])


def halving_plans(size, width):
    bits = [1 << at for at in range(size.bit_length() - 1)]
    if (width // size) % 16:
        return (bits[::-1], [0]), (bits[::-1], [0])
    plans = []
    for steps in (bits, bits[:1] + bits[2:] + bits[1:2]):
        order = [sum(((at // bit) % 2) * (size >> (step + 1)) for step, bit in enumerate(steps)) for at in range(size)]
        plans.append((steps, order))
    return plans


def body(
    hidden_in,
    memory,
    cotangent,
    self_query,
    self_keyval,
    self_output,
    cross_query,
    cross_keyval,
    cross_output,
    ffn_input,
    ffn_output,
    norm_gains,
    rel_bias,
    dec_segments,
    mem_segments,
    rel_bucket,
):
    dp = lax.axis_size("dp")
    position = lax.axis_index("dp")
    half = lax.axis_index("mp")
    own = hidden_in[0]
    rows, width = own.shape
    length = 2 * rows
    buckets, heads = rel_bias.shape
    inner = self_query.shape[1]
    units = ffn_output.shape[0]
    memory_own = memory[0]
    cot = cotangent[0]
    (steps, order), (ffn_steps, ffn_order) = halving_plans(dp, width)
    quarter = [position % 2, (position // 2) % 2]
    idx = jnp.stack([half] + [(position // bit) % 2 for bit in steps] + quarter).astype(jnp.int32)
    order_token = [idx]

    def run(group):
        if not group.stages:
            return []
        values = group.call(order_token[0])
        order_token[0] = lax.optimization_barrier((idx, values[-1]))[0]
        return values

    def single(name, kernel, outs, args, **options):
        group = Group(name)
        group.add(kernel, outs, args, **options)
        return run(group)

    places = steps

    class Scatter:
        def __init__(self, steps, send, keep):
            self.steps, self.keep, self.at, self.extra = steps, keep, 0, 0
            self.got = flip(send, self.steps[0], dp)

        def halve(self, group, *small):
            self.at += 1
            keep = settled(self.keep)
            cut, bit = (keep.shape[0] - self.extra) // 2, self.steps[self.at]
            if small or self.extra:
                kernel = functools.partial(halve_small_kernel, 1 + places.index(bit), self.extra > 0)
                self.extra = 16
                shape = ((cut + 16, keep.shape[1]), bf16)
                self.out, self.keep = group.add(kernel, [shape] * 2, [keep, self.got, *small])
            elif cut % 16 == 0:
                kernel = functools.partial(halve_kernel, 1 + places.index(bit))
                self.out, self.keep = group.add(kernel, [((cut, keep.shape[1]), bf16)] * 2, [keep, self.got])
            else:
                mine = ((position // bit) % 2) * cut
                take = functools.partial(lax.dynamic_slice_in_dim, slice_size=cut, axis=0)
                total = [(take(keep, at).astype(f32) + take(self.got, at).astype(f32)) for at in (cut - mine, mine)]
                self.out, self.keep = [values.astype(bf16) for values in total]

        def send(self):
            self.got = flip(self.out, self.steps[self.at], dp)

        def step(self, name, *small):
            group = Group(name)
            self.halve(group, *small)
            run(group)
            self.send()

        def total(self):
            while self.at < len(self.steps) - 1:
                self.step("halve")
            return settled(self.keep), self.got

    def together(name, *sums):
        group = Group(name)
        for item in sums:
            item.halve(group)
        run(group)
        for item in sums:
            item.send()

    def finish(group, sums, widths):
        left = width // dp
        shapes = [((left, w), f32) if n == 1 else ((n, left, w), f32) for n, w in widths]
        if left % 16 == 0:
            return group.add(finish_kernel, shapes, sums)
        total = jnp.concatenate([k.astype(f32) + g.astype(f32) for k, g in zip(sums[::2], sums[1::2], strict=True)], axis=1)
        outs, at = [], 0
        for n, w in widths:
            outs.append(total[:, at : at + n * w])
            at += n * w
        return [o if n == 1 else jnp.stack(jnp.split(o, n, axis=1)) for o, (n, w) in zip(outs, widths, strict=True)]

    recv = swap(own)
    piece = inner // 4
    spot = (position % 4) * piece
    cut = functools.partial(lax.dynamic_slice_in_dim, start_index=spot, slice_size=piece, axis=0)
    weight_own = swap(jnp.concatenate([cut(self_output), cut(cross_output)]))

    def after(values, made):
        return lax.optimization_barrier((values, settled(made)))[0]


    count = length // block
    lane = np.arange(2 * block)
    spot = np.arange(count)[:, None] * block + np.where(lane < block, -lane, 2 * block - lane)[None]
    spot = np.clip(spot, 0, length - 1).reshape(-1).astype(np.int32)
    firsts = jnp.sum((rel_bucket[None, :] < jnp.arange(buckets + 1, dtype=jnp.int32)[:, None]).astype(jnp.int32), axis=1)
    hot = ((spot[None] >= firsts[:-1, None]) & (spot[None] < firsts[1:, None])).astype(f32)
    line = jnp.einsum("bh,bs->hs", rel_bias, hot.astype(bf16), preferred_element_type=f32)
    line = jnp.pad(line, ((0, 8 - heads), (0, 0)))
    seg_col = dec_segments.reshape(length, 1)
    group = Group("bias_table")
    (table,) = group.add(bias_kernel, [((heads, block, length), bf16)], [line])
    projected = [((rows, width), bf16), ((rows, 3 * inner), bf16)]
    weights = [norm_gains, self_query, self_keyval]
    run(group)
    memory_recv = swap(after(memory_own, table))

    def self_attend(group, chunk):
        return group.add(
            functools.partial(self_attend_kernel, chunk),
            [((rows, inner), bf16), ((heads, rows, (chunk + 1) * rows), bf16)],
            [qkv, seg_col, dec_segments, table],
        )

    group = Group("self_forward_a")
    normed_own, qkv_own = group.add(self_project_kernel, projected, [own] + weights)
    normed_recv, qkv_recv = group.add(self_project_kernel, projected, [recv] + weights)
    normed_one_a, normed_one_b, qkv = group.add(
        self_order_kernel,
        [((rows, width), bf16), ((rows, width), bf16), ((length, 3 * inner), bf16)],
        [normed_own, qkv_own, normed_recv, qkv_recv],
    )
    ctx_one_a, prob_one_a = self_attend(group, 0)
    run(group)
    ctx_one_recv_a = swap(ctx_one_a)
    weight_beside = flip(after(weight_own, ctx_one_a), 2, dp)
    weight_core = flip(after(weight_own, ctx_one_a), 1, dp)
    group = Group("self_forward_b")
    ctx_one_b, prob_one_b = self_attend(group, 1)
    run(group)
    ctx_one_recv_b = swap(ctx_one_b)
    cot_recv = swap(after(cot, ctx_one_b))

    group = Group("memory_keyval")
    memory_all, kv = group.add(
        memory_kernel,
        [((length, width), bf16), ((length, 2 * inner), bf16)],
        [memory_own, memory_recv, cross_keyval],
    )
    run(group)
    weight_beside_core = flip(after(weight_beside, ctx_one_b), 1, dp)
    def cross_forward(group, chunk, before, before_recv):
        return group.add(
            functools.partial(cross_forward_kernel, chunk),
            [
                ((rows, width), f32),
                ((rows, width), bf16),
                ((rows, inner), bf16),
                ((rows, inner), bf16),
                ((heads, rows, length), bf16),
            ],
            [
                own,
                recv,
                before,
                before_recv,
                norm_gains,
                self_output,
                self_output_pair,
                cross_query,
                kv,
                seg_col,
                mem_segments,
            ],
        )

    group = Group("cross_forward_a")
    self_output_pair, cross_output_pair = group.add(
        functools.partial(weights_kernel, len(steps) + 1),
        [((inner, width), bf16), ((inner, width), bf16)],
        [weight_own, weight_beside, weight_core, weight_beside_core],
    )
    after_self_a, normed_two_a, query_two_a, ctx_two_a, prob_two_a = cross_forward(group, 0, ctx_one_a, ctx_one_recv_a)
    run(group)
    ctx_two_recv_a = swap(ctx_two_a)
    group = Group("cross_forward_b")
    after_self_b, normed_two_b, query_two_b, ctx_two_b, prob_two_b = cross_forward(group, 1, ctx_one_b, ctx_one_recv_b)
    run(group)
    ctx_two_recv_b = swap(ctx_two_b)

    def ffn(group, chunk, after_self, before, before_recv):
        return group.add(
            functools.partial(ffn_kernel, chunk),
            [
                ((rows, width), f32),
                ((rows, width), bf16),
                ((rows, units), bf16),
                ((rows, 2 * units), bf16),
                ((rows, width), bf16),
            ],
            [
                after_self,
                before,
                before_recv,
                cot,
                cot_recv,
                norm_gains,
                cross_output,
                cross_output_pair,
                ffn_input,
                ffn_output,
            ],
            scratch=[pltpu.VMEM((rows, width), bf16)],
        )

    group = Group("ffn_a")
    after_cross_a, normed_three_a, hidden_a, gate_grads_a, back_three_a = ffn(
        group, 0, after_self_a, ctx_two_a, ctx_two_recv_a
    )
    run(group)
    back_three_recv_a = swap(back_three_a)
    group = Group("ffn_b")
    after_cross_b, normed_three_b, hidden_b, gate_grads_b, back_three_b = ffn(
        group, 1, after_self_b, ctx_two_b, ctx_two_recv_b
    )
    first_send, first_keep, second_send, second_keep = group.add(
        functools.partial(ffn_grads_kernel, [order, ffn_order]),
        [((width // 2, 3 * units // 2), bf16)] * 4,
        [
            normed_three_a,
            normed_three_b,
            gate_grads_a,
            gate_grads_b,
            hidden_a,
            hidden_b,
            cot,
            cot_recv,
        ],
        scratch=[pltpu.VMEM((width, length), bf16)] * 3,
        flops=2 * length * width * units * 3,
    )
    run(group)
    back_three_recv_b = swap(back_three_b)
    ffn_sums = [Scatter(steps, first_send, first_keep), Scatter(ffn_steps, second_send, second_keep)]

    def cross_back(group, chunk, after, back, back_recv, prob):
        return group.add(
            functools.partial(cross_back_kernel, chunk),
            [
                ((rows, width), f32),
                ((rows, width), bf16),
                ((rows, inner), bf16),
                ((rows, inner), bf16),
                ((heads, rows, length), bf16),
                ((rows, width), bf16),
                ((8, width), f32),
            ],
            [after, back, back_recv, cot, cot_recv, norm_gains, cross_output, cross_query, kv, prob],
            flops=2 * rows * width * inner * 4,
        )

    group = Group("cross_back_a")
    grad_cross_a, sent_two_a, dctx_two_a, dq_two_a, score_two_a, back_two_a, three_a = cross_back(
        group, 0, after_cross_a, back_three_a, back_three_recv_a, prob_two_a
    )
    run(group)
    back_two_recv_a = swap(back_two_a)
    together("halve_ffn_one", *ffn_sums)
    group = Group("cross_back_b")
    grad_cross_b, sent_two_b, dctx_two_b, dq_two_b, score_two_b, back_two_b, three_b = cross_back(
        group, 1, after_cross_b, back_three_b, back_three_recv_b, prob_two_b
    )
    run(group)
    back_two_recv_b = swap(back_two_b)
    group = Group("self_back_a")
    cross_send, cross_keep, memory_send, memory_keep = group.add(
        functools.partial(cross_grads_kernel, order),
        [
            ((width // 2, 4 * inner), bf16),
            ((width // 2, 4 * inner), bf16),
            ((rows, width), bf16),
            ((rows, width), f32),
        ],
        [
            normed_two_a,
            normed_two_b,
            dq_two_a,
            dq_two_b,
            query_two_a,
            query_two_b,
            score_two_a,
            score_two_b,
            prob_two_a,
            prob_two_b,
            dctx_two_a,
            dctx_two_b,
            ctx_two_a,
            ctx_two_b,
            sent_two_a,
            sent_two_b,
            memory_all,
            cross_keyval,
        ],
        scratch=[pltpu.VMEM((width, length), bf16)] * 3 + [pltpu.VMEM((length, 2 * inner), bf16)],
        flops=2 * length * width * inner * 8,
    )

    def self_back(group, chunk, after, back, back_recv, grad_cross, prob):
        end = (chunk + 1) * rows
        return group.add(
            functools.partial(self_back_kernel, chunk),
            [
                ((rows, width), f32),
                ((rows, width), bf16),
                ((rows, inner), bf16),
                ((rows, inner), bf16),
                ((heads, rows, end), bf16),
                ((8, width), f32),
            ],
            [after, back, back_recv, grad_cross, norm_gains, self_output, qkv, prob],
            flops=2 * rows * width * inner * 3,
        )

    grad_self_a, sent_one_a, dctx_one_a, dq_one_a, score_one_a, two_a = self_back(
        group, 0, after_self_a, back_two_a, back_two_recv_a, grad_cross_a, prob_one_a
    )
    run(group)
    cross_sum = Scatter(steps, cross_send, cross_keep)
    group = Group("self_back_b")
    grad_self_b, sent_one_b, dctx_one_b, dq_one_b, score_one_b, two_b = self_back(
        group, 1, after_self_b, back_two_b, back_two_recv_b, grad_cross_b, prob_one_b
    )

    self_send, self_keep, dqkv = group.add(
        functools.partial(self_grads_kernel, order),
        [((width // 2, 4 * inner), bf16), ((width // 2, 4 * inner), bf16), ((length, 3 * inner), bf16)],
        [
            normed_one_a,
            normed_one_b,
            dq_one_a,
            dq_one_b,
            qkv,
            score_one_a,
            score_one_b,
            prob_one_a,
            prob_one_b,
            dctx_one_a,
            dctx_one_b,
            ctx_one_a,
            ctx_one_b,
            sent_one_a,
            sent_one_b,
        ],
        scratch=[pltpu.VMEM((width, length), bf16)] * 2,
        flops=2 * length * width * inner * 6,
    )
    run(group)
    self_sum = Scatter(steps, self_send, self_keep)
    together("halve_ffn_two", *ffn_sums)
    cross_sum.step("halve_cross_one")
    group = Group("self_input")
    back_one_send, back_one_keep, small_part = group.add(
        self_input_kernel,
        [((rows + 32, width), bf16), ((rows, width), f32), ((16, width), f32)],
        [
            dqkv,
            own,
            recv,
            self_query,
            self_keyval,
            score_one_a,
            score_one_b,
            hot,
            two_a,
            two_b,
            three_a,
            three_b,
        ],
        scratch=[pltpu.VMEM((8, 2 * length), f32)],
    )
    run(group)
    back_one_recv = swap(back_one_send)
    self_sum.step("halve_self_one")
    (out_part,) = single("down", down_kernel, [((rows, width), bf16)], [hidden_a, hidden_b, ffn_output])
    cross_sum.step("halve_cross_two")
    together("halve_ffn_three", *ffn_sums)
    group = Group("input_grad")
    (grad_input,) = group.add(
        input_grad_kernel,
        [((rows, width), f32)],
        [own, back_one_keep, back_one_recv, grad_self_a, grad_self_b, norm_gains],
    )
    pair = ((16, 2 * width), bf16)
    (small,) = group.add(add_first_kernel, [pair], [small_part, back_one_recv])
    run(group)
    small_got = flip(small, 1, dp)
    (small,) = single("small_add", add_kernel, [pair], [settled(small), small_got])
    small_got = flip(small, 2, dp)
    cross_sum.step("halve_cross_three")
    carried = steps == [1, 2, 4, 8] and 2 * width == 4 * inner
    if carried:
        group = Group("halve_self_two")
        self_sum.halve(group, small, small_got)
    else:
        for bit in sorted(steps)[2:]:
            (small,) = single("small_add", add_kernel, [pair], [settled(small), small_got])
            small_got = flip(small, bit, dp)
        (small,) = single("small_add", add_kernel, [pair], [small, small_got])
        group = Group("halve_self_two")
        self_sum.halve(group)
    (out_send,) = group.add(join_kernel, [((length, width), bf16)], [out_part, memory_send])
    run(group)
    self_sum.send()
    out_recv = swap(out_send)
    self_sum.step("halve_self_three")
    widths = [(1, inner), (2, inner), (1, inner)]
    group = Group("final")
    (output,) = group.add(
        final_kernel,
        [((rows, width), bf16)],
        [hidden_a, hidden_b, after_cross_a, after_cross_b, out_recv, ffn_output],
    )
    (grad_memory,) = group.add(memory_add_kernel, [((rows, width), f32)], [memory_keep, out_recv])
    grads_cross = finish(group, cross_sum.total(), widths)
    grads_ffn = finish(group, [part for item in ffn_sums for part in item.total()], [(2, units), (1, units)])
    run(group)
    group = Group("finish_self")
    rest = self_sum.total()
    grads_self = finish(group, rest, widths)
    small_outs = [((3, width), f32), ((2 * heads, buckets), f32)]
    gains, bias = group.add(last_small_kernel, small_outs, [*rest] if carried else [small])
    run(group)
    grads_ffn, grads_cross, grads_self = [[settled(g) for g in grads] for grads in (grads_ffn, grads_cross, grads_self)]
    return (
        settled(output)[None],
        settled(grad_input)[None],
        settled(grad_memory)[None],
        *grads_self[:-1],
        grads_self[-1].T,
        *grads_cross[:-1],
        grads_cross[-1].T,
        *grads_ffn[:-1],
        grads_ffn[-1].T,
        settled(gains),
        settled(bias).T,
    )


def solution(mesh):
    in_specs = (
        P("dp", "mp", None),
        P("dp", "mp", None),
        P("dp", "mp", None),
        P(None, "mp"),
        P(None, None, "mp"),
        P("mp", None),
        P(None, "mp"),
        P(None, None, "mp"),
        P("mp", None),
        P(None, None, "mp"),
        P("mp", None),
        P(),
        P(None, "mp"),
        P("dp", None),
        P("dp", None),
        P(),
    )
    out_specs = (
        P("dp", "mp", None),
        P("dp", "mp", None),
        P("dp", "mp", None),
        P("dp", "mp"),
        P(None, "dp", "mp"),
        P("mp", "dp"),
        P("dp", "mp"),
        P(None, "dp", "mp"),
        P("mp", "dp"),
        P(None, "dp", "mp"),
        P("mp", "dp"),
        P(),
        P(),
    )
    return jax.shard_map(body, mesh=mesh, in_specs=in_specs, out_specs=out_specs, check_vma=False)
```
